32 devices in a mesh: seq: 16 (over z, x, core), ulys: 2 (over y).
Axes of the slice: x: 2, y: 2, z: 4, core: 2. Of those that a mesh axis runs over, the one named last changes fastest.
Arguments:
- queries: bfloat16 [4096, 3072], P(('seq', 'ulys')), may hold values from -40 to 40
- keys: bfloat16 [4096, 3072], P(('seq', 'ulys')), may hold values from -14 to 14
- values: bfloat16 [4096, 3072], P(('seq', 'ulys')), may hold values from -6 to 6
- dout: bfloat16 [4096, 3072], P(('seq', 'ulys')), may hold values from -6144 to 6144
- changed_blocks: int32 [4], replicated, may hold values from 0 to 31, as said below
- half_mask: int32 [4, 2], replicated, may hold values from 0 to 1, as said below
Outputs:
- dq_changed: bfloat16 [512, 3072], P('seq', 'ulys')
- dkeys: bfloat16 [4096, 3072], P(('seq', 'ulys'))
- dvalues: bfloat16 [4096, 3072], P(('seq', 'ulys'))
The draws below stay inside these ranges and needn't reach their ends.
Inputs may be any that keep to these rules, and one draw needn't show every extreme that they name: `changed_blocks`: 4 distinct block ids; block c covers tokens c * 128 to (c + 1) * 128 - 1; the last block of the latent is always among them. `half_mask`: every row holds at least one 1.
All inputs are finite; a program needn't handle non-finite values.
Results may differ from the reference program's by a relative error of at most 0.0051.
Values may be sent and summed in bfloat16 or wider, within the bound.
A program may use at most 64 MiB of HBM per device.

```python
import jax
import jax.numpy as jnp
from jax import lax

HEADS = 24
HEAD_DIM = 128
BLOCK = 128
CHANGED = 4
TOKENS = 4096


def changed_list(key):
    nblocks = TOKENS // BLOCK
    base_key = jax.random.fold_in(key, 11)
    key_center, key_noise, key_half = jax.random.split(base_key, 3)
    center = jax.random.randint(key_center, (), 0, nblocks)
    index = jnp.arange(nblocks, dtype=jnp.int32)
    near = (jnp.abs(index - center) < max(CHANGED, nblocks // 8)).astype(jnp.int32)
    noise = jax.random.randint(key_noise, (nblocks,), 0, 1024)
    score = (noise + 2048 * near) * nblocks + index
    score = jnp.where(index == nblocks - 1, 4096 * nblocks + index, score)
    chosen = lax.top_k(score, CHANGED)[1].astype(jnp.int32)
    pattern = jax.random.randint(key_half, (CHANGED,), 0, 3)
    halves = jnp.stack([pattern != 1, pattern != 0], axis=1).astype(jnp.int32)
    return (chosen, halves)


def draw_changed_blocks(key, part):
    return changed_list(key)[0]


def draw_half_mask(key, part):
    return changed_list(key)[1]


def draw_keys(key, part):
    width = HEADS * HEAD_DIM
    own_key = jax.random.fold_in(key, 31)
    key_base, key_row = jax.random.split(own_key, 2)
    trend = 0.5 + jnp.arange(TOKENS, dtype=jnp.float32) / TOKENS
    base = jnp.clip(jax.random.normal(key_base, (TOKENS, width), jnp.float32), -6.0, 6.0)
    row_scale = jnp.exp(jax.random.uniform(key_row, (TOKENS, 1), jnp.float32, -0.4, 0.4))
    result = base * trend[:, None] * row_scale
    return result.astype(jnp.bfloat16)


def draw_queries(key, part):
    width = HEADS * HEAD_DIM
    own_key = jax.random.fold_in(key, 41)
    result = jnp.clip(jax.random.normal(own_key, (TOKENS, width), jnp.float32), -6.0, 6.0)
    return result.astype(jnp.bfloat16)


def draw_dout(key, part):
    width = HEADS * HEAD_DIM
    own_key = jax.random.fold_in(key, 43)
    result = jnp.clip(jax.random.normal(own_key, (TOKENS, width), jnp.float32), -6.0, 6.0) * 1024.0
    return result.astype(jnp.bfloat16)


def block_levels(rng, dims, cuts, least, largest):
    level = 1.0
    for position, parts in cuts:
        steps = jax.random.uniform(jax.random.fold_in(jax.random.fold_in(rng, 6), position), (parts,), jnp.float32, least / len(cuts), largest / len(cuts))
        level = level * jnp.repeat(jnp.exp(steps), dims[position] // parts).reshape((-1,) + (1,) * (len(dims) - 1 - position))
    return level


def bell_draw(key, dims, deviation, reach, shards=(), held_as=jnp.bfloat16):
    values = jax.random.normal(key, dims, jnp.float32) * deviation
    if len(shards) > 0:
        values = block_levels(key, dims, shards, -0.22, 0.18) * values
    return jnp.clip(values, min=-reach, max=reach).astype(held_as)


def setup_inputs(seed: int = 0) -> dict:
    splits = jax.random.split(jax.random.key(seed), 7)
    queries = draw_queries(jax.random.fold_in(splits[6], 71), 0)
    keys = draw_keys(jax.random.fold_in(splits[6], 71), 0)
    values = bell_draw(splits[2], (TOKENS, HEADS * HEAD_DIM), 1.0, 6.0, ((0, 32),))
    dout = draw_dout(jax.random.fold_in(splits[6], 71), 0)
    changed_blocks = draw_changed_blocks(jax.random.fold_in(splits[6], 71), 0)
    half_mask = draw_half_mask(jax.random.fold_in(splits[6], 71), 0)
    return {"queries": queries, "keys": keys, "values": values, "dout": dout, "changed_blocks": changed_blocks, "half_mask": half_mask}


def contract_last(a, b):
    return lax.dot_general(a, b, (((1,), (1,)), ((), ())), preferred_element_type=jnp.float32)


def contract_first(a, b):
    return lax.dot_general(a, b, (((0,), (0,)), ((), ())), preferred_element_type=jnp.float32)


def reference(queries, keys, values, dout, changed_blocks, half_mask):
    offsets = jnp.arange(BLOCK, dtype=jnp.int32)
    rows = (changed_blocks[:, None] * BLOCK + offsets[None, :]).reshape(-1).astype(jnp.int32)
    q_sel = queries[rows]
    live = jnp.where(offsets[None, :] < BLOCK // 2, half_mask[:, 0:1], half_mask[:, 1:2]).reshape(-1)
    do_sel = dout[rows] * live[:, None].astype(jnp.bfloat16)
    count = rows.shape[0]
    scale = 1.0 / (HEAD_DIM ** 0.5)
    q_heads = q_sel.reshape(count, HEADS, HEAD_DIM).transpose(1, 0, 2)
    do_heads = do_sel.reshape(count, HEADS, HEAD_DIM).transpose(1, 0, 2)
    k_heads = keys.reshape(TOKENS, HEADS, HEAD_DIM).transpose(1, 0, 2)
    v_heads = values.reshape(TOKENS, HEADS, HEAD_DIM).transpose(1, 0, 2)

    def per_head(pieces):
        q_one, k_one, v_one, d_one = pieces
        scores = contract_last(q_one, k_one) * scale
        rowmax = jnp.max(scores, axis=1, keepdims=True)
        expo = jnp.exp(scores - rowmax)
        total = jnp.sum(expo, axis=1, keepdims=True)
        probs = expo / total
        probs_b = probs.astype(jnp.bfloat16)
        dprobs = contract_last(d_one, v_one)
        delta = jnp.sum(probs * dprobs, axis=1, keepdims=True)
        dscores = (probs * (dprobs - delta)).astype(jnp.bfloat16)
        dq_one = (jnp.dot(dscores, k_one, preferred_element_type=jnp.float32) * scale).astype(jnp.bfloat16)
        dk_one = (contract_first(dscores, q_one) * scale).astype(jnp.bfloat16)
        dv_one = contract_first(probs_b, d_one).astype(jnp.bfloat16)
        return dq_one, dk_one, dv_one

    dq_all, dk_all, dv_all = lax.map(per_head, (q_heads, k_heads, v_heads, do_heads))
    dq_changed = dq_all.transpose(1, 0, 2).reshape(count, HEADS * HEAD_DIM)
    dkeys = dk_all.transpose(1, 0, 2).reshape(TOKENS, HEADS * HEAD_DIM)
    dvalues = dv_all.transpose(1, 0, 2).reshape(TOKENS, HEADS * HEAD_DIM)
    return (dq_changed, dkeys, dvalues)
```

```python
import functools

import jax
import jax.numpy as jnp
from jax import lax
from jax.experimental import pallas as pl
from jax.experimental.pallas import tpu as pltpu
from jax.sharding import PartitionSpec as P

HEAD_DIM = 128
BLOCK = 128
PART = 32
CHANGED = 4
ROWS = CHANGED * BLOCK
CORES = 2
INNER = 2
SCALE = 1.0 / HEAD_DIM**0.5
HALF = BLOCK // 2
DELAYS = (0, 1, 2, 3, 4, 5, 6, 7)
MESH = pl.DeviceIdType.MESH


class Sizes:
    def __init__(self, seq, ulys, width):
        self.ulys = ulys
        self.inner = INNER
        self.outer = seq // (INNER * CORES)
        self.width = width // ulys
        self.heads = self.width // HEAD_DIM
        self.group = 2 if self.heads % 2 == 0 else 1
        self.cols = self.group * HEAD_DIM
        self.chunks = self.heads // self.group
        self.shard = ROWS // seq
        self.seq = seq
        self.keys = ulys * BLOCK
        self.stat_rows = -(-3 * self.group // 8) * 8
        self.sum_type = jnp.bfloat16 if self.shard >= 16 else jnp.float32


def contract(a, b, dims):
    return lax.dot_general(a, b, (dims, ((), ())), preferred_element_type=jnp.float32)


def kernel(
    z,
    changed, live, q_in, do_in, k_in, v_in,
    dq_out, dk_out, dv_out,
    ybuf, kv, z0, zr, zl, zro, zlo, full,
    expo, dpro, stb, sta, fin, ret,
    dq0, dq1, dt1, dq2, dt2, dq3,
    y_s, y_r, kv_s, kv_r, zs, zrs, f_s, f_r,
    sb_s, sb_r, sa_s, sa_r, ret_s, ret_r,
    d1_s, d1_r, d2_s, d2_r, d3_s, d3_r,
):
    seq = lax.axis_index("seq")
    u = lax.axis_index("ulys")
    c = lax.rem(seq, CORES)
    b = lax.rem(seq // CORES, z.inner)
    a = seq // (CORES * z.inner)
    U, B, A, G, W, N, g = z.ulys, z.inner, z.outer, z.cols, z.width, z.chunks, z.group

    def dev(a_, b_, c_, u_):
        return ((a_ * B + b_) * CORES + c_, u_)

    def copy(src, dst, ss, rs, to):
        return pltpu.make_async_remote_copy(
            src_ref=src, dst_ref=dst, send_sem=ss, recv_sem=rs, device_id=to, device_id_type=MESH
        )

    def at_u(d):
        return lax.rem(u + d, U)

    def at_c(d):
        return lax.rem(c + d, CORES)

    def at_b(d):
        return lax.rem(b + d, B)

    def at_a(d):
        return lax.rem(a + d, A)

    def col(block, i):
        return pl.ds(pl.multiple_of(block * W + i * G, HEAD_DIM), G)

    part = b * CORES + c
    near = [(db, dc) for db in range(B) for dc in range(CORES)]
    pairs = [(du, k) for k in range(len(near)) for du in range(U)]

    def near_dev(k, u_):
        return dev(a, at_b(near[k][0]), at_c(near[k][1]), u_)

    def part_of(k):
        return at_b(near[k][0]) * CORES + at_c(near[k][1])

    peers = [near_dev(k, at_u(du)) for du, k in pairs if du or k]
    peers += [dev(at_a(d), b, c, u) for d in range(1, A)]
    barrier = pltpu.get_barrier_semaphore()
    for peer in peers:
        pl.semaphore_signal(barrier, inc=1, device_id=peer, device_id_type=MESH)
    pl.semaphore_wait(barrier, len(peers))

    def y_rows(k):
        return pl.ds(pl.multiple_of(part_of(k) * PART, PART), PART)

    def y_copy(i, n, du, k):
        ref = (q_in, do_in)[n]
        return copy(
            ref.at[y_rows(k), col(at_u(du), i)], ybuf.at[i, n, du, k],
            y_s.at[0 if du else 1], y_r.at[i], near_dev(k, at_u(du)),
        )

    def y_own(i, n):
        ref = (q_in, do_in)[n]
        return pltpu.make_async_copy(
            ref.at[y_rows(0), col(u, i)], ybuf.at[i, n, 0, 0], y_r.at[i]
        )

    def kv_own(i, n):
        ref = (k_in, v_in)[n]
        return pltpu.make_async_copy(ref.at[:, col(u, i)], kv.at[i, n, 0], kv_r.at[i])

    def kv_copy(i, n, du):
        ref = (k_in, v_in)[n]
        return copy(
            ref.at[:, col(at_u(du), i)], kv.at[i, n, du],
            kv_s.at[0], kv_r.at[i], dev(a, b, c, at_u(du)),
        )

    def each(body):
        def step(i, carry):
            body(i)
            return carry

        lax.fori_loop(0, N, step, 0)

    def send_y(i):
        for n in range(2):
            y_own(i, n).start()
            for du, k in pairs:
                if du or k:
                    y_copy(i, n, du, k).start()

    def send_kv(i):
        for n in range(2):
            kv_own(i, n).start()
            for du in range(1, U):
                kv_copy(i, n, du).start()

    each(send_y)
    each(send_kv)

    def line(i, p, n, right, left, src, rin, lin, rout, lout, ss, rs):
        def r_copy():
            return copy(rout.at[i], rin.at[i], ss.at[i, 0], rs.at[i, 0], right)

        def l_copy():
            return copy(lout.at[i], lin.at[i], ss.at[i, 1], rs.at[i, 1], left)

        def do_right():
            @pl.when(p == 0)
            def _():
                rin[i] = jnp.zeros(rin.shape[1:], rin.dtype)

            @pl.when(p > 0)
            def _():
                r_copy().wait_recv()

            @pl.when(p < n - 1)
            def _():
                rout[i] = src[i] + rin[i]
                r_copy().start()

        def do_left():
            @pl.when(p == n - 1)
            def _():
                lin[i] = jnp.zeros(lin.shape[1:], lin.dtype)

            @pl.when(p < n - 1)
            def _():
                l_copy().wait_recv()

            @pl.when(p > 0)
            def _():
                lout[i] = src[i] + lin[i]
                l_copy().start()

        def hop(h):
            pl.when(p == h)(do_right)
            pl.when(p == n - 1 - h)(do_left)

        def finish():
            @pl.when(p < n - 1)
            def _():
                r_copy().wait_send()

            @pl.when(p > 0)
            def _():
                l_copy().wait_send()

        return hop, finish

    def z_line(i):
        return line(
            i, a, A, dev(lax.rem(a + 1, A), b, c, u), dev(lax.rem(a + A - 1, A), b, c, u),
            z0, zr, zl, zro, zlo, zs, zrs,
        )

    def select(i):
        pltpu.make_async_copy(ybuf.at[i], ybuf.at[i], y_r.at[i]).wait()
        for n in range(2):
            totals = [None] * CHANGED
            for du, k in pairs:
                from_b = lax.rem(b + B - near[k][0], B)
                from_c = lax.rem(c + CORES - near[k][1], CORES)
                from_u = lax.rem(u + U - du, U)
                block = ((a * B + from_b) * CORES + from_c) * U + from_u
                piece = ybuf[i, n, du, k]
                for slot in range(CHANGED):
                    weight = jnp.where(changed[slot] == block, 1.0, 0.0)
                    if n == 1:
                        weight = weight * jnp.where(
                            b == 0, live[slot, 0], live[slot, 1]
                        ).astype(jnp.float32)
                    weight = jnp.full((PART, G), weight, jnp.float32).astype(jnp.bfloat16)
                    term = piece * weight
                    totals[slot] = term if totals[slot] is None else totals[slot] + term
            for slot in range(CHANGED):
                z0[i, n, slot] = totals[slot]
        z_line(i)[0](0)

    def hop(h, i):
        z_line(i)[0](h)

    def spread_copy(i, n, came=False):
        at = (part, part, at_b(1) * CORES + c)[n]
        to = (dev(a, b, at_c(1), u), dev(a, at_b(1), c, u), dev(a, b, at_c(1), u))[n]
        if came:
            at_in = (
                b * CORES + at_c(1), at_b(1) * CORES + c, at_b(1) * CORES + at_c(1)
            )[n]
            return copy(full.at[i, at], full.at[i, at_in], f_s.at[i, n], f_r.at[i, n], to)
        return copy(full.at[i, at], full.at[i, at], f_s.at[i, n], f_r.at[i, n], to)

    def spread(i):
        z_line(i)[0](A - 1)
        full[i, part] = z0[i] + zr[i] + zl[i]
        spread_copy(i, 1).start()
        spread_copy(i, 0).start()

    def relay(i):
        spread_copy(i, 1, True).wait_recv()
        spread_copy(i, 2).start()

    def head(j):
        return slice(j * HEAD_DIM, (j + 1) * HEAD_DIM)

    def q_of(i, j):
        return full[i, :, 0, :, :, head(j)].reshape(ROWS, HEAD_DIM)

    def do_of(i, j):
        return full[i, :, 1, :, :, head(j)].reshape(ROWS, HEAD_DIM)

    def kv_of(i, n, j):
        return kv[i, n, :, :, head(j)].reshape(z.keys, HEAD_DIM)

    def b_stat(i, k):
        return copy(
            stb.at[i, 0], stb.at[i, k], sb_s.at[i, k], sb_r.at[i, k], near_dev(k, u)
        )

    def a_stat(i, d):
        return copy(
            sta.at[i, 0], sta.at[i, d], sa_s.at[i, d], sa_r.at[i, d], dev(at_a(d), b, c, u)
        )

    def first_pass(i):
        spread_copy(i, 0, True).wait_recv()
        spread_copy(i, 2, True).wait_recv()
        pltpu.make_async_copy(kv.at[i], kv.at[i], kv_r.at[i]).wait()
        for j in range(g):
            scores = contract(kv_of(i, 0, j), q_of(i, j), ((1,), (1,))) * SCALE
            top = jnp.max(scores, axis=0, keepdims=True)
            e = jnp.exp(scores - top)
            dp = contract(kv_of(i, 1, j), do_of(i, j), ((1,), (1,)))
            stb[i, 0, j : j + 1, :] = top
            stb[i, 0, g + j : g + j + 1, :] = jnp.sum(e, axis=0, keepdims=True)
            stb[i, 0, 2 * g + j : 2 * g + j + 1, :] = jnp.sum(e * dp, axis=0, keepdims=True)
            expo[i * g + j] = e
            dpro[i * g + j] = dp
        for row in range(3 * g, z.stat_rows):
            stb[i, 0, row : row + 1, :] = jnp.zeros((1, ROWS), jnp.float32)
        for k in range(1, len(near)):
            b_stat(i, k).start()

    def merge(src, i, n, dst):
        parts = [src[i, d] for d in range(n)]
        top = functools.reduce(jnp.maximum, [part[0:g] for part in parts])
        factors = [jnp.exp(part[0:g] - top) for part in parts]
        total = sum(part[g : 2 * g] * f for part, f in zip(parts, factors))
        weighted = sum(part[2 * g : 3 * g] * f for part, f in zip(parts, factors))
        dst[0:g, :] = top
        dst[g : 2 * g, :] = total
        dst[2 * g : 3 * g, :] = weighted
        if z.stat_rows > 3 * g:
            dst[3 * g :, :] = jnp.zeros((z.stat_rows - 3 * g, ROWS), jnp.float32)

    def stat_a(i):
        for k in range(1, len(near)):
            b_stat(i, k).wait_recv()
        merge(stb, i, len(near), sta.at[i, 0])
        for d in range(1, A):
            a_stat(i, d).start()

    def back(i, n, d):
        out = (dk_out, dv_out)[n]
        return copy(
            ret.at[i, n, d], out.at[:, col(u, i)], ret_s.at[i, n, d], ret_r.at[i, n, d],
            dev(a, b, c, lax.rem(u + U - d, U)),
        )

    def back_wait(i, n, d):
        out = (dk_out, dv_out)[n]
        return copy(
            ret.at[i, n, d], out.at[:, col(at_u(d), i)], ret_s.at[i, n, d], ret_r.at[i, n, d],
            dev(a, b, c, lax.rem(u + U - d, U)),
        )

    def c_dq(i):
        return copy(
            dq0.at[i, at_c(1)], dq1.at[i], d1_s.at[i], d1_r.at[i], dev(a, b, at_c(1), u)
        )

    def b_dq(i, d):
        return copy(
            dt1.at[i, at_b(d)], dq2.at[i, d], d2_s.at[i, d], d2_r.at[i, d], dev(a, at_b(d), c, u)
        )

    def a_dq(i, d):
        return copy(
            dt2.at[i, at_a(d)], dq3.at[i, d], d3_s.at[i, d], d3_r.at[i, d], dev(at_a(d), b, c, u)
        )

    def second_pass(i):
        for d in range(1, A):
            a_stat(i, d).wait_recv()
        merge(sta, i, A, fin.at[i])
        for j in range(g):
            factor = jnp.exp(stb[i, 0, j : j + 1, :] - fin[i, j : j + 1, :])
            total = fin[i, g + j : g + j + 1, :]
            factor = factor / total
            delta = fin[i, 2 * g + j : 2 * g + j + 1, :] / total
            probs = expo[i * g + j] * factor
            ds = (probs * (dpro[i * g + j] - delta)).astype(jnp.bfloat16)
            dk = (contract(ds, q_of(i, j), ((1,), (0,))) * SCALE).astype(jnp.bfloat16)
            dv = contract(probs.astype(jnp.bfloat16), do_of(i, j), ((1,), (0,)))
            dv = dv.astype(jnp.bfloat16)
            ret[i, 0, :, :, head(j)] = dk.reshape(U, BLOCK, HEAD_DIM)
            ret[i, 1, :, :, head(j)] = dv.reshape(U, BLOCK, HEAD_DIM)
            dq = contract(ds, kv_of(i, 0, j), ((0,), (0,))) * SCALE
            for s in range(z.seq):
                row = s * z.shard
                at = (row % BLOCK) // PART * (CHANGED * PART) + row // BLOCK * PART + row % PART
                dq0[i, s % CORES, s // CORES % B, s // (CORES * B), :, head(j)] = dq[
                    at : at + z.shard
                ]
        c_dq(i).start()
        for n in range(2):
            for d in range(1, U):
                back(i, n, d).start()
        dk_out[:, col(u, i)] = ret[i, 0, 0]
        dv_out[:, col(u, i)] = ret[i, 1, 0]

    def dq_b(i):
        c_dq(i).wait_recv()
        dt1[i] = (dq0[i, c] + dq1[i]).astype(z.sum_type)
        for d in range(1, B):
            b_dq(i, d).start()

    def dq_a(i):
        total = dt1[i, b].astype(jnp.float32)
        for d in range(1, B):
            b_dq(i, d).wait_recv()
            total = total + dq2[i, d].astype(jnp.float32)
        dt2[i] = total.astype(z.sum_type)
        for d in range(1, A):
            a_dq(i, d).start()

    def dq_end(i):
        total = dt2[i, a].astype(jnp.float32)
        for d in range(1, A):
            a_dq(i, d).wait_recv()
            total = total + dq3[i, d].astype(jnp.float32)
        dq_out[:, pl.ds(pl.multiple_of(i * G, HEAD_DIM), G)] = total.astype(jnp.bfloat16)

    stages = [select, *[functools.partial(hop, h) for h in range(1, A - 1)], spread, relay]
    stages += [first_pass, stat_a, second_pass, dq_b, dq_a, dq_end]

    def step(t, carry):
        for delay, stage in enumerate(stages):
            i = t - delay
            pl.when((i >= 0) & (i < N))(functools.partial(stage, i))
        return carry

    lax.fori_loop(0, N + len(stages) - 1, step, 0)

    def drain(i):
        for n in range(2):
            for d in range(1, U):
                back(i, n, d).wait_send()
                back_wait(i, n, d).wait_recv()
        z_line(i)[1]()
        for n in range(3):
            spread_copy(i, n).wait_send()
        for k in range(1, len(near)):
            b_stat(i, k).wait_send()
        c_dq(i).wait_send()
        for d in range(1, B):
            b_dq(i, d).wait_send()
        for d in range(1, A):
            a_stat(i, d).wait_send()
            a_dq(i, d).wait_send()

    each(drain)
    far, close, others = ybuf.at[:, :, 1:], ybuf.at[:, :, 0, 1:], kv.at[:, :, 1:]
    pltpu.make_async_copy(far, far, y_s.at[0]).wait()
    pltpu.make_async_copy(close, close, y_s.at[1]).wait()
    pltpu.make_async_copy(others, others, kv_s.at[0]).wait()


def local(seq_size, ulys_size, queries, keys, values, dout, changed_blocks, half_mask):
    z = Sizes(seq_size, ulys_size, queries.shape[1])
    N, U, B, A, G, R = z.chunks, z.ulys, z.inner, z.outer, z.cols, z.shard
    bf16, f32 = jnp.bfloat16, jnp.float32
    line = pltpu.VMEM((N, 2, CHANGED, PART, G), bf16)
    near = INNER * CORES
    stat = (z.stat_rows, ROWS)
    dma = pltpu.SemaphoreType.DMA
    vmem = pl.BlockSpec(memory_space=pltpu.VMEM)
    hbm = pl.BlockSpec(memory_space=pl.ANY)
    smem = pl.BlockSpec(memory_space=pltpu.SMEM)
    scratch = [
        pltpu.VMEM((N, 2, U, near, PART, G), bf16),
        pltpu.VMEM((N, 2, U, BLOCK, G), bf16),
        *[line] * 5,
        pltpu.VMEM((N, near, 2, CHANGED, PART, G), bf16),
        pltpu.VMEM((z.heads, z.keys, ROWS), f32),
        pltpu.VMEM((z.heads, z.keys, ROWS), f32),
        pltpu.VMEM((N, near, *stat), f32),
        pltpu.VMEM((N, A, *stat), f32),
        pltpu.VMEM((N, *stat), f32),
        pltpu.VMEM((N, 2, U, BLOCK, G), bf16),
        pltpu.VMEM((N, CORES, B, A, R, G), f32),
        pltpu.VMEM((N, B, A, R, G), f32),
        pltpu.VMEM((N, B, A, R, G), z.sum_type),
        pltpu.VMEM((N, B, A, R, G), z.sum_type),
        pltpu.VMEM((N, A, R, G), z.sum_type),
        pltpu.VMEM((N, A, R, G), z.sum_type),
        dma((2,)),
        dma((N,)),
        dma((1,)),
        dma((N,)),
        *[dma((N, 2))] * 2,
        *[dma((N, 3))] * 2,
        *[dma((N, near))] * 2,
        *[dma((N, A))] * 2,
        *[dma((N, 2, U))] * 2,
        *[dma((N,))] * 2,
        *[dma((N, B))] * 2,
        *[dma((N, A))] * 2,
    ]
    return pl.pallas_call(
        functools.partial(kernel, z),
        out_shape=(
            jax.ShapeDtypeStruct((R, z.width), bf16),
            jax.ShapeDtypeStruct(keys.shape, bf16),
            jax.ShapeDtypeStruct(values.shape, bf16),
        ),
        in_specs=[smem, smem, hbm, hbm, hbm, hbm],
        out_specs=(vmem, vmem, vmem),
        scratch_shapes=scratch,
        compiler_params=pltpu.CompilerParams(
            collective_id=0, has_side_effects=True, vmem_limit_bytes=62 * 1024 * 1024
        ),
    )(changed_blocks, half_mask, queries, dout, keys, values)


class Split:
    def __init__(self, seq, ulys, width):
        self.ulys = ulys
        self.outer = seq // (INNER * CORES)
        self.groups = ulys * CORES
        self.width = width // self.groups
        self.chunks = self.width // HEAD_DIM
        self.seq = seq
        self.shard = ROWS // seq
        self.keys = self.groups * BLOCK

    @staticmethod
    def fits(seq, ulys, width):
        return (
            width % (ulys * CORES * HEAD_DIM) == 0
            and seq == INNER * CORES * CHANGED
            and ROWS // seq % 16 == 0
            and ulys * CORES * BLOCK <= 512
        )


def split_kernel(
    z,
    changed, live, q_in, do_in, k_in, v_in,
    dq_out, dk_out, dv_out,
    ybuf, kv, z0, za, zb, zc, full, expo, dpro, stats, ret, dq0, dq1, dt1, dq2,
    y_s, y_r, kv_s, kv_r, za_s, za_r, zb_s, zb_r, g_s, g_r, x_s, x_r, st_s, st_r,
    o_s, o_r, l_s, d1_s, d1_r, d2_s, d2_r,
):
    seq = lax.axis_index("seq")
    u = lax.axis_index("ulys")
    c = lax.rem(seq, CORES)
    b = lax.rem(seq // CORES, INNER)
    a = seq // (CORES * INNER)
    U, B, A, C, W, N = z.ulys, INNER, z.outer, CORES, z.width, z.chunks
    D = HEAD_DIM

    def dev(da, db, dc, du):
        a_, b_, c_, u_ = at_a(da), at_b(db), at_c(dc), at_u(du)
        return ((a_ * B + b_) * C + c_, u_)

    def at_u(d):
        return lax.rem(u + U + d, U)

    def at_c(d):
        return lax.rem(c + C + d, C)

    def at_b(d):
        return lax.rem(b + B + d, B)

    def at_a(d):
        return lax.rem(a + A + d, A)

    def copy(src, dst, ss, rs, to):
        return pltpu.make_async_remote_copy(
            src_ref=src, dst_ref=dst, send_sem=ss, recv_sem=rs, device_id=to, device_id_type=MESH
        )

    def arrived(ref, sem):
        pltpu.make_async_copy(ref, ref, sem).wait()

    def col(u_, c_, i):
        return pl.ds(pl.multiple_of((u_ * C + c_) * W + i * D, D), D)

    owners = [(du, dc) for du in range(U) for dc in range(C)]
    near = [(db, du, dc) for db in range(B) for du, dc in owners]
    others = [(da, db) for da in range(A) for db in range(B)]
    rows = [(da, dc) for da in range(A) for dc in range(C)]

    peers = {(0, db, dc, du) for db, du, dc in near}
    peers |= {(da, db, 0, 0) for da, db in others}
    peers |= {(da, 0, dc, 0) for da, dc in rows}
    peers = sorted(peers - {(0, 0, 0, 0)})
    barrier = pltpu.get_barrier_semaphore()
    for peer in peers:
        pl.semaphore_signal(barrier, inc=1, device_id=dev(*peer), device_id_type=MESH)
    pl.semaphore_wait(barrier, len(peers))

    def send_y(i):
        for k, (db, du, dc) in enumerate(near):
            part = pl.ds(pl.multiple_of(at_b(db) * HALF, HALF), HALF)
            for n, ref in enumerate((q_in, do_in)):
                src = ref.at[part, col(at_u(du), at_c(dc), i)]
                if k:
                    copy(src, ybuf.at[i, n, k], y_s.at[0], y_r.at[i], dev(0, db, dc, du)).start()
                else:
                    pltpu.make_async_copy(src, ybuf.at[i, n, k], y_r.at[i]).start()

    def send_kv(i):
        for k, (du, dc) in enumerate(owners):
            for n, ref in enumerate((k_in, v_in)):
                src = ref.at[:, col(at_u(du), at_c(dc), i)]
                if k:
                    copy(src, kv.at[i, n, k], kv_s.at[0], kv_r.at[i], dev(0, 0, dc, du)).start()
                else:
                    pltpu.make_async_copy(src, kv.at[i, n, k], kv_r.at[i]).start()

    def each(body):
        def step(i, carry):
            body(i)
            return carry

        lax.fori_loop(0, N, step, 0)

    each(send_y)

    def select(i):
        send_kv(i)
        arrived(ybuf.at[i], y_r.at[i])
        totals = [[None] * CHANGED for _ in range(2)]
        for k, (db, du, dc) in enumerate(near):
            block = ((a * B + at_b(-db)) * C + at_c(-dc)) * U + at_u(-du)
            pieces = [ybuf[i, n, k] for n in range(2)]
            for slot in range(CHANGED):
                here = jnp.where(changed[slot] == block, 1.0, 0.0)
                lives = jnp.where(b == 0, live[0, slot], live[1, slot]).astype(jnp.float32)
                for n, weight in enumerate((here, here * lives)):
                    weight = jnp.full((HALF, D), weight, jnp.float32).astype(jnp.bfloat16)
                    term = pieces[n] * weight
                    old = totals[n][slot]
                    totals[n][slot] = term if old is None else old + term
        for slot in range(CHANGED):
            for n in range(2):
                z0[i, n, slot] = totals[n][slot]

        @pl.when(outside)
        def _():
            pair_copy(i).start()

    mate = a + 1 - 2 * lax.rem(a, 2)
    outside = (a == 0) | (a == A - 1)
    inside = (a != 0) & (a != A - 1)

    def line_dev(a_):
        return ((a_ * B + b) * C + c, u)

    def pair_copy(i):
        return copy(z0.at[i], za.at[i], za_s.at[i], za_r.at[i], line_dev(mate))

    def middle_copy(i):
        return copy(zb.at[i], zc.at[i], zb_s.at[i], zb_r.at[i], line_dev(A - 1 - a))

    def back_copy(i):
        here = full.at[i, :, :, b]
        return copy(here, here, g_s.at[i], g_r.at[i], line_dev(mate))

    def x_copy(i, came):
        here = full.at[i, :, :, b]
        there = full.at[i, :, :, at_b(1)] if came else here
        return copy(here, there, x_s.at[i], x_r.at[i], dev(0, 1, 0, 0))

    def middle(i):
        @pl.when(inside)
        def _():
            pair_copy(i).wait_recv()
            zb[i] = z0[i] + za[i]
            middle_copy(i).start()

    def give_back(i):
        @pl.when(inside)
        def _():
            middle_copy(i).wait_recv()
            full[i, :, :, b] = zb[i] + zc[i]
            back_copy(i).start()
            x_copy(i, False).start()

    def across(i):
        @pl.when(outside)
        def _():
            back_copy(i).wait_recv()
            x_copy(i, False).start()

    def q_of(i, n):
        return full[i, n].reshape(ROWS, D)

    def kv_of(i, n):
        return kv[i, n].reshape(z.keys, D)

    def first_pass(i):
        x_copy(i, True).wait_recv()
        arrived(kv.at[i], kv_r.at[i])
        scores = contract(kv_of(i, 0), q_of(i, 0), ((1,), (1,))) * SCALE
        top = jnp.max(scores, axis=0, keepdims=True)
        e = jnp.exp(scores - top)
        dp = contract(kv_of(i, 1), q_of(i, 1), ((1,), (1,)))
        found = (top, jnp.sum(e, axis=0, keepdims=True), jnp.sum(e * dp, axis=0, keepdims=True))
        expo[i] = e
        dpro[i] = dp
        for r, row in enumerate(found):
            for j in range(CHANGED):
                at = r * CHANGED + j
                stats[i, 0, at : at + 1, :] = row[:, j * BLOCK : (j + 1) * BLOCK]
        stats[i, 0, 3 * CHANGED :, :] = jnp.zeros((CHANGED, BLOCK), jnp.float32)
        for k, (da, db) in enumerate(others):
            if k:
                copy(
                    stats.at[i, 0], stats.at[i, k], st_s.at[0], st_r.at[i], dev(da, db, 0, 0)
                ).start()

    def wide(x):
        return jnp.concatenate([x[j : j + 1] for j in range(CHANGED)], axis=1)

    def second_pass(i):
        arrived(stats.at[i, 1:], st_r.at[i])
        parts = [stats[i, k] for k in range(len(others))]
        tops = [part[0:CHANGED] for part in parts]
        top = functools.reduce(jnp.maximum, tops)
        factors = [jnp.exp(t - top) for t in tops]
        total = sum(p[CHANGED : 2 * CHANGED] * f for p, f in zip(parts, factors))
        weighted = sum(p[2 * CHANGED : 3 * CHANGED] * f for p, f in zip(parts, factors))
        factor = wide(factors[0] / total)
        delta = wide(weighted / total)
        probs = expo[i] * factor
        ds = (probs * (dpro[i] - delta)).astype(jnp.bfloat16)
        dq = contract(ds, kv_of(i, 0), ((0,), (0,))) * SCALE
        dq0[i] = dq.astype(jnp.bfloat16).reshape(A, B, z.shard * C, D)
        dq_x(i).start()
        dk = (contract(ds, q_of(i, 0), ((1,), (0,))) * SCALE).astype(jnp.bfloat16)
        ret[i, 0] = dk.reshape(len(owners), BLOCK, D)
        send_out(i, 0)
        dv = contract(probs.astype(jnp.bfloat16), q_of(i, 1), ((1,), (0,))).astype(jnp.bfloat16)
        ret[i, 1] = dv.reshape(len(owners), BLOCK, D)
        send_out(i, 1)

    def send_out(i, n):
        out = (dk_out, dv_out)[n].at[:, col(u, c, i)]
        for k, (du, dc) in enumerate(owners):
            if k:
                copy(ret.at[i, n, k], out, o_s.at[0], o_r.at[0], dev(0, 0, -dc, -du)).start()
            else:
                pltpu.make_async_copy(ret.at[i, n, k], out, l_s.at[0]).start()

    def dq_x(i):
        return copy(
            dq0.at[i, :, at_b(1)], dq1.at[i], d1_s.at[i], d1_r.at[i], dev(0, 1, 0, 0)
        )

    def dq_mid(i):
        dq_x(i).wait_recv()
        mine = dq0[i, :, b].astype(jnp.float32) + dq1[i].astype(jnp.float32)
        dt1[i] = mine.astype(jnp.bfloat16).reshape(A, C, z.shard, D)
        for k, (da, dc) in enumerate(rows):
            if k:
                copy(
                    dt1.at[i, at_a(da), at_c(dc)], dq2.at[i, k - 1],
                    d2_s.at[0], d2_r.at[i], dev(da, 0, dc, 0),
                ).start()

    def dq_end(i):
        arrived(dq2.at[i], d2_r.at[i])
        for dc in range(C):
            total = None
            for k, (da, e) in enumerate(rows):
                if e == dc:
                    term = (dq2[i, k - 1] if k else dt1[i, a, c]).astype(jnp.float32)
                    total = term if total is None else total + term
            at = pl.ds(pl.multiple_of(at_c(-dc) * W + i * D, D), D)
            dq_out[:, at] = total.astype(jnp.bfloat16)

    stages = [select, middle, give_back, across, first_pass, second_pass, dq_mid, dq_end]

    def step(t, carry):
        for stage, delay in zip(stages, DELAYS):
            i = t - delay
            pl.when((i >= 0) & (i < N))(functools.partial(stage, i))
        return carry

    lax.fori_loop(0, N + DELAYS[-1], step, 0)

    def drain(i):
        @pl.when(outside)
        def _():
            pair_copy(i).wait_send()

        @pl.when(inside)
        def _():
            middle_copy(i).wait_send()
            back_copy(i).wait_send()

        x_copy(i, False).wait_send()
        dq_x(i).wait_send()
        for k in range(1, len(others)):
            arrived(stats.at[i, k], st_s.at[0])

    each(drain)
    arrived(ybuf.at[:, :, 1:], y_s.at[0])
    arrived(kv.at[:, :, 1:], kv_s.at[0])
    arrived(dq2, d2_s.at[0])
    arrived(ret.at[:, :, 1:], o_s.at[0])
    arrived(ret.at[:, :, 1:], o_r.at[0])
    arrived(ret.at[:, :, 0], l_s.at[0])


def split_local(seq_size, ulys_size, queries, keys, values, dout, changed_blocks, half_mask):
    z = Split(seq_size, ulys_size, queries.shape[1])
    N, U, A, C, D, R = z.chunks, z.ulys, z.outer, CORES, HEAD_DIM, z.shard
    bf16, f32 = jnp.bfloat16, jnp.float32
    dma = pltpu.SemaphoreType.DMA
    vmem = pl.BlockSpec(memory_space=pltpu.VMEM)
    hbm = pl.BlockSpec(memory_space=pl.ANY)
    smem = pl.BlockSpec(memory_space=pltpu.SMEM)
    scratch = [
        pltpu.VMEM((N, 2, INNER * z.groups, HALF, D), bf16),
        pltpu.VMEM((N, 2, z.groups, BLOCK, D), bf16),
        *[pltpu.VMEM((N, 2, CHANGED, HALF, D), bf16)] * 4,
        pltpu.VMEM((N, 2, CHANGED, INNER, HALF, D), bf16),
        pltpu.VMEM((N, z.keys, ROWS), f32),
        pltpu.VMEM((N, z.keys, ROWS), f32),
        pltpu.VMEM((N, A * INNER, 16, BLOCK), f32),
        pltpu.VMEM((N, 2, z.groups, BLOCK, D), bf16),
        pltpu.VMEM((N, A, INNER, C * R, D), bf16),
        pltpu.VMEM((N, A, C * R, D), bf16),
        pltpu.VMEM((N, A, C, R, D), bf16),
        pltpu.VMEM((N, A * C - 1, R, D), bf16),
        dma((1,)), dma((N,)),
        dma((1,)), dma((N,)),
        *[dma((N,))] * 8,
        dma((1,)), dma((N,)),
        dma((1,)), dma((1,)), dma((1,)),
        dma((N,)), dma((N,)),
        dma((1,)), dma((N,)),
    ]
    outs = (
        jax.ShapeDtypeStruct((R, z.width * C), bf16),
        jax.ShapeDtypeStruct(keys.shape, bf16),
        jax.ShapeDtypeStruct(values.shape, bf16),
    )
    found = pl.pallas_call(
        functools.partial(split_kernel, z),
        out_shape=outs,
        in_specs=[smem, smem, hbm, hbm, hbm, hbm],
        out_specs=(vmem, hbm, hbm),
        scratch_shapes=scratch,
        compiler_params=pltpu.CompilerParams(
            collective_id=1, has_side_effects=True, vmem_limit_bytes=56 * 1024 * 1024
        ),
    )(changed_blocks, half_mask.T, queries, dout, keys, values)
    return found


def solution(mesh):
    rows = P(("seq", "ulys"), None)
    seq, ulys = mesh.shape["seq"], mesh.shape["ulys"]

    def run(queries, keys, values, dout, changed_blocks, half_mask):
        body = split_local if Split.fits(seq, ulys, queries.shape[1]) else local
        return body(seq, ulys, queries, keys, values, dout, changed_blocks, half_mask)

    return jax.shard_map(
        run,
        mesh=mesh,
        in_specs=(rows, rows, rows, rows, P(), P()),
        out_specs=(P("seq", "ulys"), rows, rows),
        check_vma=False,
    )
```

```python
import functools

import jax
import jax.numpy as jnp
from jax import lax
from jax.experimental import pallas as pl
from jax.experimental.pallas import tpu as pltpu
from jax.sharding import PartitionSpec as P

HEAD_DIM = 128
BLOCK = 128
PART = 32
CHANGED = 4
ROWS = CHANGED * BLOCK
CORES = 2
INNER = 2
SCALE = 1.0 / HEAD_DIM**0.5
HALF = BLOCK // 2
PIECES = 2
SPAN = CHANGED // PIECES
DELAYS = (0, 2, 4, 6, 9, 12, 15, 18)
MESH = pl.DeviceIdType.MESH


class Sizes:
    def __init__(self, seq, ulys, width):
        self.ulys = ulys
        self.inner = INNER
        self.outer = seq // (INNER * CORES)
        self.width = width // ulys
        self.heads = self.width // HEAD_DIM
        self.group = 2 if self.heads % 2 == 0 else 1
        self.cols = self.group * HEAD_DIM
        self.chunks = self.heads // self.group
        self.shard = ROWS // seq
        self.seq = seq
        self.keys = ulys * BLOCK
        self.stat_rows = -(-3 * self.group // 8) * 8
        self.sum_type = jnp.bfloat16 if self.shard >= 16 else jnp.float32


def contract(a, b, dims):
    return lax.dot_general(a, b, (dims, ((), ())), preferred_element_type=jnp.float32)


def kernel(
    z,
    changed, live, q_in, do_in, k_in, v_in,
    dq_out, dk_out, dv_out,
    ybuf, kv, z0, zr, zl, zro, zlo, full,
    expo, dpro, stb, sta, fin, ret,
    dq0, dq1, dt1, dq2, dt2, dq3,
    y_s, y_r, kv_s, kv_r, zs, zrs, f_s, f_r,
    sb_s, sb_r, sa_s, sa_r, ret_s, ret_r,
    d1_s, d1_r, d2_s, d2_r, d3_s, d3_r,
):
    seq = lax.axis_index("seq")
    u = lax.axis_index("ulys")
    c = lax.rem(seq, CORES)
    b = lax.rem(seq // CORES, z.inner)
    a = seq // (CORES * z.inner)
    U, B, A, G, W, N, g = z.ulys, z.inner, z.outer, z.cols, z.width, z.chunks, z.group

    def dev(a_, b_, c_, u_):
        return ((a_ * B + b_) * CORES + c_, u_)

    def copy(src, dst, ss, rs, to):
        return pltpu.make_async_remote_copy(
            src_ref=src, dst_ref=dst, send_sem=ss, recv_sem=rs, device_id=to, device_id_type=MESH
        )

    def at_u(d):
        return lax.rem(u + d, U)

    def at_c(d):
        return lax.rem(c + d, CORES)

    def at_b(d):
        return lax.rem(b + d, B)

    def at_a(d):
        return lax.rem(a + d, A)

    def col(block, i):
        return pl.ds(pl.multiple_of(block * W + i * G, HEAD_DIM), G)

    part = b * CORES + c
    near = [(db, dc) for db in range(B) for dc in range(CORES)]
    pairs = [(du, k) for k in range(len(near)) for du in range(U)]

    def near_dev(k, u_):
        return dev(a, at_b(near[k][0]), at_c(near[k][1]), u_)

    def part_of(k):
        return at_b(near[k][0]) * CORES + at_c(near[k][1])

    peers = [near_dev(k, at_u(du)) for du, k in pairs if du or k]
    peers += [dev(at_a(d), b, c, u) for d in range(1, A)]
    barrier = pltpu.get_barrier_semaphore()
    for peer in peers:
        pl.semaphore_signal(barrier, inc=1, device_id=peer, device_id_type=MESH)
    pl.semaphore_wait(barrier, len(peers))

    def y_rows(k):
        return pl.ds(pl.multiple_of(part_of(k) * PART, PART), PART)

    def y_copy(i, n, du, k):
        ref = (q_in, do_in)[n]
        return copy(
            ref.at[y_rows(k), col(at_u(du), i)], ybuf.at[i, n, du, k],
            y_s.at[0 if du else 1], y_r.at[i], near_dev(k, at_u(du)),
        )

    def y_own(i, n):
        ref = (q_in, do_in)[n]
        return pltpu.make_async_copy(
            ref.at[y_rows(0), col(u, i)], ybuf.at[i, n, 0, 0], y_r.at[i]
        )

    def kv_own(i, n):
        ref = (k_in, v_in)[n]
        return pltpu.make_async_copy(ref.at[:, col(u, i)], kv.at[i, n, 0], kv_r.at[i])

    def kv_copy(i, n, du):
        ref = (k_in, v_in)[n]
        return copy(
            ref.at[:, col(at_u(du), i)], kv.at[i, n, du],
            kv_s.at[0], kv_r.at[i], dev(a, b, c, at_u(du)),
        )

    def each(body):
        def step(i, carry):
            body(i)
            return carry

        lax.fori_loop(0, N, step, 0)

    def send_y(i):
        for n in range(2):
            y_own(i, n).start()
            for du, k in pairs:
                if du or k:
                    y_copy(i, n, du, k).start()

    def send_kv(i):
        for n in range(2):
            kv_own(i, n).start()
            for du in range(1, U):
                kv_copy(i, n, du).start()

    each(send_y)
    each(send_kv)

    def line(i, p, n, right, left, src, rin, lin, rout, lout, ss, rs):
        def r_copy():
            return copy(rout.at[i], rin.at[i], ss.at[i, 0], rs.at[i, 0], right)

        def l_copy():
            return copy(lout.at[i], lin.at[i], ss.at[i, 1], rs.at[i, 1], left)

        def do_right():
            @pl.when(p == 0)
            def _():
                rin[i] = jnp.zeros(rin.shape[1:], rin.dtype)

            @pl.when(p > 0)
            def _():
                r_copy().wait_recv()

            @pl.when(p < n - 1)
            def _():
                rout[i] = src[i] + rin[i]
                r_copy().start()

        def do_left():
            @pl.when(p == n - 1)
            def _():
                lin[i] = jnp.zeros(lin.shape[1:], lin.dtype)

            @pl.when(p < n - 1)
            def _():
                l_copy().wait_recv()

            @pl.when(p > 0)
            def _():
                lout[i] = src[i] + lin[i]
                l_copy().start()

        def hop(h):
            pl.when(p == h)(do_right)
            pl.when(p == n - 1 - h)(do_left)

        def finish():
            @pl.when(p < n - 1)
            def _():
                r_copy().wait_send()

            @pl.when(p > 0)
            def _():
                l_copy().wait_send()

        return hop, finish

    def z_line(i):
        return line(
            i, a, A, dev(lax.rem(a + 1, A), b, c, u), dev(lax.rem(a + A - 1, A), b, c, u),
            z0, zr, zl, zro, zlo, zs, zrs,
        )

    def select(i):
        pltpu.make_async_copy(ybuf.at[i], ybuf.at[i], y_r.at[i]).wait()
        for n in range(2):
            totals = [None] * CHANGED
            for du, k in pairs:
                from_b = lax.rem(b + B - near[k][0], B)
                from_c = lax.rem(c + CORES - near[k][1], CORES)
                from_u = lax.rem(u + U - du, U)
                block = ((a * B + from_b) * CORES + from_c) * U + from_u
                piece = ybuf[i, n, du, k]
                for slot in range(CHANGED):
                    weight = jnp.where(changed[slot] == block, 1.0, 0.0)
                    if n == 1:
                        weight = weight * jnp.where(
                            b == 0, live[slot, 0], live[slot, 1]
                        ).astype(jnp.float32)
                    weight = jnp.full((PART, G), weight, jnp.float32).astype(jnp.bfloat16)
                    term = piece * weight
                    totals[slot] = term if totals[slot] is None else totals[slot] + term
            for slot in range(CHANGED):
                z0[i, n, slot] = totals[slot]
        z_line(i)[0](0)

    def hop(h, i):
        z_line(i)[0](h)

    def spread_copy(i, n, came=False):
        at = (part, part, at_b(1) * CORES + c)[n]
        to = (dev(a, b, at_c(1), u), dev(a, at_b(1), c, u), dev(a, b, at_c(1), u))[n]
        if came:
            at_in = (
                b * CORES + at_c(1), at_b(1) * CORES + c, at_b(1) * CORES + at_c(1)
            )[n]
            return copy(full.at[i, at], full.at[i, at_in], f_s.at[i, n], f_r.at[i, n], to)
        return copy(full.at[i, at], full.at[i, at], f_s.at[i, n], f_r.at[i, n], to)

    def spread(i):
        z_line(i)[0](A - 1)
        full[i, part] = z0[i] + zr[i] + zl[i]
        spread_copy(i, 1).start()
        spread_copy(i, 0).start()

    def relay(i):
        spread_copy(i, 1, True).wait_recv()
        spread_copy(i, 2).start()

    def head(j):
        return slice(j * HEAD_DIM, (j + 1) * HEAD_DIM)

    def q_of(i, j):
        return full[i, :, 0, :, :, head(j)].reshape(ROWS, HEAD_DIM)

    def do_of(i, j):
        return full[i, :, 1, :, :, head(j)].reshape(ROWS, HEAD_DIM)

    def kv_of(i, n, j):
        return kv[i, n, :, :, head(j)].reshape(z.keys, HEAD_DIM)

    def b_stat(i, k):
        return copy(
            stb.at[i, 0], stb.at[i, k], sb_s.at[i, k], sb_r.at[i, k], near_dev(k, u)
        )

    def a_stat(i, d):
        return copy(
            sta.at[i, 0], sta.at[i, d], sa_s.at[i, d], sa_r.at[i, d], dev(at_a(d), b, c, u)
        )

    def first_pass(i):
        spread_copy(i, 0, True).wait_recv()
        spread_copy(i, 2, True).wait_recv()
        pltpu.make_async_copy(kv.at[i], kv.at[i], kv_r.at[i]).wait()
        for j in range(g):
            scores = contract(kv_of(i, 0, j), q_of(i, j), ((1,), (1,))) * SCALE
            top = jnp.max(scores, axis=0, keepdims=True)
            e = jnp.exp(scores - top)
            dp = contract(kv_of(i, 1, j), do_of(i, j), ((1,), (1,)))
            stb[i, 0, j : j + 1, :] = top
            stb[i, 0, g + j : g + j + 1, :] = jnp.sum(e, axis=0, keepdims=True)
            stb[i, 0, 2 * g + j : 2 * g + j + 1, :] = jnp.sum(e * dp, axis=0, keepdims=True)
            expo[i * g + j] = e
            dpro[i * g + j] = dp
        for row in range(3 * g, z.stat_rows):
            stb[i, 0, row : row + 1, :] = jnp.zeros((1, ROWS), jnp.float32)
        for k in range(1, len(near)):
            b_stat(i, k).start()

    def merge(src, i, n, dst):
        parts = [src[i, d] for d in range(n)]
        top = functools.reduce(jnp.maximum, [part[0:g] for part in parts])
        factors = [jnp.exp(part[0:g] - top) for part in parts]
        total = sum(part[g : 2 * g] * f for part, f in zip(parts, factors))
        weighted = sum(part[2 * g : 3 * g] * f for part, f in zip(parts, factors))
        dst[0:g, :] = top
        dst[g : 2 * g, :] = total
        dst[2 * g : 3 * g, :] = weighted
        if z.stat_rows > 3 * g:
            dst[3 * g :, :] = jnp.zeros((z.stat_rows - 3 * g, ROWS), jnp.float32)

    def stat_a(i):
        for k in range(1, len(near)):
            b_stat(i, k).wait_recv()
        merge(stb, i, len(near), sta.at[i, 0])
        for d in range(1, A):
            a_stat(i, d).start()

    def back(i, n, d):
        out = (dk_out, dv_out)[n]
        return copy(
            ret.at[i, n, d], out.at[:, col(u, i)], ret_s.at[i, n, d], ret_r.at[i, n, d],
            dev(a, b, c, lax.rem(u + U - d, U)),
        )

    def back_wait(i, n, d):
        out = (dk_out, dv_out)[n]
        return copy(
            ret.at[i, n, d], out.at[:, col(at_u(d), i)], ret_s.at[i, n, d], ret_r.at[i, n, d],
            dev(a, b, c, lax.rem(u + U - d, U)),
        )

    def c_dq(i):
        return copy(
            dq0.at[i, at_c(1)], dq1.at[i], d1_s.at[i], d1_r.at[i], dev(a, b, at_c(1), u)
        )

    def b_dq(i, d):
        return copy(
            dt1.at[i, at_b(d)], dq2.at[i, d], d2_s.at[i, d], d2_r.at[i, d], dev(a, at_b(d), c, u)
        )

    def a_dq(i, d):
        return copy(
            dt2.at[i, at_a(d)], dq3.at[i, d], d3_s.at[i, d], d3_r.at[i, d], dev(at_a(d), b, c, u)
        )

    def second_pass(i):
        for d in range(1, A):
            a_stat(i, d).wait_recv()
        merge(sta, i, A, fin.at[i])
        for j in range(g):
            factor = jnp.exp(stb[i, 0, j : j + 1, :] - fin[i, j : j + 1, :])
            total = fin[i, g + j : g + j + 1, :]
            factor = factor / total
            delta = fin[i, 2 * g + j : 2 * g + j + 1, :] / total
            probs = expo[i * g + j] * factor
            ds = (probs * (dpro[i * g + j] - delta)).astype(jnp.bfloat16)
            dk = (contract(ds, q_of(i, j), ((1,), (0,))) * SCALE).astype(jnp.bfloat16)
            dv = contract(probs.astype(jnp.bfloat16), do_of(i, j), ((1,), (0,)))
            dv = dv.astype(jnp.bfloat16)
            ret[i, 0, :, :, head(j)] = dk.reshape(U, BLOCK, HEAD_DIM)
            ret[i, 1, :, :, head(j)] = dv.reshape(U, BLOCK, HEAD_DIM)
            dq = contract(ds, kv_of(i, 0, j), ((0,), (0,))) * SCALE
            for s in range(z.seq):
                row = s * z.shard
                at = (row % BLOCK) // PART * (CHANGED * PART) + row // BLOCK * PART + row % PART
                dq0[i, s % CORES, s // CORES % B, s // (CORES * B), :, head(j)] = dq[
                    at : at + z.shard
                ]
        c_dq(i).start()
        for n in range(2):
            for d in range(1, U):
                back(i, n, d).start()
        dk_out[:, col(u, i)] = ret[i, 0, 0]
        dv_out[:, col(u, i)] = ret[i, 1, 0]

    def dq_b(i):
        c_dq(i).wait_recv()
        dt1[i] = (dq0[i, c] + dq1[i]).astype(z.sum_type)
        for d in range(1, B):
            b_dq(i, d).start()

    def dq_a(i):
        total = dt1[i, b].astype(jnp.float32)
        for d in range(1, B):
            b_dq(i, d).wait_recv()
            total = total + dq2[i, d].astype(jnp.float32)
        dt2[i] = total.astype(z.sum_type)
        for d in range(1, A):
            a_dq(i, d).start()

    def dq_end(i):
        total = dt2[i, a].astype(jnp.float32)
        for d in range(1, A):
            a_dq(i, d).wait_recv()
            total = total + dq3[i, d].astype(jnp.float32)
        dq_out[:, pl.ds(pl.multiple_of(i * G, HEAD_DIM), G)] = total.astype(jnp.bfloat16)

    stages = [select, *[functools.partial(hop, h) for h in range(1, A - 1)], spread, relay]
    stages += [first_pass, stat_a, second_pass, dq_b, dq_a, dq_end]

    def step(t, carry):
        for delay, stage in enumerate(stages):
            i = t - delay
            pl.when((i >= 0) & (i < N))(functools.partial(stage, i))
        return carry

    lax.fori_loop(0, N + len(stages) - 1, step, 0)

    def drain(i):
        for n in range(2):
            for d in range(1, U):
                back(i, n, d).wait_send()
                back_wait(i, n, d).wait_recv()
        z_line(i)[1]()
        for n in range(3):
            spread_copy(i, n).wait_send()
        for k in range(1, len(near)):
            b_stat(i, k).wait_send()
        c_dq(i).wait_send()
        for d in range(1, B):
            b_dq(i, d).wait_send()
        for d in range(1, A):
            a_stat(i, d).wait_send()
            a_dq(i, d).wait_send()

    each(drain)
    far, close, others = ybuf.at[:, :, 1:], ybuf.at[:, :, 0, 1:], kv.at[:, :, 1:]
    pltpu.make_async_copy(far, far, y_s.at[0]).wait()
    pltpu.make_async_copy(close, close, y_s.at[1]).wait()
    pltpu.make_async_copy(others, others, kv_s.at[0]).wait()


def local(seq_size, ulys_size, queries, keys, values, dout, changed_blocks, half_mask):
    z = Sizes(seq_size, ulys_size, queries.shape[1])
    N, U, B, A, G, R = z.chunks, z.ulys, z.inner, z.outer, z.cols, z.shard
    bf16, f32 = jnp.bfloat16, jnp.float32
    line = pltpu.VMEM((N, 2, CHANGED, PART, G), bf16)
    near = INNER * CORES
    stat = (z.stat_rows, ROWS)
    dma = pltpu.SemaphoreType.DMA
    vmem = pl.BlockSpec(memory_space=pltpu.VMEM)
    hbm = pl.BlockSpec(memory_space=pl.ANY)
    smem = pl.BlockSpec(memory_space=pltpu.SMEM)
    scratch = [
        pltpu.VMEM((N, 2, U, near, PART, G), bf16),
        pltpu.VMEM((N, 2, U, BLOCK, G), bf16),
        *[line] * 5,
        pltpu.VMEM((N, near, 2, CHANGED, PART, G), bf16),
        pltpu.VMEM((z.heads, z.keys, ROWS), f32),
        pltpu.VMEM((z.heads, z.keys, ROWS), f32),
        pltpu.VMEM((N, near, *stat), f32),
        pltpu.VMEM((N, A, *stat), f32),
        pltpu.VMEM((N, *stat), f32),
        pltpu.VMEM((N, 2, U, BLOCK, G), bf16),
        pltpu.VMEM((N, CORES, B, A, R, G), f32),
        pltpu.VMEM((N, B, A, R, G), f32),
        pltpu.VMEM((N, B, A, R, G), z.sum_type),
        pltpu.VMEM((N, B, A, R, G), z.sum_type),
        pltpu.VMEM((N, A, R, G), z.sum_type),
        pltpu.VMEM((N, A, R, G), z.sum_type),
        dma((2,)),
        dma((N,)),
        dma((1,)),
        dma((N,)),
        *[dma((N, 2))] * 2,
        *[dma((N, 3))] * 2,
        *[dma((N, near))] * 2,
        *[dma((N, A))] * 2,
        *[dma((N, 2, U))] * 2,
        *[dma((N,))] * 2,
        *[dma((N, B))] * 2,
        *[dma((N, A))] * 2,
    ]
    return pl.pallas_call(
        functools.partial(kernel, z),
        out_shape=(
            jax.ShapeDtypeStruct((R, z.width), bf16),
            jax.ShapeDtypeStruct(keys.shape, bf16),
            jax.ShapeDtypeStruct(values.shape, bf16),
        ),
        in_specs=[smem, smem, hbm, hbm, hbm, hbm],
        out_specs=(vmem, vmem, vmem),
        scratch_shapes=scratch,
        compiler_params=pltpu.CompilerParams(
            collective_id=0, has_side_effects=True, vmem_limit_bytes=62 * 1024 * 1024
        ),
    )(changed_blocks, half_mask, queries, dout, keys, values)


class Split:
    def __init__(self, seq, ulys, width):
        self.ulys = ulys
        self.outer = seq // (INNER * CORES)
        self.groups = ulys * CORES
        self.width = width // self.groups
        self.chunks = self.width // HEAD_DIM
        self.seq = seq
        self.shard = ROWS // seq
        self.keys = self.groups * BLOCK

    @staticmethod
    def fits(seq, ulys, width):
        return (
            width % (ulys * CORES * HEAD_DIM) == 0
            and seq == INNER * CORES * CHANGED
            and ROWS // seq % 16 == 0
            and ulys * CORES * BLOCK <= 512
        )


def split_kernel(
    z,
    changed, live, q_in, do_in, k_in, v_in,
    dq_out, dk_out, dv_out,
    ybuf, kv, z0, za, zb, zc, full, expo, dpro, stats, ret, dq0, dq1, dt1, dq2,
    y_s, y_r, kv_s, kv_r, za_s, za_r, zb_s, zb_r, g_s, g_r, x_s, x_r, st_s, st_r,
    o_s, o_r, l_s, d1_s, d1_r, d2_s, d2_r,
):
    seq = lax.axis_index("seq")
    u = lax.axis_index("ulys")
    c = lax.rem(seq, CORES)
    b = lax.rem(seq // CORES, INNER)
    a = seq // (CORES * INNER)
    U, B, A, C, W, N = z.ulys, INNER, z.outer, CORES, z.width, z.chunks
    D = HEAD_DIM

    def dev(da, db, dc, du):
        a_, b_, c_, u_ = at_a(da), at_b(db), at_c(dc), at_u(du)
        return ((a_ * B + b_) * C + c_, u_)

    def at_u(d):
        return lax.rem(u + U + d, U)

    def at_c(d):
        return lax.rem(c + C + d, C)

    def at_b(d):
        return lax.rem(b + B + d, B)

    def at_a(d):
        return lax.rem(a + A + d, A)

    def copy(src, dst, ss, rs, to):
        return pltpu.make_async_remote_copy(
            src_ref=src, dst_ref=dst, send_sem=ss, recv_sem=rs, device_id=to, device_id_type=MESH
        )

    def arrived(ref, sem):
        pltpu.make_async_copy(ref, ref, sem).wait()

    def col(u_, c_, i):
        return pl.ds(pl.multiple_of((u_ * C + c_) * W + i * D, D), D)

    owners = [(du, dc) for du in range(U) for dc in range(C)]
    near = [(db, du, dc) for db in range(B) for du, dc in owners]
    others = [(da, db) for da in range(A) for db in range(B)]
    rows = [(da, dc) for da in range(A) for dc in range(C)]

    peers = {(0, db, dc, du) for db, du, dc in near}
    peers |= {(da, db, 0, 0) for da, db in others}
    peers |= {(da, 0, dc, 0) for da, dc in rows}
    peers = sorted(peers - {(0, 0, 0, 0)})
    barrier = pltpu.get_barrier_semaphore()
    for peer in peers:
        pl.semaphore_signal(barrier, inc=1, device_id=dev(*peer), device_id_type=MESH)
    pl.semaphore_wait(barrier, len(peers))

    def send_y(i):
        for k, (db, du, dc) in enumerate(near):
            part = pl.ds(pl.multiple_of(at_b(db) * HALF, HALF), HALF)
            for n, ref in enumerate((q_in, do_in)):
                src = ref.at[part, col(at_u(du), at_c(dc), i)]
                if k:
                    copy(src, ybuf.at[i, n, k], y_s.at[0], y_r.at[i], dev(0, db, dc, du)).start()
                else:
                    pltpu.make_async_copy(src, ybuf.at[i, n, k], y_r.at[i]).start()

    def send_kv(i):
        for k, (du, dc) in enumerate(owners):
            for n, ref in enumerate((k_in, v_in)):
                src = ref.at[:, col(at_u(du), at_c(dc), i)]
                if k:
                    copy(src, kv.at[i, n, k], kv_s.at[0], kv_r.at[i], dev(0, 0, dc, du)).start()
                else:
                    pltpu.make_async_copy(src, kv.at[i, n, k], kv_r.at[i]).start()

    def each(body):
        def step(i, carry):
            body(i)
            return carry

        lax.fori_loop(0, N, step, 0)

    each(send_y)

    def select(i):
        send_kv(i)
        arrived(ybuf.at[i], y_r.at[i])
        totals = [[None] * CHANGED for _ in range(2)]
        for k, (db, du, dc) in enumerate(near):
            block = ((a * B + at_b(-db)) * C + at_c(-dc)) * U + at_u(-du)
            pieces = [ybuf[i, n, k] for n in range(2)]
            for slot in range(CHANGED):
                here = jnp.where(changed[slot] == block, 1.0, 0.0)
                lives = jnp.where(b == 0, live[0, slot], live[1, slot]).astype(jnp.float32)
                for n, weight in enumerate((here, here * lives)):
                    weight = jnp.full((HALF, D), weight, jnp.float32).astype(jnp.bfloat16)
                    term = pieces[n] * weight
                    old = totals[n][slot]
                    totals[n][slot] = term if old is None else old + term
        for slot in range(CHANGED):
            for n in range(2):
                z0[i, n, slot] = totals[n][slot]

        @pl.when(outside)
        def _():
            for p in range(PIECES):
                pair_copy(i, p).start()

    mate = a + 1 - 2 * lax.rem(a, 2)
    outside = (a == 0) | (a == A - 1)
    inside = (a != 0) & (a != A - 1)

    def line_dev(a_):
        return ((a_ * B + b) * C + c, u)

    def some(p):
        return slice(p * SPAN, (p + 1) * SPAN)

    def pair_copy(i, p):
        return copy(
            z0.at[i, :, some(p)], za.at[i, :, some(p)], za_s.at[i, p], za_r.at[i, p], line_dev(mate)
        )

    def middle_copy(i, p):
        return copy(
            zb.at[i, :, some(p)], zc.at[i, :, some(p)], zb_s.at[i, p], zb_r.at[i, p],
            line_dev(A - 1 - a),
        )

    def back_copy(i, p):
        here = full.at[i, :, some(p), b]
        return copy(here, here, g_s.at[i, p], g_r.at[i, p], line_dev(mate))

    def x_copy(i, p, came=False):
        here = full.at[i, :, some(p), b]
        there = full.at[i, :, some(p), at_b(1)] if came else here
        return copy(here, there, x_s.at[i, p], x_r.at[i, p], dev(0, 1, 0, 0))

    def middle(i):
        @pl.when(inside)
        def _():
            for p in range(PIECES):
                pair_copy(i, p).wait_recv()
                zb[i, :, some(p)] = z0[i, :, some(p)] + za[i, :, some(p)]
                middle_copy(i, p).start()

    def give_back(i):
        @pl.when(inside)
        def _():
            for p in range(PIECES):
                middle_copy(i, p).wait_recv()
                full[i, :, some(p), b] = zb[i, :, some(p)] + zc[i, :, some(p)]
                back_copy(i, p).start()
                x_copy(i, p).start()

    def across(i):
        @pl.when(outside)
        def _():
            for p in range(PIECES):
                back_copy(i, p).wait_recv()
                x_copy(i, p).start()

    def q_of(i, n):
        return full[i, n].reshape(ROWS, D)

    def kv_of(i, n):
        return kv[i, n].reshape(z.keys, D)

    def first_pass(i):
        for p in range(PIECES):
            x_copy(i, p, True).wait_recv()
        arrived(kv.at[i], kv_r.at[i])
        scores = contract(kv_of(i, 0), q_of(i, 0), ((1,), (1,))) * SCALE
        top = jnp.max(scores, axis=0, keepdims=True)
        e = jnp.exp(scores - top)
        dp = contract(kv_of(i, 1), q_of(i, 1), ((1,), (1,)))
        found = (top, jnp.sum(e, axis=0, keepdims=True), jnp.sum(e * dp, axis=0, keepdims=True))
        expo[i] = e
        dpro[i] = dp
        for r, row in enumerate(found):
            for j in range(CHANGED):
                at = r * CHANGED + j
                stats[i, 0, at : at + 1, :] = row[:, j * BLOCK : (j + 1) * BLOCK]
        stats[i, 0, 3 * CHANGED :, :] = jnp.zeros((CHANGED, BLOCK), jnp.float32)
        for k, (da, db) in enumerate(others):
            if k:
                copy(
                    stats.at[i, 0], stats.at[i, k], st_s.at[0], st_r.at[i], dev(da, db, 0, 0)
                ).start()

    def wide(x):
        return jnp.concatenate([x[j : j + 1] for j in range(CHANGED)], axis=1)

    def second_pass(i):
        arrived(stats.at[i, 1:], st_r.at[i])
        parts = [stats[i, k] for k in range(len(others))]
        tops = [part[0:CHANGED] for part in parts]
        top = functools.reduce(jnp.maximum, tops)
        factors = [jnp.exp(t - top) for t in tops]
        total = sum(p[CHANGED : 2 * CHANGED] * f for p, f in zip(parts, factors))
        weighted = sum(p[2 * CHANGED : 3 * CHANGED] * f for p, f in zip(parts, factors))
        factor = wide(factors[0] / total)
        delta = wide(weighted / total)
        probs = expo[i] * factor
        ds = (probs * (dpro[i] - delta)).astype(jnp.bfloat16)
        dq = contract(ds, kv_of(i, 0), ((0,), (0,))) * SCALE
        dq0[i] = dq.astype(jnp.bfloat16).reshape(A, B, z.shard * C, D)
        dq_x(i).start()
        dk = (contract(ds, q_of(i, 0), ((1,), (0,))) * SCALE).astype(jnp.bfloat16)
        ret[i, 0] = dk.reshape(len(owners), BLOCK, D)
        send_out(i, 0)
        dv = contract(probs.astype(jnp.bfloat16), q_of(i, 1), ((1,), (0,))).astype(jnp.bfloat16)
        ret[i, 1] = dv.reshape(len(owners), BLOCK, D)
        send_out(i, 1)

    def send_out(i, n):
        out = (dk_out, dv_out)[n].at[:, col(u, c, i)]
        for k, (du, dc) in enumerate(owners):
            if k:
                copy(ret.at[i, n, k], out, o_s.at[0], o_r.at[0], dev(0, 0, -dc, -du)).start()
            else:
                pltpu.make_async_copy(ret.at[i, n, k], out, l_s.at[0]).start()

    def dq_x(i):
        return copy(
            dq0.at[i, :, at_b(1)], dq1.at[i], d1_s.at[i], d1_r.at[i], dev(0, 1, 0, 0)
        )

    def dq_mid(i):
        dq_x(i).wait_recv()
        mine = dq0[i, :, b].astype(jnp.float32) + dq1[i].astype(jnp.float32)
        dt1[i] = mine.astype(jnp.bfloat16).reshape(A, C, z.shard, D)
        for k, (da, dc) in enumerate(rows):
            if k:
                copy(
                    dt1.at[i, at_a(da), at_c(dc)], dq2.at[i, k - 1],
                    d2_s.at[0], d2_r.at[i], dev(da, 0, dc, 0),
                ).start()

    def dq_end(i):
        arrived(dq2.at[i], d2_r.at[i])
        for dc in range(C):
            total = None
            for k, (da, e) in enumerate(rows):
                if e == dc:
                    term = (dq2[i, k - 1] if k else dt1[i, a, c]).astype(jnp.float32)
                    total = term if total is None else total + term
            at = pl.ds(pl.multiple_of(at_c(-dc) * W + i * D, D), D)
            dq_out[:, at] = total.astype(jnp.bfloat16)

    stages = [select, middle, give_back, across, first_pass, second_pass, dq_mid, dq_end]

    def step(t, carry):
        for stage, delay in reversed(list(zip(stages, DELAYS))):
            i = t - delay
            pl.when((i >= 0) & (i < N))(functools.partial(stage, i))
        return carry

    lax.fori_loop(0, N + DELAYS[-1], step, 0)

    def drain(i):
        for p in range(PIECES):
            @pl.when(outside)
            def _():
                pair_copy(i, p).wait_send()

            @pl.when(inside)
            def _():
                middle_copy(i, p).wait_send()
                back_copy(i, p).wait_send()

            x_copy(i, p).wait_send()

        dq_x(i).wait_send()
        for k in range(1, len(others)):
            arrived(stats.at[i, k], st_s.at[0])

    each(drain)
    arrived(ybuf.at[:, :, 1:], y_s.at[0])
    arrived(kv.at[:, :, 1:], kv_s.at[0])
    arrived(dq2, d2_s.at[0])
    arrived(ret.at[:, :, 1:], o_s.at[0])
    arrived(ret.at[:, :, 1:], o_r.at[0])
    arrived(ret.at[:, :, 0], l_s.at[0])


def hand_over(dq_in, dk_in, dv_in, dq_out, dk_out, dv_out, dq, dk, dv, in_s, out_s):
    held = (dq, dk, dv)
    loads = [
        pltpu.make_async_copy(src, held[n], in_s.at[n])
        for n, src in enumerate((dq_in, dk_in, dv_in))
    ]
    stores = [
        pltpu.make_async_copy(held[n], dst, out_s.at[n])
        for n, dst in enumerate((dq_out, dk_out, dv_out))
    ]
    for load in loads:
        load.start()
    for load, store in zip(loads, stores):
        load.wait()
        store.start()
    for store in stores:
        store.wait()


def split_local(seq_size, ulys_size, queries, keys, values, dout, changed_blocks, half_mask):
    z = Split(seq_size, ulys_size, queries.shape[1])
    N, U, A, C, D, R = z.chunks, z.ulys, z.outer, CORES, HEAD_DIM, z.shard
    bf16, f32 = jnp.bfloat16, jnp.float32
    dma = pltpu.SemaphoreType.DMA
    vmem = pl.BlockSpec(memory_space=pltpu.VMEM)
    hbm = pl.BlockSpec(memory_space=pl.ANY)
    smem = pl.BlockSpec(memory_space=pltpu.SMEM)
    scratch = [
        pltpu.VMEM((N, 2, INNER * z.groups, HALF, D), bf16),
        pltpu.VMEM((N, 2, z.groups, BLOCK, D), bf16),
        *[pltpu.VMEM((N, 2, CHANGED, HALF, D), bf16)] * 4,
        pltpu.VMEM((N, 2, CHANGED, INNER, HALF, D), bf16),
        pltpu.VMEM((N, z.keys, ROWS), f32),
        pltpu.VMEM((N, z.keys, ROWS), f32),
        pltpu.VMEM((N, A * INNER, 16, BLOCK), f32),
        pltpu.VMEM((N, 2, z.groups, BLOCK, D), bf16),
        pltpu.VMEM((N, A, INNER, C * R, D), bf16),
        pltpu.VMEM((N, A, C * R, D), bf16),
        pltpu.VMEM((N, A, C, R, D), bf16),
        pltpu.VMEM((N, A * C - 1, R, D), bf16),
        dma((1,)), dma((N,)),
        dma((1,)), dma((N,)),
        *[dma((N, PIECES))] * 8,
        dma((1,)), dma((N,)),
        dma((1,)), dma((1,)), dma((1,)),
        dma((N,)), dma((N,)),
        dma((1,)), dma((N,)),
    ]
    outs = (
        jax.ShapeDtypeStruct((R, z.width * C), bf16),
        jax.ShapeDtypeStruct(keys.shape, bf16),
        jax.ShapeDtypeStruct(values.shape, bf16),
    )
    found = pl.pallas_call(
        functools.partial(split_kernel, z),
        out_shape=outs,
        in_specs=[smem, smem, hbm, hbm, hbm, hbm],
        out_specs=(vmem, hbm, hbm),
        scratch_shapes=scratch,
        compiler_params=pltpu.CompilerParams(
            collective_id=1, has_side_effects=True, vmem_limit_bytes=56 * 1024 * 1024
        ),
    )(changed_blocks, half_mask.T, queries, dout, keys, values)
    return pl.pallas_call(
        hand_over,
        out_shape=outs,
        in_specs=[hbm] * 3,
        out_specs=[hbm] * 3,
        scratch_shapes=[
            *[pltpu.VMEM(out.shape, bf16) for out in outs],
            dma((len(outs),)), dma((len(outs),)),
        ],
    )(*found)


def solution(mesh):
    rows = P(("seq", "ulys"), None)
    seq, ulys = mesh.shape["seq"], mesh.shape["ulys"]

    def run(queries, keys, values, dout, changed_blocks, half_mask):
        body = split_local if Split.fits(seq, ulys, queries.shape[1]) else local
        return body(seq, ulys, queries, keys, values, dout, changed_blocks, half_mask)

    return jax.shard_map(
        run,
        mesh=mesh,
        in_specs=(rows, rows, rows, rows, P(), P()),
        out_specs=(P("seq", "ulys"), rows, rows),
        check_vma=False,
    )
```

```python
import functools

import jax
import jax.numpy as jnp
from jax import lax
from jax.experimental import pallas as pl
from jax.experimental.pallas import tpu as pltpu
from jax.sharding import PartitionSpec as P

HEAD_DIM = 128
BLOCK = 128
PART = 32
CHANGED = 4
ROWS = CHANGED * BLOCK
CORES = 2
INNER = 2
SCALE = 1.0 / HEAD_DIM**0.5
HALF = BLOCK // 2
PIECES = 2
SPAN = CHANGED // PIECES
DELAYS = (0, 2, 4, 6, 9, 12, 15, 18)
MESH = pl.DeviceIdType.MESH


class Sizes:
    def __init__(self, seq, ulys, width):
        self.ulys = ulys
        self.inner = INNER
        self.outer = seq // (INNER * CORES)
        self.width = width // ulys
        self.heads = self.width // HEAD_DIM
        self.group = 2 if self.heads % 2 == 0 else 1
        self.cols = self.group * HEAD_DIM
        self.chunks = self.heads // self.group
        self.shard = ROWS // seq
        self.seq = seq
        self.keys = ulys * BLOCK
        self.stat_rows = -(-3 * self.group // 8) * 8
        self.sum_type = jnp.bfloat16 if self.shard >= 16 else jnp.float32


def contract(a, b, dims):
    return lax.dot_general(a, b, (dims, ((), ())), preferred_element_type=jnp.float32)


def kernel(
    z,
    changed, live, q_in, do_in, k_in, v_in,
    dq_out, dk_out, dv_out,
    ybuf, kv, z0, zr, zl, zro, zlo, full,
    expo, dpro, stb, sta, fin, ret,
    dq0, dq1, dt1, dq2, dt2, dq3,
    y_s, y_r, kv_s, kv_r, zs, zrs, f_s, f_r,
    sb_s, sb_r, sa_s, sa_r, ret_s, ret_r,
    d1_s, d1_r, d2_s, d2_r, d3_s, d3_r,
):
    seq = lax.axis_index("seq")
    u = lax.axis_index("ulys")
    c = lax.rem(seq, CORES)
    b = lax.rem(seq // CORES, z.inner)
    a = seq // (CORES * z.inner)
    U, B, A, G, W, N, g = z.ulys, z.inner, z.outer, z.cols, z.width, z.chunks, z.group

    def dev(a_, b_, c_, u_):
        return ((a_ * B + b_) * CORES + c_, u_)

    def copy(src, dst, ss, rs, to):
        return pltpu.make_async_remote_copy(
            src_ref=src, dst_ref=dst, send_sem=ss, recv_sem=rs, device_id=to, device_id_type=MESH
        )

    def at_u(d):
        return lax.rem(u + d, U)

    def at_c(d):
        return lax.rem(c + d, CORES)

    def at_b(d):
        return lax.rem(b + d, B)

    def at_a(d):
        return lax.rem(a + d, A)

    def col(block, i):
        return pl.ds(pl.multiple_of(block * W + i * G, HEAD_DIM), G)

    part = b * CORES + c
    near = [(db, dc) for db in range(B) for dc in range(CORES)]
    pairs = [(du, k) for k in range(len(near)) for du in range(U)]

    def near_dev(k, u_):
        return dev(a, at_b(near[k][0]), at_c(near[k][1]), u_)

    def part_of(k):
        return at_b(near[k][0]) * CORES + at_c(near[k][1])

    peers = [near_dev(k, at_u(du)) for du, k in pairs if du or k]
    peers += [dev(at_a(d), b, c, u) for d in range(1, A)]
    barrier = pltpu.get_barrier_semaphore()
    for peer in peers:
        pl.semaphore_signal(barrier, inc=1, device_id=peer, device_id_type=MESH)
    pl.semaphore_wait(barrier, len(peers))

    def y_rows(k):
        return pl.ds(pl.multiple_of(part_of(k) * PART, PART), PART)

    def y_copy(i, n, du, k):
        ref = (q_in, do_in)[n]
        return copy(
            ref.at[y_rows(k), col(at_u(du), i)], ybuf.at[i, n, du, k],
            y_s.at[0 if du else 1], y_r.at[i], near_dev(k, at_u(du)),
        )

    def y_own(i, n):
        ref = (q_in, do_in)[n]
        return pltpu.make_async_copy(
            ref.at[y_rows(0), col(u, i)], ybuf.at[i, n, 0, 0], y_r.at[i]
        )

    def kv_own(i, n):
        ref = (k_in, v_in)[n]
        return pltpu.make_async_copy(ref.at[:, col(u, i)], kv.at[i, n, 0], kv_r.at[i])

    def kv_copy(i, n, du):
        ref = (k_in, v_in)[n]
        return copy(
            ref.at[:, col(at_u(du), i)], kv.at[i, n, du],
            kv_s.at[0], kv_r.at[i], dev(a, b, c, at_u(du)),
        )

    def each(body):
        def step(i, carry):
            body(i)
            return carry

        lax.fori_loop(0, N, step, 0)

    def send_y(i):
        for n in range(2):
            y_own(i, n).start()
            for du, k in pairs:
                if du or k:
                    y_copy(i, n, du, k).start()

    def send_kv(i):
        for n in range(2):
            kv_own(i, n).start()
            for du in range(1, U):
                kv_copy(i, n, du).start()

    each(send_y)
    each(send_kv)

    def line(i, p, n, right, left, src, rin, lin, rout, lout, ss, rs):
        def r_copy():
            return copy(rout.at[i], rin.at[i], ss.at[i, 0], rs.at[i, 0], right)

        def l_copy():
            return copy(lout.at[i], lin.at[i], ss.at[i, 1], rs.at[i, 1], left)

        def do_right():
            @pl.when(p == 0)
            def _():
                rin[i] = jnp.zeros(rin.shape[1:], rin.dtype)

            @pl.when(p > 0)
            def _():
                r_copy().wait_recv()

            @pl.when(p < n - 1)
            def _():
                rout[i] = src[i] + rin[i]
                r_copy().start()

        def do_left():
            @pl.when(p == n - 1)
            def _():
                lin[i] = jnp.zeros(lin.shape[1:], lin.dtype)

            @pl.when(p < n - 1)
            def _():
                l_copy().wait_recv()

            @pl.when(p > 0)
            def _():
                lout[i] = src[i] + lin[i]
                l_copy().start()

        def hop(h):
            pl.when(p == h)(do_right)
            pl.when(p == n - 1 - h)(do_left)

        def finish():
            @pl.when(p < n - 1)
            def _():
                r_copy().wait_send()

            @pl.when(p > 0)
            def _():
                l_copy().wait_send()

        return hop, finish

    def z_line(i):
        return line(
            i, a, A, dev(lax.rem(a + 1, A), b, c, u), dev(lax.rem(a + A - 1, A), b, c, u),
            z0, zr, zl, zro, zlo, zs, zrs,
        )

    def select(i):
        pltpu.make_async_copy(ybuf.at[i], ybuf.at[i], y_r.at[i]).wait()
        for n in range(2):
            totals = [None] * CHANGED
            for du, k in pairs:
                from_b = lax.rem(b + B - near[k][0], B)
                from_c = lax.rem(c + CORES - near[k][1], CORES)
                from_u = lax.rem(u + U - du, U)
                block = ((a * B + from_b) * CORES + from_c) * U + from_u
                piece = ybuf[i, n, du, k]
                for slot in range(CHANGED):
                    weight = jnp.where(changed[slot] == block, 1.0, 0.0)
                    if n == 1:
                        weight = weight * jnp.where(
                            b == 0, live[slot, 0], live[slot, 1]
                        ).astype(jnp.float32)
                    weight = jnp.full((PART, G), weight, jnp.float32).astype(jnp.bfloat16)
                    term = piece * weight
                    totals[slot] = term if totals[slot] is None else totals[slot] + term
            for slot in range(CHANGED):
                z0[i, n, slot] = totals[slot]
        z_line(i)[0](0)

    def hop(h, i):
        z_line(i)[0](h)

    def spread_copy(i, n, came=False):
        at = (part, part, at_b(1) * CORES + c)[n]
        to = (dev(a, b, at_c(1), u), dev(a, at_b(1), c, u), dev(a, b, at_c(1), u))[n]
        if came:
            at_in = (
                b * CORES + at_c(1), at_b(1) * CORES + c, at_b(1) * CORES + at_c(1)
            )[n]
            return copy(full.at[i, at], full.at[i, at_in], f_s.at[i, n], f_r.at[i, n], to)
        return copy(full.at[i, at], full.at[i, at], f_s.at[i, n], f_r.at[i, n], to)

    def spread(i):
        z_line(i)[0](A - 1)
        full[i, part] = z0[i] + zr[i] + zl[i]
        spread_copy(i, 1).start()
        spread_copy(i, 0).start()

    def relay(i):
        spread_copy(i, 1, True).wait_recv()
        spread_copy(i, 2).start()

    def head(j):
        return slice(j * HEAD_DIM, (j + 1) * HEAD_DIM)

    def q_of(i, j):
        return full[i, :, 0, :, :, head(j)].reshape(ROWS, HEAD_DIM)

    def do_of(i, j):
        return full[i, :, 1, :, :, head(j)].reshape(ROWS, HEAD_DIM)

    def kv_of(i, n, j):
        return kv[i, n, :, :, head(j)].reshape(z.keys, HEAD_DIM)

    def b_stat(i, k):
        return copy(
            stb.at[i, 0], stb.at[i, k], sb_s.at[i, k], sb_r.at[i, k], near_dev(k, u)
        )

    def a_stat(i, d):
        return copy(
            sta.at[i, 0], sta.at[i, d], sa_s.at[i, d], sa_r.at[i, d], dev(at_a(d), b, c, u)
        )

    def first_pass(i):
        spread_copy(i, 0, True).wait_recv()
        spread_copy(i, 2, True).wait_recv()
        pltpu.make_async_copy(kv.at[i], kv.at[i], kv_r.at[i]).wait()
        for j in range(g):
            scores = contract(kv_of(i, 0, j), q_of(i, j), ((1,), (1,))) * SCALE
            top = jnp.max(scores, axis=0, keepdims=True)
            e = jnp.exp(scores - top)
            dp = contract(kv_of(i, 1, j), do_of(i, j), ((1,), (1,)))
            stb[i, 0, j : j + 1, :] = top
            stb[i, 0, g + j : g + j + 1, :] = jnp.sum(e, axis=0, keepdims=True)
            stb[i, 0, 2 * g + j : 2 * g + j + 1, :] = jnp.sum(e * dp, axis=0, keepdims=True)
            expo[i * g + j] = e
            dpro[i * g + j] = dp
        for row in range(3 * g, z.stat_rows):
            stb[i, 0, row : row + 1, :] = jnp.zeros((1, ROWS), jnp.float32)
        for k in range(1, len(near)):
            b_stat(i, k).start()

    def merge(src, i, n, dst):
        parts = [src[i, d] for d in range(n)]
        top = functools.reduce(jnp.maximum, [part[0:g] for part in parts])
        factors = [jnp.exp(part[0:g] - top) for part in parts]
        total = sum(part[g : 2 * g] * f for part, f in zip(parts, factors))
        weighted = sum(part[2 * g : 3 * g] * f for part, f in zip(parts, factors))
        dst[0:g, :] = top
        dst[g : 2 * g, :] = total
        dst[2 * g : 3 * g, :] = weighted
        if z.stat_rows > 3 * g:
            dst[3 * g :, :] = jnp.zeros((z.stat_rows - 3 * g, ROWS), jnp.float32)

    def stat_a(i):
        for k in range(1, len(near)):
            b_stat(i, k).wait_recv()
        merge(stb, i, len(near), sta.at[i, 0])
        for d in range(1, A):
            a_stat(i, d).start()

    def back(i, n, d):
        out = (dk_out, dv_out)[n]
        return copy(
            ret.at[i, n, d], out.at[:, col(u, i)], ret_s.at[i, n, d], ret_r.at[i, n, d],
            dev(a, b, c, lax.rem(u + U - d, U)),
        )

    def back_wait(i, n, d):
        out = (dk_out, dv_out)[n]
        return copy(
            ret.at[i, n, d], out.at[:, col(at_u(d), i)], ret_s.at[i, n, d], ret_r.at[i, n, d],
            dev(a, b, c, lax.rem(u + U - d, U)),
        )

    def c_dq(i):
        return copy(
            dq0.at[i, at_c(1)], dq1.at[i], d1_s.at[i], d1_r.at[i], dev(a, b, at_c(1), u)
        )

    def b_dq(i, d):
        return copy(
            dt1.at[i, at_b(d)], dq2.at[i, d], d2_s.at[i, d], d2_r.at[i, d], dev(a, at_b(d), c, u)
        )

    def a_dq(i, d):
        return copy(
            dt2.at[i, at_a(d)], dq3.at[i, d], d3_s.at[i, d], d3_r.at[i, d], dev(at_a(d), b, c, u)
        )

    def second_pass(i):
        for d in range(1, A):
            a_stat(i, d).wait_recv()
        merge(sta, i, A, fin.at[i])
        for j in range(g):
            factor = jnp.exp(stb[i, 0, j : j + 1, :] - fin[i, j : j + 1, :])
            total = fin[i, g + j : g + j + 1, :]
            factor = factor / total
            delta = fin[i, 2 * g + j : 2 * g + j + 1, :] / total
            probs = expo[i * g + j] * factor
            ds = (probs * (dpro[i * g + j] - delta)).astype(jnp.bfloat16)
            dk = (contract(ds, q_of(i, j), ((1,), (0,))) * SCALE).astype(jnp.bfloat16)
            dv = contract(probs.astype(jnp.bfloat16), do_of(i, j), ((1,), (0,)))
            dv = dv.astype(jnp.bfloat16)
            ret[i, 0, :, :, head(j)] = dk.reshape(U, BLOCK, HEAD_DIM)
            ret[i, 1, :, :, head(j)] = dv.reshape(U, BLOCK, HEAD_DIM)
            dq = contract(ds, kv_of(i, 0, j), ((0,), (0,))) * SCALE
            for s in range(z.seq):
                row = s * z.shard
                at = (row % BLOCK) // PART * (CHANGED * PART) + row // BLOCK * PART + row % PART
                dq0[i, s % CORES, s // CORES % B, s // (CORES * B), :, head(j)] = dq[
                    at : at + z.shard
                ]
        c_dq(i).start()
        for n in range(2):
            for d in range(1, U):
                back(i, n, d).start()
        dk_out[:, col(u, i)] = ret[i, 0, 0]
        dv_out[:, col(u, i)] = ret[i, 1, 0]

    def dq_b(i):
        c_dq(i).wait_recv()
        dt1[i] = (dq0[i, c] + dq1[i]).astype(z.sum_type)
        for d in range(1, B):
            b_dq(i, d).start()

    def dq_a(i):
        total = dt1[i, b].astype(jnp.float32)
        for d in range(1, B):
            b_dq(i, d).wait_recv()
            total = total + dq2[i, d].astype(jnp.float32)
        dt2[i] = total.astype(z.sum_type)
        for d in range(1, A):
            a_dq(i, d).start()

    def dq_end(i):
        total = dt2[i, a].astype(jnp.float32)
        for d in range(1, A):
            a_dq(i, d).wait_recv()
            total = total + dq3[i, d].astype(jnp.float32)
        dq_out[:, pl.ds(pl.multiple_of(i * G, HEAD_DIM), G)] = total.astype(jnp.bfloat16)

    stages = [select, *[functools.partial(hop, h) for h in range(1, A - 1)], spread, relay]
    stages += [first_pass, stat_a, second_pass, dq_b, dq_a, dq_end]

    def step(t, carry):
        for delay, stage in enumerate(stages):
            i = t - delay
            pl.when((i >= 0) & (i < N))(functools.partial(stage, i))
        return carry

    lax.fori_loop(0, N + len(stages) - 1, step, 0)

    def drain(i):
        for n in range(2):
            for d in range(1, U):
                back(i, n, d).wait_send()
                back_wait(i, n, d).wait_recv()
        z_line(i)[1]()
        for n in range(3):
            spread_copy(i, n).wait_send()
        for k in range(1, len(near)):
            b_stat(i, k).wait_send()
        c_dq(i).wait_send()
        for d in range(1, B):
            b_dq(i, d).wait_send()
        for d in range(1, A):
            a_stat(i, d).wait_send()
            a_dq(i, d).wait_send()

    each(drain)
    far, close, others = ybuf.at[:, :, 1:], ybuf.at[:, :, 0, 1:], kv.at[:, :, 1:]
    pltpu.make_async_copy(far, far, y_s.at[0]).wait()
    pltpu.make_async_copy(close, close, y_s.at[1]).wait()
    pltpu.make_async_copy(others, others, kv_s.at[0]).wait()


def local(seq_size, ulys_size, queries, keys, values, dout, changed_blocks, half_mask):
    z = Sizes(seq_size, ulys_size, queries.shape[1])
    N, U, B, A, G, R = z.chunks, z.ulys, z.inner, z.outer, z.cols, z.shard
    bf16, f32 = jnp.bfloat16, jnp.float32
    line = pltpu.VMEM((N, 2, CHANGED, PART, G), bf16)
    near = INNER * CORES
    stat = (z.stat_rows, ROWS)
    dma = pltpu.SemaphoreType.DMA
    vmem = pl.BlockSpec(memory_space=pltpu.VMEM)
    hbm = pl.BlockSpec(memory_space=pl.ANY)
    smem = pl.BlockSpec(memory_space=pltpu.SMEM)
    scratch = [
        pltpu.VMEM((N, 2, U, near, PART, G), bf16),
        pltpu.VMEM((N, 2, U, BLOCK, G), bf16),
        *[line] * 5,
        pltpu.VMEM((N, near, 2, CHANGED, PART, G), bf16),
        pltpu.VMEM((z.heads, z.keys, ROWS), f32),
        pltpu.VMEM((z.heads, z.keys, ROWS), f32),
        pltpu.VMEM((N, near, *stat), f32),
        pltpu.VMEM((N, A, *stat), f32),
        pltpu.VMEM((N, *stat), f32),
        pltpu.VMEM((N, 2, U, BLOCK, G), bf16),
        pltpu.VMEM((N, CORES, B, A, R, G), f32),
        pltpu.VMEM((N, B, A, R, G), f32),
        pltpu.VMEM((N, B, A, R, G), z.sum_type),
        pltpu.VMEM((N, B, A, R, G), z.sum_type),
        pltpu.VMEM((N, A, R, G), z.sum_type),
        pltpu.VMEM((N, A, R, G), z.sum_type),
        dma((2,)),
        dma((N,)),
        dma((1,)),
        dma((N,)),
        *[dma((N, 2))] * 2,
        *[dma((N, 3))] * 2,
        *[dma((N, near))] * 2,
        *[dma((N, A))] * 2,
        *[dma((N, 2, U))] * 2,
        *[dma((N,))] * 2,
        *[dma((N, B))] * 2,
        *[dma((N, A))] * 2,
    ]
    return pl.pallas_call(
        functools.partial(kernel, z),
        out_shape=(
            jax.ShapeDtypeStruct((R, z.width), bf16),
            jax.ShapeDtypeStruct(keys.shape, bf16),
            jax.ShapeDtypeStruct(values.shape, bf16),
        ),
        in_specs=[smem, smem, hbm, hbm, hbm, hbm],
        out_specs=(vmem, vmem, vmem),
        scratch_shapes=scratch,
        compiler_params=pltpu.CompilerParams(
            collective_id=0, has_side_effects=True, vmem_limit_bytes=62 * 1024 * 1024
        ),
    )(changed_blocks, half_mask, queries, dout, keys, values)


class Split:
    def __init__(self, seq, ulys, width):
        self.ulys = ulys
        self.outer = seq // (INNER * CORES)
        self.groups = ulys * CORES
        self.width = width // self.groups
        self.chunks = self.width // HEAD_DIM
        self.seq = seq
        self.shard = ROWS // seq
        self.keys = self.groups * BLOCK

    @staticmethod
    def fits(seq, ulys, width):
        return (
            width % (ulys * CORES * HEAD_DIM) == 0
            and seq == INNER * CORES * CHANGED
            and ROWS // seq % 16 == 0
            and ulys * CORES * BLOCK <= 512
        )


def split_kernel(
    z,
    changed, live, q_in, do_in, k_in, v_in,
    dq_out, dk_out, dv_out,
    ybuf, kv, z0, za, zb, zc, full, expo, dpro, stats, ret, dq0, dq1, dt1, dq2,
    y_s, y_r, kv_s, kv_r, za_s, za_r, zb_s, zb_r, g_s, g_r, x_s, x_r, st_s, st_r,
    o_s, o_r, l_s, d1_s, d1_r, d2_s, d2_r,
):
    seq = lax.axis_index("seq")
    u = lax.axis_index("ulys")
    c = lax.rem(seq, CORES)
    b = lax.rem(seq // CORES, INNER)
    a = seq // (CORES * INNER)
    U, B, A, C, W, N = z.ulys, INNER, z.outer, CORES, z.width, z.chunks
    D = HEAD_DIM

    def dev(da, db, dc, du):
        a_, b_, c_, u_ = at_a(da), at_b(db), at_c(dc), at_u(du)
        return ((a_ * B + b_) * C + c_, u_)

    def at_u(d):
        return lax.rem(u + U + d, U)

    def at_c(d):
        return lax.rem(c + C + d, C)

    def at_b(d):
        return lax.rem(b + B + d, B)

    def at_a(d):
        return lax.rem(a + A + d, A)

    def copy(src, dst, ss, rs, to):
        return pltpu.make_async_remote_copy(
            src_ref=src, dst_ref=dst, send_sem=ss, recv_sem=rs, device_id=to, device_id_type=MESH
        )

    def arrived(ref, sem):
        pltpu.make_async_copy(ref, ref, sem).wait()

    def col(u_, c_, i):
        return pl.ds(pl.multiple_of((u_ * C + c_) * W + i * D, D), D)

    owners = [(du, dc) for du in range(U) for dc in range(C)]
    near = [(db, du, dc) for db in range(B) for du, dc in owners]
    others = [(da, db) for da in range(A) for db in range(B)]
    rows = [(da, dc) for da in range(A) for dc in range(C)]

    mate = a + 1 - 2 * lax.rem(a, 2)
    outside = (a == 0) | (a == A - 1)
    inside = (a != 0) & (a != A - 1)

    def line_dev(a_):
        return ((a_ * B + b) * C + c, u)

    barrier = pltpu.get_barrier_semaphore()
    for db, du, dc in near:
        if db or du or dc:
            peer = dev(0, db, dc, du)
            pl.semaphore_signal(barrier, inc=1, device_id=peer, device_id_type=MESH)
    pl.semaphore_signal(barrier, inc=1, device_id=line_dev(mate), device_id_type=MESH)

    @pl.when(inside)
    def _():
        pl.semaphore_signal(barrier, inc=1, device_id=line_dev(A - 1 - a), device_id_type=MESH)
        pl.semaphore_wait(barrier, len(near) + 1)

    @pl.when(outside)
    def _():
        pl.semaphore_wait(barrier, len(near))

    def send_y(i):
        for k, (db, du, dc) in enumerate(near):
            part = pl.ds(pl.multiple_of(at_b(db) * HALF, HALF), HALF)
            for n, ref in enumerate((q_in, do_in)):
                src = ref.at[part, col(at_u(du), at_c(dc), i)]
                if k:
                    copy(src, ybuf.at[i, n, k], y_s.at[0], y_r.at[i], dev(0, db, dc, du)).start()
                else:
                    pltpu.make_async_copy(src, ybuf.at[i, n, k], y_r.at[i]).start()

    def send_kv(i):
        for k, (du, dc) in enumerate(owners):
            for n, ref in enumerate((k_in, v_in)):
                src = ref.at[:, col(at_u(du), at_c(dc), i)]
                if k:
                    copy(src, kv.at[i, n, k], kv_s.at[0], kv_r.at[i], dev(0, 0, dc, du)).start()
                else:
                    pltpu.make_async_copy(src, kv.at[i, n, k], kv_r.at[i]).start()

    def each(body):
        def step(i, carry):
            body(i)
            return carry

        lax.fori_loop(0, N, step, 0)

    each(send_y)

    def select(i):
        send_kv(i)
        arrived(ybuf.at[i], y_r.at[i])
        totals = [[None] * CHANGED for _ in range(2)]
        for k, (db, du, dc) in enumerate(near):
            block = ((a * B + at_b(-db)) * C + at_c(-dc)) * U + at_u(-du)
            pieces = [ybuf[i, n, k] for n in range(2)]
            for slot in range(CHANGED):
                here = jnp.where(changed[slot] == block, 1.0, 0.0)
                lives = jnp.where(b == 0, live[0, slot], live[1, slot]).astype(jnp.float32)
                for n, weight in enumerate((here, here * lives)):
                    weight = jnp.full((HALF, D), weight, jnp.float32).astype(jnp.bfloat16)
                    term = pieces[n] * weight
                    old = totals[n][slot]
                    totals[n][slot] = term if old is None else old + term
        for slot in range(CHANGED):
            for n in range(2):
                z0[i, n, slot] = totals[n][slot]

        @pl.when(outside)
        def _():
            for p in range(PIECES):
                pair_copy(i, p).start()

    def some(p):
        return slice(p * SPAN, (p + 1) * SPAN)

    def pair_copy(i, p):
        return copy(
            z0.at[i, :, some(p)], za.at[i, :, some(p)], za_s.at[i, p], za_r.at[i, p], line_dev(mate)
        )

    def middle_copy(i, p):
        return copy(
            zb.at[i, :, some(p)], zc.at[i, :, some(p)], zb_s.at[i, p], zb_r.at[i, p],
            line_dev(A - 1 - a),
        )

    def back_copy(i, p):
        here = full.at[i, :, some(p), b]
        return copy(here, here, g_s.at[i, p], g_r.at[i, p], line_dev(mate))

    def x_copy(i, p, came=False):
        here = full.at[i, :, some(p), b]
        there = full.at[i, :, some(p), at_b(1)] if came else here
        return copy(here, there, x_s.at[i, p], x_r.at[i, p], dev(0, 1, 0, 0))

    def middle(i):
        @pl.when(inside)
        def _():
            for p in range(PIECES):
                pair_copy(i, p).wait_recv()
                zb[i, :, some(p)] = z0[i, :, some(p)] + za[i, :, some(p)]
                middle_copy(i, p).start()

    def give_back(i):
        @pl.when(inside)
        def _():
            for p in range(PIECES):
                middle_copy(i, p).wait_recv()
                full[i, :, some(p), b] = zb[i, :, some(p)] + zc[i, :, some(p)]
                back_copy(i, p).start()
                x_copy(i, p).start()

    def across(i):
        @pl.when(outside)
        def _():
            for p in range(PIECES):
                back_copy(i, p).wait_recv()
                x_copy(i, p).start()

    def q_of(i, n):
        return full[i, n].reshape(ROWS, D)

    def kv_of(i, n):
        return kv[i, n].reshape(z.keys, D)

    def first_pass(i):
        for p in range(PIECES):
            x_copy(i, p, True).wait_recv()
        arrived(kv.at[i], kv_r.at[i])
        scores = contract(kv_of(i, 0), q_of(i, 0), ((1,), (1,))) * SCALE
        top = jnp.max(scores, axis=0, keepdims=True)
        e = jnp.exp(scores - top)
        dp = contract(kv_of(i, 1), q_of(i, 1), ((1,), (1,)))
        found = (top, jnp.sum(e, axis=0, keepdims=True), jnp.sum(e * dp, axis=0, keepdims=True))
        expo[i] = e
        dpro[i] = dp
        for r, row in enumerate(found):
            for j in range(CHANGED):
                at = r * CHANGED + j
                stats[i, 0, at : at + 1, :] = row[:, j * BLOCK : (j + 1) * BLOCK]
        stats[i, 0, 3 * CHANGED :, :] = jnp.zeros((CHANGED, BLOCK), jnp.float32)
        for k, (da, db) in enumerate(others):
            if k:
                copy(
                    stats.at[i, 0], stats.at[i, k], st_s.at[0], st_r.at[i], dev(da, db, 0, 0)
                ).start()

    def wide(x):
        return jnp.concatenate([x[j : j + 1] for j in range(CHANGED)], axis=1)

    def second_pass(i):
        arrived(stats.at[i, 1:], st_r.at[i])
        parts = [stats[i, k] for k in range(len(others))]
        tops = [part[0:CHANGED] for part in parts]
        top = functools.reduce(jnp.maximum, tops)
        factors = [jnp.exp(t - top) for t in tops]
        total = sum(p[CHANGED : 2 * CHANGED] * f for p, f in zip(parts, factors))
        weighted = sum(p[2 * CHANGED : 3 * CHANGED] * f for p, f in zip(parts, factors))
        factor = wide(factors[0] / total)
        delta = wide(weighted / total)
        probs = expo[i] * factor
        ds = (probs * (dpro[i] - delta)).astype(jnp.bfloat16)
        dq = contract(ds, kv_of(i, 0), ((0,), (0,))) * SCALE
        dq0[i] = dq.astype(jnp.bfloat16).reshape(A, B, z.shard * C, D)
        dq_x(i).start()
        dk = (contract(ds, q_of(i, 0), ((1,), (0,))) * SCALE).astype(jnp.bfloat16)
        ret[i, 0] = dk.reshape(len(owners), BLOCK, D)
        send_out(i, 0)
        dv = contract(probs.astype(jnp.bfloat16), q_of(i, 1), ((1,), (0,))).astype(jnp.bfloat16)
        ret[i, 1] = dv.reshape(len(owners), BLOCK, D)
        send_out(i, 1)

    def send_out(i, n):
        out = (dk_out, dv_out)[n].at[:, col(u, c, i)]
        for k, (du, dc) in enumerate(owners):
            if k:
                copy(ret.at[i, n, k], out, o_s.at[0], o_r.at[0], dev(0, 0, -dc, -du)).start()
            else:
                pltpu.make_async_copy(ret.at[i, n, k], out, l_s.at[0]).start()

    def dq_x(i):
        return copy(
            dq0.at[i, :, at_b(1)], dq1.at[i], d1_s.at[i], d1_r.at[i], dev(0, 1, 0, 0)
        )

    def dq_mid(i):
        dq_x(i).wait_recv()
        mine = dq0[i, :, b].astype(jnp.float32) + dq1[i].astype(jnp.float32)
        dt1[i] = mine.astype(jnp.bfloat16).reshape(A, C, z.shard, D)
        for k, (da, dc) in enumerate(rows):
            if k:
                copy(
                    dt1.at[i, at_a(da), at_c(dc)], dq2.at[i, k - 1],
                    d2_s.at[0], d2_r.at[i], dev(da, 0, dc, 0),
                ).start()

    def dq_end(i):
        arrived(dq2.at[i], d2_r.at[i])
        for dc in range(C):
            total = None
            for k, (da, e) in enumerate(rows):
                if e == dc:
                    term = (dq2[i, k - 1] if k else dt1[i, a, c]).astype(jnp.float32)
                    total = term if total is None else total + term
            at = pl.ds(pl.multiple_of(at_c(-dc) * W + i * D, D), D)
            dq_out[:, at] = total.astype(jnp.bfloat16)

    stages = [select, middle, give_back, across, first_pass, second_pass, dq_mid, dq_end]

    def step(t, carry):
        for stage, delay in reversed(list(zip(stages, DELAYS))):
            i = t - delay
            pl.when((i >= 0) & (i < N))(functools.partial(stage, i))
        return carry

    lax.fori_loop(0, N + DELAYS[-1], step, 0)

    def drain(i):
        for p in range(PIECES):
            @pl.when(outside)
            def _():
                pair_copy(i, p).wait_send()

            @pl.when(inside)
            def _():
                middle_copy(i, p).wait_send()
                back_copy(i, p).wait_send()

            x_copy(i, p).wait_send()

        dq_x(i).wait_send()
        for k in range(1, len(others)):
            arrived(stats.at[i, k], st_s.at[0])

    each(drain)
    arrived(ybuf.at[:, :, 1:], y_s.at[0])
    arrived(kv.at[:, :, 1:], kv_s.at[0])
    arrived(dq2, d2_s.at[0])
    arrived(ret.at[:, :, 1:], o_s.at[0])
    arrived(ret.at[:, :, 1:], o_r.at[0])
    arrived(ret.at[:, :, 0], l_s.at[0])


def hand_over(dq_in, dk_in, dv_in, dq_out, dk_out, dv_out, sems):
    pairs = ((dq_in, dq_out), (dk_in, dk_out), (dv_in, dv_out))
    copies = [pltpu.make_async_copy(src, dst, sems.at[n]) for n, (src, dst) in enumerate(pairs)]
    for one in copies:
        one.start()
    for one in copies:
        one.wait()


def split_local(seq_size, ulys_size, queries, keys, values, dout, changed_blocks, half_mask):
    z = Split(seq_size, ulys_size, queries.shape[1])
    N, U, A, C, D, R = z.chunks, z.ulys, z.outer, CORES, HEAD_DIM, z.shard
    bf16, f32 = jnp.bfloat16, jnp.float32
    dma = pltpu.SemaphoreType.DMA
    vmem = pl.BlockSpec(memory_space=pltpu.VMEM)
    hbm = pl.BlockSpec(memory_space=pl.ANY)
    smem = pl.BlockSpec(memory_space=pltpu.SMEM)
    scratch = [
        pltpu.VMEM((N, 2, INNER * z.groups, HALF, D), bf16),
        pltpu.VMEM((N, 2, z.groups, BLOCK, D), bf16),
        *[pltpu.VMEM((N, 2, CHANGED, HALF, D), bf16)] * 4,
        pltpu.VMEM((N, 2, CHANGED, INNER, HALF, D), bf16),
        pltpu.VMEM((N, z.keys, ROWS), f32),
        pltpu.VMEM((N, z.keys, ROWS), f32),
        pltpu.VMEM((N, A * INNER, 16, BLOCK), f32),
        pltpu.VMEM((N, 2, z.groups, BLOCK, D), bf16),
        pltpu.VMEM((N, A, INNER, C * R, D), bf16),
        pltpu.VMEM((N, A, C * R, D), bf16),
        pltpu.VMEM((N, A, C, R, D), bf16),
        pltpu.VMEM((N, A * C - 1, R, D), bf16),
        dma((1,)), dma((N,)),
        dma((1,)), dma((N,)),
        *[dma((N, PIECES))] * 8,
        dma((1,)), dma((N,)),
        dma((1,)), dma((1,)), dma((1,)),
        dma((N,)), dma((N,)),
        dma((1,)), dma((N,)),
    ]
    outs = (
        jax.ShapeDtypeStruct((R, z.width * C), bf16),
        jax.ShapeDtypeStruct(keys.shape, bf16),
        jax.ShapeDtypeStruct(values.shape, bf16),
    )
    found = pl.pallas_call(
        functools.partial(split_kernel, z),
        out_shape=tuple(pltpu.VMEM(out.shape, bf16) for out in outs),
        in_specs=[smem, smem, hbm, hbm, hbm, hbm],
        out_specs=(vmem, vmem, vmem),
        scratch_shapes=scratch,
        compiler_params=pltpu.CompilerParams(
            collective_id=1, has_side_effects=True, vmem_limit_bytes=56 * 1024 * 1024
        ),
    )(changed_blocks, half_mask.T, queries, dout, keys, values)
    return pl.pallas_call(
        hand_over,
        out_shape=outs,
        in_specs=[vmem] * 3,
        out_specs=[hbm] * 3,
        scratch_shapes=[dma((len(outs),))],
    )(*[pltpu.with_memory_space_constraint(x, pltpu.VMEM) for x in found])


def solution(mesh):
    rows = P(("seq", "ulys"), None)
    seq, ulys = mesh.shape["seq"], mesh.shape["ulys"]

    def run(queries, keys, values, dout, changed_blocks, half_mask):
        body = split_local if Split.fits(seq, ulys, queries.shape[1]) else local
        return body(seq, ulys, queries, keys, values, dout, changed_blocks, half_mask)

    return jax.shard_map(
        run,
        mesh=mesh,
        in_specs=(rows, rows, rows, rows, P(), P()),
        out_specs=(P("seq", "ulys"), rows, rows),
        check_vma=False,
    )
```

```python
import functools

import jax
import jax.numpy as jnp
from jax import lax
from jax.experimental import pallas as pl
from jax.experimental.pallas import tpu as pltpu
from jax.sharding import PartitionSpec as P

HEAD_DIM = 128
BLOCK = 128
PART = 32
CHANGED = 4
ROWS = CHANGED * BLOCK
CORES = 2
INNER = 2
SCALE = 1.0 / HEAD_DIM**0.5
HALF = BLOCK // 2
PIECES = 2
SPAN = CHANGED // PIECES
DELAYS = (0, 2, 4, 6, 9, 12, 15, 18)
MESH = pl.DeviceIdType.MESH


class Sizes:
    def __init__(self, seq, ulys, width):
        self.ulys = ulys
        self.inner = INNER
        self.outer = seq // (INNER * CORES)
        self.width = width // ulys
        self.heads = self.width // HEAD_DIM
        self.group = 2 if self.heads % 2 == 0 else 1
        self.cols = self.group * HEAD_DIM
        self.chunks = self.heads // self.group
        self.shard = ROWS // seq
        self.seq = seq
        self.keys = ulys * BLOCK
        self.stat_rows = -(-3 * self.group // 8) * 8
        self.sum_type = jnp.bfloat16 if self.shard >= 16 else jnp.float32


def contract(a, b, dims):
    return lax.dot_general(a, b, (dims, ((), ())), preferred_element_type=jnp.float32)


def kernel(
    z,
    changed, live, q_in, do_in, k_in, v_in,
    dq_out, dk_out, dv_out,
    ybuf, kv, z0, zr, zl, zro, zlo, full,
    expo, dpro, stb, sta, fin, ret,
    dq0, dq1, dt1, dq2, dt2, dq3,
    y_s, y_r, kv_s, kv_r, zs, zrs, f_s, f_r,
    sb_s, sb_r, sa_s, sa_r, ret_s, ret_r,
    d1_s, d1_r, d2_s, d2_r, d3_s, d3_r,
):
    seq = lax.axis_index("seq")
    u = lax.axis_index("ulys")
    c = lax.rem(seq, CORES)
    b = lax.rem(seq // CORES, z.inner)
    a = seq // (CORES * z.inner)
    U, B, A, G, W, N, g = z.ulys, z.inner, z.outer, z.cols, z.width, z.chunks, z.group

    def dev(a_, b_, c_, u_):
        return ((a_ * B + b_) * CORES + c_, u_)

    def copy(src, dst, ss, rs, to):
        return pltpu.make_async_remote_copy(
            src_ref=src, dst_ref=dst, send_sem=ss, recv_sem=rs, device_id=to, device_id_type=MESH
        )

    def at_u(d):
        return lax.rem(u + d, U)

    def at_c(d):
        return lax.rem(c + d, CORES)

    def at_b(d):
        return lax.rem(b + d, B)

    def at_a(d):
        return lax.rem(a + d, A)

    def col(block, i):
        return pl.ds(pl.multiple_of(block * W + i * G, HEAD_DIM), G)

    part = b * CORES + c
    near = [(db, dc) for db in range(B) for dc in range(CORES)]
    pairs = [(du, k) for k in range(len(near)) for du in range(U)]

    def near_dev(k, u_):
        return dev(a, at_b(near[k][0]), at_c(near[k][1]), u_)

    def part_of(k):
        return at_b(near[k][0]) * CORES + at_c(near[k][1])

    peers = [near_dev(k, at_u(du)) for du, k in pairs if du or k]
    peers += [dev(at_a(d), b, c, u) for d in range(1, A)]
    barrier = pltpu.get_barrier_semaphore()
    for peer in peers:
        pl.semaphore_signal(barrier, inc=1, device_id=peer, device_id_type=MESH)
    pl.semaphore_wait(barrier, len(peers))

    def y_rows(k):
        return pl.ds(pl.multiple_of(part_of(k) * PART, PART), PART)

    def y_copy(i, n, du, k):
        ref = (q_in, do_in)[n]
        return copy(
            ref.at[y_rows(k), col(at_u(du), i)], ybuf.at[i, n, du, k],
            y_s.at[0 if du else 1], y_r.at[i], near_dev(k, at_u(du)),
        )

    def y_own(i, n):
        ref = (q_in, do_in)[n]
        return pltpu.make_async_copy(
            ref.at[y_rows(0), col(u, i)], ybuf.at[i, n, 0, 0], y_r.at[i]
        )

    def kv_own(i, n):
        ref = (k_in, v_in)[n]
        return pltpu.make_async_copy(ref.at[:, col(u, i)], kv.at[i, n, 0], kv_r.at[i])

    def kv_copy(i, n, du):
        ref = (k_in, v_in)[n]
        return copy(
            ref.at[:, col(at_u(du), i)], kv.at[i, n, du],
            kv_s.at[0], kv_r.at[i], dev(a, b, c, at_u(du)),
        )

    def each(body):
        def step(i, carry):
            body(i)
            return carry

        lax.fori_loop(0, N, step, 0)

    def send_y(i):
        for n in range(2):
            y_own(i, n).start()
            for du, k in pairs:
                if du or k:
                    y_copy(i, n, du, k).start()

    def send_kv(i):
        for n in range(2):
            kv_own(i, n).start()
            for du in range(1, U):
                kv_copy(i, n, du).start()

    each(send_y)
    each(send_kv)

    def line(i, p, n, right, left, src, rin, lin, rout, lout, ss, rs):
        def r_copy():
            return copy(rout.at[i], rin.at[i], ss.at[i, 0], rs.at[i, 0], right)

        def l_copy():
            return copy(lout.at[i], lin.at[i], ss.at[i, 1], rs.at[i, 1], left)

        def do_right():
            @pl.when(p == 0)
            def _():
                rin[i] = jnp.zeros(rin.shape[1:], rin.dtype)

            @pl.when(p > 0)
            def _():
                r_copy().wait_recv()

            @pl.when(p < n - 1)
            def _():
                rout[i] = src[i] + rin[i]
                r_copy().start()

        def do_left():
            @pl.when(p == n - 1)
            def _():
                lin[i] = jnp.zeros(lin.shape[1:], lin.dtype)

            @pl.when(p < n - 1)
            def _():
                l_copy().wait_recv()

            @pl.when(p > 0)
            def _():
                lout[i] = src[i] + lin[i]
                l_copy().start()

        def hop(h):
            pl.when(p == h)(do_right)
            pl.when(p == n - 1 - h)(do_left)

        def finish():
            @pl.when(p < n - 1)
            def _():
                r_copy().wait_send()

            @pl.when(p > 0)
            def _():
                l_copy().wait_send()

        return hop, finish

    def z_line(i):
        return line(
            i, a, A, dev(lax.rem(a + 1, A), b, c, u), dev(lax.rem(a + A - 1, A), b, c, u),
            z0, zr, zl, zro, zlo, zs, zrs,
        )

    def select(i):
        pltpu.make_async_copy(ybuf.at[i], ybuf.at[i], y_r.at[i]).wait()
        for n in range(2):
            totals = [None] * CHANGED
            for du, k in pairs:
                from_b = lax.rem(b + B - near[k][0], B)
                from_c = lax.rem(c + CORES - near[k][1], CORES)
                from_u = lax.rem(u + U - du, U)
                block = ((a * B + from_b) * CORES + from_c) * U + from_u
                piece = ybuf[i, n, du, k]
                for slot in range(CHANGED):
                    weight = jnp.where(changed[slot] == block, 1.0, 0.0)
                    if n == 1:
                        weight = weight * jnp.where(
                            b == 0, live[slot, 0], live[slot, 1]
                        ).astype(jnp.float32)
                    weight = jnp.full((PART, G), weight, jnp.float32).astype(jnp.bfloat16)
                    term = piece * weight
                    totals[slot] = term if totals[slot] is None else totals[slot] + term
            for slot in range(CHANGED):
                z0[i, n, slot] = totals[slot]
        z_line(i)[0](0)

    def hop(h, i):
        z_line(i)[0](h)

    def spread_copy(i, n, came=False):
        at = (part, part, at_b(1) * CORES + c)[n]
        to = (dev(a, b, at_c(1), u), dev(a, at_b(1), c, u), dev(a, b, at_c(1), u))[n]
        if came:
            at_in = (
                b * CORES + at_c(1), at_b(1) * CORES + c, at_b(1) * CORES + at_c(1)
            )[n]
            return copy(full.at[i, at], full.at[i, at_in], f_s.at[i, n], f_r.at[i, n], to)
        return copy(full.at[i, at], full.at[i, at], f_s.at[i, n], f_r.at[i, n], to)

    def spread(i):
        z_line(i)[0](A - 1)
        full[i, part] = z0[i] + zr[i] + zl[i]
        spread_copy(i, 1).start()
        spread_copy(i, 0).start()

    def relay(i):
        spread_copy(i, 1, True).wait_recv()
        spread_copy(i, 2).start()

    def head(j):
        return slice(j * HEAD_DIM, (j + 1) * HEAD_DIM)

    def q_of(i, j):
        return full[i, :, 0, :, :, head(j)].reshape(ROWS, HEAD_DIM)

    def do_of(i, j):
        return full[i, :, 1, :, :, head(j)].reshape(ROWS, HEAD_DIM)

    def kv_of(i, n, j):
        return kv[i, n, :, :, head(j)].reshape(z.keys, HEAD_DIM)

    def b_stat(i, k):
        return copy(
            stb.at[i, 0], stb.at[i, k], sb_s.at[i, k], sb_r.at[i, k], near_dev(k, u)
        )

    def a_stat(i, d):
        return copy(
            sta.at[i, 0], sta.at[i, d], sa_s.at[i, d], sa_r.at[i, d], dev(at_a(d), b, c, u)
        )

    def first_pass(i):
        spread_copy(i, 0, True).wait_recv()
        spread_copy(i, 2, True).wait_recv()
        pltpu.make_async_copy(kv.at[i], kv.at[i], kv_r.at[i]).wait()
        for j in range(g):
            scores = contract(kv_of(i, 0, j), q_of(i, j), ((1,), (1,))) * SCALE
            top = jnp.max(scores, axis=0, keepdims=True)
            e = jnp.exp(scores - top)
            dp = contract(kv_of(i, 1, j), do_of(i, j), ((1,), (1,)))
            stb[i, 0, j : j + 1, :] = top
            stb[i, 0, g + j : g + j + 1, :] = jnp.sum(e, axis=0, keepdims=True)
            stb[i, 0, 2 * g + j : 2 * g + j + 1, :] = jnp.sum(e * dp, axis=0, keepdims=True)
            expo[i * g + j] = e
            dpro[i * g + j] = dp
        for row in range(3 * g, z.stat_rows):
            stb[i, 0, row : row + 1, :] = jnp.zeros((1, ROWS), jnp.float32)
        for k in range(1, len(near)):
            b_stat(i, k).start()

    def merge(src, i, n, dst):
        parts = [src[i, d] for d in range(n)]
        top = functools.reduce(jnp.maximum, [part[0:g] for part in parts])
        factors = [jnp.exp(part[0:g] - top) for part in parts]
        total = sum(part[g : 2 * g] * f for part, f in zip(parts, factors))
        weighted = sum(part[2 * g : 3 * g] * f for part, f in zip(parts, factors))
        dst[0:g, :] = top
        dst[g : 2 * g, :] = total
        dst[2 * g : 3 * g, :] = weighted
        if z.stat_rows > 3 * g:
            dst[3 * g :, :] = jnp.zeros((z.stat_rows - 3 * g, ROWS), jnp.float32)

    def stat_a(i):
        for k in range(1, len(near)):
            b_stat(i, k).wait_recv()
        merge(stb, i, len(near), sta.at[i, 0])
        for d in range(1, A):
            a_stat(i, d).start()

    def back(i, n, d):
        out = (dk_out, dv_out)[n]
        return copy(
            ret.at[i, n, d], out.at[:, col(u, i)], ret_s.at[i, n, d], ret_r.at[i, n, d],
            dev(a, b, c, lax.rem(u + U - d, U)),
        )

    def back_wait(i, n, d):
        out = (dk_out, dv_out)[n]
        return copy(
            ret.at[i, n, d], out.at[:, col(at_u(d), i)], ret_s.at[i, n, d], ret_r.at[i, n, d],
            dev(a, b, c, lax.rem(u + U - d, U)),
        )

    def c_dq(i):
        return copy(
            dq0.at[i, at_c(1)], dq1.at[i], d1_s.at[i], d1_r.at[i], dev(a, b, at_c(1), u)
        )

    def b_dq(i, d):
        return copy(
            dt1.at[i, at_b(d)], dq2.at[i, d], d2_s.at[i, d], d2_r.at[i, d], dev(a, at_b(d), c, u)
        )

    def a_dq(i, d):
        return copy(
            dt2.at[i, at_a(d)], dq3.at[i, d], d3_s.at[i, d], d3_r.at[i, d], dev(at_a(d), b, c, u)
        )

    def second_pass(i):
        for d in range(1, A):
            a_stat(i, d).wait_recv()
        merge(sta, i, A, fin.at[i])
        for j in range(g):
            factor = jnp.exp(stb[i, 0, j : j + 1, :] - fin[i, j : j + 1, :])
            total = fin[i, g + j : g + j + 1, :]
            factor = factor / total
            delta = fin[i, 2 * g + j : 2 * g + j + 1, :] / total
            probs = expo[i * g + j] * factor
            ds = (probs * (dpro[i * g + j] - delta)).astype(jnp.bfloat16)
            dk = (contract(ds, q_of(i, j), ((1,), (0,))) * SCALE).astype(jnp.bfloat16)
            dv = contract(probs.astype(jnp.bfloat16), do_of(i, j), ((1,), (0,)))
            dv = dv.astype(jnp.bfloat16)
            ret[i, 0, :, :, head(j)] = dk.reshape(U, BLOCK, HEAD_DIM)
            ret[i, 1, :, :, head(j)] = dv.reshape(U, BLOCK, HEAD_DIM)
            dq = contract(ds, kv_of(i, 0, j), ((0,), (0,))) * SCALE
            for s in range(z.seq):
                row = s * z.shard
                at = (row % BLOCK) // PART * (CHANGED * PART) + row // BLOCK * PART + row % PART
                dq0[i, s % CORES, s // CORES % B, s // (CORES * B), :, head(j)] = dq[
                    at : at + z.shard
                ]
        c_dq(i).start()
        for n in range(2):
            for d in range(1, U):
                back(i, n, d).start()
        dk_out[:, col(u, i)] = ret[i, 0, 0]
        dv_out[:, col(u, i)] = ret[i, 1, 0]

    def dq_b(i):
        c_dq(i).wait_recv()
        dt1[i] = (dq0[i, c] + dq1[i]).astype(z.sum_type)
        for d in range(1, B):
            b_dq(i, d).start()

    def dq_a(i):
        total = dt1[i, b].astype(jnp.float32)
        for d in range(1, B):
            b_dq(i, d).wait_recv()
            total = total + dq2[i, d].astype(jnp.float32)
        dt2[i] = total.astype(z.sum_type)
        for d in range(1, A):
            a_dq(i, d).start()

    def dq_end(i):
        total = dt2[i, a].astype(jnp.float32)
        for d in range(1, A):
            a_dq(i, d).wait_recv()
            total = total + dq3[i, d].astype(jnp.float32)
        dq_out[:, pl.ds(pl.multiple_of(i * G, HEAD_DIM), G)] = total.astype(jnp.bfloat16)

    stages = [select, *[functools.partial(hop, h) for h in range(1, A - 1)], spread, relay]
    stages += [first_pass, stat_a, second_pass, dq_b, dq_a, dq_end]

    def step(t, carry):
        for delay, stage in enumerate(stages):
            i = t - delay
            pl.when((i >= 0) & (i < N))(functools.partial(stage, i))
        return carry

    lax.fori_loop(0, N + len(stages) - 1, step, 0)

    def drain(i):
        for n in range(2):
            for d in range(1, U):
                back(i, n, d).wait_send()
                back_wait(i, n, d).wait_recv()
        z_line(i)[1]()
        for n in range(3):
            spread_copy(i, n).wait_send()
        for k in range(1, len(near)):
            b_stat(i, k).wait_send()
        c_dq(i).wait_send()
        for d in range(1, B):
            b_dq(i, d).wait_send()
        for d in range(1, A):
            a_stat(i, d).wait_send()
            a_dq(i, d).wait_send()

    each(drain)
    far, close, others = ybuf.at[:, :, 1:], ybuf.at[:, :, 0, 1:], kv.at[:, :, 1:]
    pltpu.make_async_copy(far, far, y_s.at[0]).wait()
    pltpu.make_async_copy(close, close, y_s.at[1]).wait()
    pltpu.make_async_copy(others, others, kv_s.at[0]).wait()


def local(seq_size, ulys_size, queries, keys, values, dout, changed_blocks, half_mask):
    z = Sizes(seq_size, ulys_size, queries.shape[1])
    N, U, B, A, G, R = z.chunks, z.ulys, z.inner, z.outer, z.cols, z.shard
    bf16, f32 = jnp.bfloat16, jnp.float32
    line = pltpu.VMEM((N, 2, CHANGED, PART, G), bf16)
    near = INNER * CORES
    stat = (z.stat_rows, ROWS)
    dma = pltpu.SemaphoreType.DMA
    vmem = pl.BlockSpec(memory_space=pltpu.VMEM)
    hbm = pl.BlockSpec(memory_space=pl.ANY)
    smem = pl.BlockSpec(memory_space=pltpu.SMEM)
    scratch = [
        pltpu.VMEM((N, 2, U, near, PART, G), bf16),
        pltpu.VMEM((N, 2, U, BLOCK, G), bf16),
        *[line] * 5,
        pltpu.VMEM((N, near, 2, CHANGED, PART, G), bf16),
        pltpu.VMEM((z.heads, z.keys, ROWS), f32),
        pltpu.VMEM((z.heads, z.keys, ROWS), f32),
        pltpu.VMEM((N, near, *stat), f32),
        pltpu.VMEM((N, A, *stat), f32),
        pltpu.VMEM((N, *stat), f32),
        pltpu.VMEM((N, 2, U, BLOCK, G), bf16),
        pltpu.VMEM((N, CORES, B, A, R, G), f32),
        pltpu.VMEM((N, B, A, R, G), f32),
        pltpu.VMEM((N, B, A, R, G), z.sum_type),
        pltpu.VMEM((N, B, A, R, G), z.sum_type),
        pltpu.VMEM((N, A, R, G), z.sum_type),
        pltpu.VMEM((N, A, R, G), z.sum_type),
        dma((2,)),
        dma((N,)),
        dma((1,)),
        dma((N,)),
        *[dma((N, 2))] * 2,
        *[dma((N, 3))] * 2,
        *[dma((N, near))] * 2,
        *[dma((N, A))] * 2,
        *[dma((N, 2, U))] * 2,
        *[dma((N,))] * 2,
        *[dma((N, B))] * 2,
        *[dma((N, A))] * 2,
    ]
    return pl.pallas_call(
        functools.partial(kernel, z),
        out_shape=(
            jax.ShapeDtypeStruct((R, z.width), bf16),
            jax.ShapeDtypeStruct(keys.shape, bf16),
            jax.ShapeDtypeStruct(values.shape, bf16),
        ),
        in_specs=[smem, smem, hbm, hbm, hbm, hbm],
        out_specs=(vmem, vmem, vmem),
        scratch_shapes=scratch,
        compiler_params=pltpu.CompilerParams(
            collective_id=0, has_side_effects=True, vmem_limit_bytes=62 * 1024 * 1024
        ),
    )(changed_blocks, half_mask, queries, dout, keys, values)


class Split:
    def __init__(self, seq, ulys, width):
        self.ulys = ulys
        self.outer = seq // (INNER * CORES)
        self.groups = ulys * CORES
        self.width = width // self.groups
        self.chunks = self.width // HEAD_DIM
        self.seq = seq
        self.shard = ROWS // seq
        self.keys = self.groups * BLOCK

    @staticmethod
    def fits(seq, ulys, width):
        return (
            width % (ulys * CORES * HEAD_DIM) == 0
            and seq == INNER * CORES * CHANGED
            and ROWS // seq % 16 == 0
            and ulys * CORES * BLOCK <= 512
        )


def split_kernel(
    z,
    changed, live, q_in, do_in, k_in, v_in,
    dq_out, dk_out, dv_out,
    ybuf, kv, z0, za, zb, zc, full, expo, dpro, stats, sums, ret, dq0, dq1, dt1, dq2,
    y_s, y_r, kv_s, kv_r, za_s, za_r, zb_s, zb_r, g_s, g_r, x_s, x_r, st_s, st_r,
    o_s, o_r, l_s, d1_s, d1_r, d2_s, d2_r,
):
    seq = lax.axis_index("seq")
    u = lax.axis_index("ulys")
    c = lax.rem(seq, CORES)
    b = lax.rem(seq // CORES, INNER)
    a = seq // (CORES * INNER)
    U, B, A, C, W, N = z.ulys, INNER, z.outer, CORES, z.width, z.chunks
    D = HEAD_DIM

    def dev(da, db, dc, du):
        a_, b_, c_, u_ = at_a(da), at_b(db), at_c(dc), at_u(du)
        return ((a_ * B + b_) * C + c_, u_)

    def at_u(d):
        return lax.rem(u + U + d, U)

    def at_c(d):
        return lax.rem(c + C + d, C)

    def at_b(d):
        return lax.rem(b + B + d, B)

    def at_a(d):
        return lax.rem(a + A + d, A)

    def copy(src, dst, ss, rs, to):
        return pltpu.make_async_remote_copy(
            src_ref=src, dst_ref=dst, send_sem=ss, recv_sem=rs, device_id=to, device_id_type=MESH
        )

    def arrived(ref, sem):
        pltpu.make_async_copy(ref, ref, sem).wait()

    def col(u_, c_, i):
        return pl.ds(pl.multiple_of((u_ * C + c_) * W + i * D, D), D)

    owners = [(du, dc) for du in range(U) for dc in range(C)]
    near = [(db, du, dc) for db in range(B) for du, dc in owners]
    others = [(da, db) for da in range(A) for db in range(B)]
    rows = [(da, dc) for da in range(A) for dc in range(C)]

    mate = a + 1 - 2 * lax.rem(a, 2)
    outside = (a == 0) | (a == A - 1)
    inside = (a != 0) & (a != A - 1)

    def line_dev(a_):
        return ((a_ * B + b) * C + c, u)

    barrier = pltpu.get_barrier_semaphore()
    for db, du, dc in near:
        if db or du or dc:
            peer = dev(0, db, dc, du)
            pl.semaphore_signal(barrier, inc=1, device_id=peer, device_id_type=MESH)
    pl.semaphore_signal(barrier, inc=1, device_id=line_dev(mate), device_id_type=MESH)

    @pl.when(inside)
    def _():
        pl.semaphore_signal(barrier, inc=1, device_id=line_dev(A - 1 - a), device_id_type=MESH)
        pl.semaphore_wait(barrier, len(near) + 1)

    @pl.when(outside)
    def _():
        pl.semaphore_wait(barrier, len(near))

    def send_y(i):
        for k, (db, du, dc) in enumerate(near):
            part = pl.ds(pl.multiple_of(at_b(db) * HALF, HALF), HALF)
            for n, ref in enumerate((q_in, do_in)):
                src = ref.at[part, col(at_u(du), at_c(dc), i)]
                if k:
                    copy(src, ybuf.at[i, n, k], y_s.at[0], y_r.at[i], dev(0, db, dc, du)).start()
                else:
                    pltpu.make_async_copy(src, ybuf.at[i, n, k], y_r.at[i]).start()

    def send_kv(i):
        for k, (du, dc) in enumerate(owners):
            for n, ref in enumerate((k_in, v_in)):
                src = ref.at[:, col(at_u(du), at_c(dc), i)]
                if k:
                    copy(src, kv.at[i, n, k], kv_s.at[0], kv_r.at[i], dev(0, 0, dc, du)).start()
                else:
                    pltpu.make_async_copy(src, kv.at[i, n, k], kv_r.at[i]).start()

    def each(body):
        def step(i, carry):
            body(i)
            return carry

        lax.fori_loop(0, N, step, 0)

    each(send_y)

    def select(i):
        send_kv(i)
        arrived(ybuf.at[i], y_r.at[i])
        totals = [[None] * CHANGED for _ in range(2)]
        for k, (db, du, dc) in enumerate(near):
            block = ((a * B + at_b(-db)) * C + at_c(-dc)) * U + at_u(-du)
            pieces = [ybuf[i, n, k] for n in range(2)]
            for slot in range(CHANGED):
                here = jnp.where(changed[slot] == block, 1.0, 0.0)
                lives = jnp.where(b == 0, live[0, slot], live[1, slot]).astype(jnp.float32)
                for n, weight in enumerate((here, here * lives)):
                    weight = jnp.full((HALF, D), weight, jnp.float32).astype(jnp.bfloat16)
                    term = pieces[n] * weight
                    old = totals[n][slot]
                    totals[n][slot] = term if old is None else old + term
        for slot in range(CHANGED):
            for n in range(2):
                z0[i, n, slot] = totals[n][slot]

        @pl.when(outside)
        def _():
            for p in range(PIECES):
                pair_copy(i, p).start()

    def some(p):
        return slice(p * SPAN, (p + 1) * SPAN)

    def pair_copy(i, p):
        return copy(
            z0.at[i, :, some(p)], za.at[i, :, some(p)], za_s.at[i, p], za_r.at[i, p], line_dev(mate)
        )

    def middle_copy(i, p):
        return copy(
            zb.at[i, :, some(p)], zc.at[i, :, some(p)], zb_s.at[i, p], zb_r.at[i, p],
            line_dev(A - 1 - a),
        )

    def back_copy(i, p):
        here = full.at[i, :, some(p), b]
        return copy(here, here, g_s.at[i, p], g_r.at[i, p], line_dev(mate))

    def x_copy(i, p, came=False):
        here = full.at[i, :, some(p), b]
        there = full.at[i, :, some(p), at_b(1)] if came else here
        return copy(here, there, x_s.at[i, p], x_r.at[i, p], dev(0, 1, 0, 0))

    def middle(i):
        @pl.when(inside)
        def _():
            for p in range(PIECES):
                pair_copy(i, p).wait_recv()
                zb[i, :, some(p)] = z0[i, :, some(p)] + za[i, :, some(p)]
                middle_copy(i, p).start()

    def give_back(i):
        @pl.when(inside)
        def _():
            for p in range(PIECES):
                middle_copy(i, p).wait_recv()
                full[i, :, some(p), b] = zb[i, :, some(p)] + zc[i, :, some(p)]
                back_copy(i, p).start()
                x_copy(i, p).start()

    def across(i):
        @pl.when(outside)
        def _():
            for p in range(PIECES):
                back_copy(i, p).wait_recv()
                x_copy(i, p).start()

    def q_of(i, n):
        return full[i, n].reshape(ROWS, D)

    def kv_of(i, n):
        return kv[i, n].reshape(z.keys, D)

    def first_pass(i):
        for p in range(PIECES):
            x_copy(i, p, True).wait_recv()
        arrived(kv.at[i], kv_r.at[i])
        scores = contract(kv_of(i, 0), q_of(i, 0), ((1,), (1,))) * SCALE
        top = jnp.max(scores, axis=0, keepdims=True)
        e = jnp.exp(scores - top)
        dp = contract(kv_of(i, 1), q_of(i, 1), ((1,), (1,)))
        total = jnp.sum(e, axis=0, keepdims=True)
        mean = jnp.sum(e * dp, axis=0, keepdims=True) / total
        sums[i] = jnp.broadcast_to(total, sums.shape[1:])
        found = (top + jnp.log(total), mean)
        expo[i] = e
        dpro[i] = dp
        for r, row in enumerate(found):
            for j in range(CHANGED):
                at = r * CHANGED + j
                stats[i, 0, at : at + 1, :] = row[:, j * BLOCK : (j + 1) * BLOCK]
        for k, (da, db) in enumerate(others):
            if k:
                copy(
                    stats.at[i, 0], stats.at[i, k], st_s.at[0], st_r.at[i], dev(da, db, 0, 0)
                ).start()

    def wide(x):
        return jnp.concatenate([x[j : j + 1] for j in range(CHANGED)], axis=1)

    def second_pass(i):
        arrived(stats.at[i, 1:], st_r.at[i])
        parts = [stats[i, k] for k in range(len(others))]
        top = functools.reduce(jnp.maximum, [part[0:CHANGED] for part in parts])
        shares = [jnp.exp(part[0:CHANGED] - top) for part in parts]
        whole = sum(shares)
        means = sum(part[CHANGED:] * share for part, share in zip(parts, shares))
        factor = wide(shares[0] / whole) / sums[i, 0:1]
        delta = wide(means / whole)
        probs = expo[i] * factor
        ds = (probs * (dpro[i] - delta)).astype(jnp.bfloat16)
        dq = contract(ds, kv_of(i, 0), ((0,), (0,))) * SCALE
        dq0[i] = dq.astype(jnp.bfloat16).reshape(A, B, z.shard * C, D)
        dq_x(i).start()
        dk = (contract(ds, q_of(i, 0), ((1,), (0,))) * SCALE).astype(jnp.bfloat16)
        ret[i, 0] = dk.reshape(len(owners), BLOCK, D)
        send_out(i, 0)
        dv = contract(probs.astype(jnp.bfloat16), q_of(i, 1), ((1,), (0,))).astype(jnp.bfloat16)
        ret[i, 1] = dv.reshape(len(owners), BLOCK, D)
        send_out(i, 1)

    def send_out(i, n):
        out = (dk_out, dv_out)[n].at[:, col(u, c, i)]
        for k, (du, dc) in enumerate(owners):
            if k:
                copy(ret.at[i, n, k], out, o_s.at[0], o_r.at[0], dev(0, 0, -dc, -du)).start()
            else:
                pltpu.make_async_copy(ret.at[i, n, k], out, l_s.at[0]).start()

    def dq_x(i):
        return copy(
            dq0.at[i, :, at_b(1)], dq1.at[i], d1_s.at[i], d1_r.at[i], dev(0, 1, 0, 0)
        )

    def dq_mid(i):
        dq_x(i).wait_recv()
        mine = dq0[i, :, b].astype(jnp.float32) + dq1[i].astype(jnp.float32)
        dt1[i] = mine.astype(jnp.bfloat16).reshape(A, C, z.shard, D)
        for k, (da, dc) in enumerate(rows):
            if k:
                copy(
                    dt1.at[i, at_a(da), at_c(dc)], dq2.at[i, k - 1],
                    d2_s.at[0], d2_r.at[i], dev(da, 0, dc, 0),
                ).start()

    def dq_end(i):
        arrived(dq2.at[i], d2_r.at[i])
        for dc in range(C):
            total = None
            for k, (da, e) in enumerate(rows):
                if e == dc:
                    term = (dq2[i, k - 1] if k else dt1[i, a, c]).astype(jnp.float32)
                    total = term if total is None else total + term
            at = pl.ds(pl.multiple_of(at_c(-dc) * W + i * D, D), D)
            dq_out[:, at] = total.astype(jnp.bfloat16)

    stages = [select, middle, give_back, across, first_pass, second_pass, dq_mid, dq_end]

    def step(t, carry):
        for stage, delay in reversed(list(zip(stages, DELAYS))):
            i = t - delay
            pl.when((i >= 0) & (i < N))(functools.partial(stage, i))
        return carry

    lax.fori_loop(0, N + DELAYS[-1], step, 0)

    def drain(i):
        for p in range(PIECES):
            @pl.when(outside)
            def _():
                pair_copy(i, p).wait_send()

            @pl.when(inside)
            def _():
                middle_copy(i, p).wait_send()
                back_copy(i, p).wait_send()

            x_copy(i, p).wait_send()

        dq_x(i).wait_send()
        for k in range(1, len(others)):
            arrived(stats.at[i, k], st_s.at[0])

    each(drain)
    arrived(ybuf.at[:, :, 1:], y_s.at[0])
    arrived(kv.at[:, :, 1:], kv_s.at[0])
    arrived(dq2, d2_s.at[0])
    arrived(ret.at[:, :, 1:], o_s.at[0])
    arrived(ret.at[:, :, 1:], o_r.at[0])
    arrived(ret.at[:, :, 0], l_s.at[0])


def hand_over(dq_in, dk_in, dv_in, dq_out, dk_out, dv_out, sems):
    pairs = ((dq_in, dq_out), (dk_in, dk_out), (dv_in, dv_out))
    copies = [pltpu.make_async_copy(src, dst, sems.at[n]) for n, (src, dst) in enumerate(pairs)]
    for one in copies:
        one.start()
    for one in copies:
        one.wait()


def split_local(seq_size, ulys_size, queries, keys, values, dout, changed_blocks, half_mask):
    z = Split(seq_size, ulys_size, queries.shape[1])
    N, U, A, C, D, R = z.chunks, z.ulys, z.outer, CORES, HEAD_DIM, z.shard
    bf16, f32 = jnp.bfloat16, jnp.float32
    dma = pltpu.SemaphoreType.DMA
    vmem = pl.BlockSpec(memory_space=pltpu.VMEM)
    hbm = pl.BlockSpec(memory_space=pl.ANY)
    smem = pl.BlockSpec(memory_space=pltpu.SMEM)
    scratch = [
        pltpu.VMEM((N, 2, INNER * z.groups, HALF, D), bf16),
        pltpu.VMEM((N, 2, z.groups, BLOCK, D), bf16),
        *[pltpu.VMEM((N, 2, CHANGED, HALF, D), bf16)] * 4,
        pltpu.VMEM((N, 2, CHANGED, INNER, HALF, D), bf16),
        pltpu.VMEM((N, z.keys, ROWS), f32),
        pltpu.VMEM((N, z.keys, ROWS), f32),
        pltpu.VMEM((N, A * INNER, 2 * CHANGED, BLOCK), f32),
        pltpu.VMEM((N, 8, ROWS), f32),
        pltpu.VMEM((N, 2, z.groups, BLOCK, D), bf16),
        pltpu.VMEM((N, A, INNER, C * R, D), bf16),
        pltpu.VMEM((N, A, C * R, D), bf16),
        pltpu.VMEM((N, A, C, R, D), bf16),
        pltpu.VMEM((N, A * C - 1, R, D), bf16),
        dma((1,)), dma((N,)),
        dma((1,)), dma((N,)),
        *[dma((N, PIECES))] * 8,
        dma((1,)), dma((N,)),
        dma((1,)), dma((1,)), dma((1,)),
        dma((N,)), dma((N,)),
        dma((1,)), dma((N,)),
    ]
    outs = (
        jax.ShapeDtypeStruct((R, z.width * C), bf16),
        jax.ShapeDtypeStruct(keys.shape, bf16),
        jax.ShapeDtypeStruct(values.shape, bf16),
    )
    found = pl.pallas_call(
        functools.partial(split_kernel, z),
        out_shape=tuple(pltpu.VMEM(out.shape, bf16) for out in outs),
        in_specs=[smem, smem, hbm, hbm, hbm, hbm],
        out_specs=(vmem, vmem, vmem),
        scratch_shapes=scratch,
        compiler_params=pltpu.CompilerParams(
            collective_id=1, has_side_effects=True, vmem_limit_bytes=56 * 1024 * 1024
        ),
    )(changed_blocks, half_mask.T, queries, dout, keys, values)
    return pl.pallas_call(
        hand_over,
        out_shape=outs,
        in_specs=[vmem] * 3,
        out_specs=[hbm] * 3,
        scratch_shapes=[dma((len(outs),))],
    )(*[pltpu.with_memory_space_constraint(x, pltpu.VMEM) for x in found])


def solution(mesh):
    rows = P(("seq", "ulys"), None)
    seq, ulys = mesh.shape["seq"], mesh.shape["ulys"]

    def run(queries, keys, values, dout, changed_blocks, half_mask):
        body = split_local if Split.fits(seq, ulys, queries.shape[1]) else local
        return body(seq, ulys, queries, keys, values, dout, changed_blocks, half_mask)

    return jax.shard_map(
        run,
        mesh=mesh,
        in_specs=(rows, rows, rows, rows, P(), P()),
        out_specs=(P("seq", "ulys"), rows, rows),
        check_vma=False,
    )
```

```python
import functools

import jax
import jax.numpy as jnp
from jax import lax
from jax.experimental import pallas as pl
from jax.experimental.pallas import tpu as pltpu
from jax.sharding import PartitionSpec as P

HEAD_DIM = 128
BLOCK = 128
PART = 32
CHANGED = 4
ROWS = CHANGED * BLOCK
CORES = 2
INNER = 2
SCALE = 1.0 / HEAD_DIM**0.5
HALF = BLOCK // 2
PIECES = 2
DELAYS = (0, 2, 4, 6, 9, 12, 15, 18)
MESH = pl.DeviceIdType.MESH


class Sizes:
    def __init__(self, seq, ulys, width):
        self.ulys = ulys
        self.inner = INNER
        self.outer = seq // (INNER * CORES)
        self.width = width // ulys
        self.heads = self.width // HEAD_DIM
        self.group = 2 if self.heads % 2 == 0 else 1
        self.cols = self.group * HEAD_DIM
        self.chunks = self.heads // self.group
        self.shard = ROWS // seq
        self.seq = seq
        self.keys = ulys * BLOCK
        self.stat_rows = -(-3 * self.group // 8) * 8
        self.sum_type = jnp.bfloat16 if self.shard >= 16 else jnp.float32


def contract(a, b, dims):
    return lax.dot_general(a, b, (dims, ((), ())), preferred_element_type=jnp.float32)


def kernel(
    z,
    changed, live, q_in, do_in, k_in, v_in,
    dq_out, dk_out, dv_out,
    ybuf, kv, z0, zr, zl, zro, zlo, full,
    expo, dpro, stb, sta, fin, ret,
    dq0, dq1, dt1, dq2, dt2, dq3,
    y_s, y_r, kv_s, kv_r, zs, zrs, f_s, f_r,
    sb_s, sb_r, sa_s, sa_r, ret_s, ret_r,
    d1_s, d1_r, d2_s, d2_r, d3_s, d3_r,
):
    seq = lax.axis_index("seq")
    u = lax.axis_index("ulys")
    c = lax.rem(seq, CORES)
    b = lax.rem(seq // CORES, z.inner)
    a = seq // (CORES * z.inner)
    U, B, A, G, W, N, g = z.ulys, z.inner, z.outer, z.cols, z.width, z.chunks, z.group

    def dev(a_, b_, c_, u_):
        return ((a_ * B + b_) * CORES + c_, u_)

    def copy(src, dst, ss, rs, to):
        return pltpu.make_async_remote_copy(
            src_ref=src, dst_ref=dst, send_sem=ss, recv_sem=rs, device_id=to, device_id_type=MESH
        )

    def at_u(d):
        return lax.rem(u + d, U)

    def at_c(d):
        return lax.rem(c + d, CORES)

    def at_b(d):
        return lax.rem(b + d, B)

    def at_a(d):
        return lax.rem(a + d, A)

    def col(block, i):
        return pl.ds(pl.multiple_of(block * W + i * G, HEAD_DIM), G)

    part = b * CORES + c
    near = [(db, dc) for db in range(B) for dc in range(CORES)]
    pairs = [(du, k) for k in range(len(near)) for du in range(U)]

    def near_dev(k, u_):
        return dev(a, at_b(near[k][0]), at_c(near[k][1]), u_)

    def part_of(k):
        return at_b(near[k][0]) * CORES + at_c(near[k][1])

    peers = [near_dev(k, at_u(du)) for du, k in pairs if du or k]
    peers += [dev(at_a(d), b, c, u) for d in range(1, A)]
    barrier = pltpu.get_barrier_semaphore()
    for peer in peers:
        pl.semaphore_signal(barrier, inc=1, device_id=peer, device_id_type=MESH)
    pl.semaphore_wait(barrier, len(peers))

    def y_rows(k):
        return pl.ds(pl.multiple_of(part_of(k) * PART, PART), PART)

    def y_copy(i, n, du, k):
        ref = (q_in, do_in)[n]
        return copy(
            ref.at[y_rows(k), col(at_u(du), i)], ybuf.at[i, n, du, k],
            y_s.at[0 if du else 1], y_r.at[i], near_dev(k, at_u(du)),
        )

    def y_own(i, n):
        ref = (q_in, do_in)[n]
        return pltpu.make_async_copy(
            ref.at[y_rows(0), col(u, i)], ybuf.at[i, n, 0, 0], y_r.at[i]
        )

    def kv_own(i, n):
        ref = (k_in, v_in)[n]
        return pltpu.make_async_copy(ref.at[:, col(u, i)], kv.at[i, n, 0], kv_r.at[i])

    def kv_copy(i, n, du):
        ref = (k_in, v_in)[n]
        return copy(
            ref.at[:, col(at_u(du), i)], kv.at[i, n, du],
            kv_s.at[0], kv_r.at[i], dev(a, b, c, at_u(du)),
        )

    def each(body):
        def step(i, carry):
            body(i)
            return carry

        lax.fori_loop(0, N, step, 0)

    def send_y(i):
        for n in range(2):
            y_own(i, n).start()
            for du, k in pairs:
                if du or k:
                    y_copy(i, n, du, k).start()

    def send_kv(i):
        for n in range(2):
            kv_own(i, n).start()
            for du in range(1, U):
                kv_copy(i, n, du).start()

    each(send_y)
    each(send_kv)

    def line(i, p, n, right, left, src, rin, lin, rout, lout, ss, rs):
        def r_copy():
            return copy(rout.at[i], rin.at[i], ss.at[i, 0], rs.at[i, 0], right)

        def l_copy():
            return copy(lout.at[i], lin.at[i], ss.at[i, 1], rs.at[i, 1], left)

        def do_right():
            @pl.when(p == 0)
            def _():
                rin[i] = jnp.zeros(rin.shape[1:], rin.dtype)

            @pl.when(p > 0)
            def _():
                r_copy().wait_recv()

            @pl.when(p < n - 1)
            def _():
                rout[i] = src[i] + rin[i]
                r_copy().start()

        def do_left():
            @pl.when(p == n - 1)
            def _():
                lin[i] = jnp.zeros(lin.shape[1:], lin.dtype)

            @pl.when(p < n - 1)
            def _():
                l_copy().wait_recv()

            @pl.when(p > 0)
            def _():
                lout[i] = src[i] + lin[i]
                l_copy().start()

        def hop(h):
            pl.when(p == h)(do_right)
            pl.when(p == n - 1 - h)(do_left)

        def finish():
            @pl.when(p < n - 1)
            def _():
                r_copy().wait_send()

            @pl.when(p > 0)
            def _():
                l_copy().wait_send()

        return hop, finish

    def z_line(i):
        return line(
            i, a, A, dev(lax.rem(a + 1, A), b, c, u), dev(lax.rem(a + A - 1, A), b, c, u),
            z0, zr, zl, zro, zlo, zs, zrs,
        )

    def select(i):
        pltpu.make_async_copy(ybuf.at[i], ybuf.at[i], y_r.at[i]).wait()
        for n in range(2):
            totals = [None] * CHANGED
            for du, k in pairs:
                from_b = lax.rem(b + B - near[k][0], B)
                from_c = lax.rem(c + CORES - near[k][1], CORES)
                from_u = lax.rem(u + U - du, U)
                block = ((a * B + from_b) * CORES + from_c) * U + from_u
                piece = ybuf[i, n, du, k]
                for slot in range(CHANGED):
                    weight = jnp.where(changed[slot] == block, 1.0, 0.0)
                    if n == 1:
                        weight = weight * jnp.where(
                            b == 0, live[slot, 0], live[slot, 1]
                        ).astype(jnp.float32)
                    weight = jnp.full((PART, G), weight, jnp.float32).astype(jnp.bfloat16)
                    term = piece * weight
                    totals[slot] = term if totals[slot] is None else totals[slot] + term
            for slot in range(CHANGED):
                z0[i, n, slot] = totals[slot]
        z_line(i)[0](0)

    def hop(h, i):
        z_line(i)[0](h)

    def spread_copy(i, n, came=False):
        at = (part, part, at_b(1) * CORES + c)[n]
        to = (dev(a, b, at_c(1), u), dev(a, at_b(1), c, u), dev(a, b, at_c(1), u))[n]
        if came:
            at_in = (
                b * CORES + at_c(1), at_b(1) * CORES + c, at_b(1) * CORES + at_c(1)
            )[n]
            return copy(full.at[i, at], full.at[i, at_in], f_s.at[i, n], f_r.at[i, n], to)
        return copy(full.at[i, at], full.at[i, at], f_s.at[i, n], f_r.at[i, n], to)

    def spread(i):
        z_line(i)[0](A - 1)
        full[i, part] = z0[i] + zr[i] + zl[i]
        spread_copy(i, 1).start()
        spread_copy(i, 0).start()

    def relay(i):
        spread_copy(i, 1, True).wait_recv()
        spread_copy(i, 2).start()

    def head(j):
        return slice(j * HEAD_DIM, (j + 1) * HEAD_DIM)

    def q_of(i, j):
        return full[i, :, 0, :, :, head(j)].reshape(ROWS, HEAD_DIM)

    def do_of(i, j):
        return full[i, :, 1, :, :, head(j)].reshape(ROWS, HEAD_DIM)

    def kv_of(i, n, j):
        return kv[i, n, :, :, head(j)].reshape(z.keys, HEAD_DIM)

    def b_stat(i, k):
        return copy(
            stb.at[i, 0], stb.at[i, k], sb_s.at[i, k], sb_r.at[i, k], near_dev(k, u)
        )

    def a_stat(i, d):
        return copy(
            sta.at[i, 0], sta.at[i, d], sa_s.at[i, d], sa_r.at[i, d], dev(at_a(d), b, c, u)
        )

    def first_pass(i):
        spread_copy(i, 0, True).wait_recv()
        spread_copy(i, 2, True).wait_recv()
        pltpu.make_async_copy(kv.at[i], kv.at[i], kv_r.at[i]).wait()
        for j in range(g):
            scores = contract(kv_of(i, 0, j), q_of(i, j), ((1,), (1,))) * SCALE
            top = jnp.max(scores, axis=0, keepdims=True)
            e = jnp.exp(scores - top)
            dp = contract(kv_of(i, 1, j), do_of(i, j), ((1,), (1,)))
            stb[i, 0, j : j + 1, :] = top
            stb[i, 0, g + j : g + j + 1, :] = jnp.sum(e, axis=0, keepdims=True)
            stb[i, 0, 2 * g + j : 2 * g + j + 1, :] = jnp.sum(e * dp, axis=0, keepdims=True)
            expo[i * g + j] = e
            dpro[i * g + j] = dp
        for row in range(3 * g, z.stat_rows):
            stb[i, 0, row : row + 1, :] = jnp.zeros((1, ROWS), jnp.float32)
        for k in range(1, len(near)):
            b_stat(i, k).start()

    def merge(src, i, n, dst):
        parts = [src[i, d] for d in range(n)]
        top = functools.reduce(jnp.maximum, [part[0:g] for part in parts])
        factors = [jnp.exp(part[0:g] - top) for part in parts]
        total = sum(part[g : 2 * g] * f for part, f in zip(parts, factors))
        weighted = sum(part[2 * g : 3 * g] * f for part, f in zip(parts, factors))
        dst[0:g, :] = top
        dst[g : 2 * g, :] = total
        dst[2 * g : 3 * g, :] = weighted
        if z.stat_rows > 3 * g:
            dst[3 * g :, :] = jnp.zeros((z.stat_rows - 3 * g, ROWS), jnp.float32)

    def stat_a(i):
        for k in range(1, len(near)):
            b_stat(i, k).wait_recv()
        merge(stb, i, len(near), sta.at[i, 0])
        for d in range(1, A):
            a_stat(i, d).start()

    def back(i, n, d):
        out = (dk_out, dv_out)[n]
        return copy(
            ret.at[i, n, d], out.at[:, col(u, i)], ret_s.at[i, n, d], ret_r.at[i, n, d],
            dev(a, b, c, lax.rem(u + U - d, U)),
        )

    def back_wait(i, n, d):
        out = (dk_out, dv_out)[n]
        return copy(
            ret.at[i, n, d], out.at[:, col(at_u(d), i)], ret_s.at[i, n, d], ret_r.at[i, n, d],
            dev(a, b, c, lax.rem(u + U - d, U)),
        )

    def c_dq(i):
        return copy(
            dq0.at[i, at_c(1)], dq1.at[i], d1_s.at[i], d1_r.at[i], dev(a, b, at_c(1), u)
        )

    def b_dq(i, d):
        return copy(
            dt1.at[i, at_b(d)], dq2.at[i, d], d2_s.at[i, d], d2_r.at[i, d], dev(a, at_b(d), c, u)
        )

    def a_dq(i, d):
        return copy(
            dt2.at[i, at_a(d)], dq3.at[i, d], d3_s.at[i, d], d3_r.at[i, d], dev(at_a(d), b, c, u)
        )

    def second_pass(i):
        for d in range(1, A):
            a_stat(i, d).wait_recv()
        merge(sta, i, A, fin.at[i])
        for j in range(g):
            factor = jnp.exp(stb[i, 0, j : j + 1, :] - fin[i, j : j + 1, :])
            total = fin[i, g + j : g + j + 1, :]
            factor = factor / total
            delta = fin[i, 2 * g + j : 2 * g + j + 1, :] / total
            probs = expo[i * g + j] * factor
            ds = (probs * (dpro[i * g + j] - delta)).astype(jnp.bfloat16)
            dk = (contract(ds, q_of(i, j), ((1,), (0,))) * SCALE).astype(jnp.bfloat16)
            dv = contract(probs.astype(jnp.bfloat16), do_of(i, j), ((1,), (0,)))
            dv = dv.astype(jnp.bfloat16)
            ret[i, 0, :, :, head(j)] = dk.reshape(U, BLOCK, HEAD_DIM)
            ret[i, 1, :, :, head(j)] = dv.reshape(U, BLOCK, HEAD_DIM)
            dq = contract(ds, kv_of(i, 0, j), ((0,), (0,))) * SCALE
            for s in range(z.seq):
                row = s * z.shard
                at = (row % BLOCK) // PART * (CHANGED * PART) + row // BLOCK * PART + row % PART
                dq0[i, s % CORES, s // CORES % B, s // (CORES * B), :, head(j)] = dq[
                    at : at + z.shard
                ]
        c_dq(i).start()
        for n in range(2):
            for d in range(1, U):
                back(i, n, d).start()
        dk_out[:, col(u, i)] = ret[i, 0, 0]
        dv_out[:, col(u, i)] = ret[i, 1, 0]

    def dq_b(i):
        c_dq(i).wait_recv()
        dt1[i] = (dq0[i, c] + dq1[i]).astype(z.sum_type)
        for d in range(1, B):
            b_dq(i, d).start()

    def dq_a(i):
        total = dt1[i, b].astype(jnp.float32)
        for d in range(1, B):
            b_dq(i, d).wait_recv()
            total = total + dq2[i, d].astype(jnp.float32)
        dt2[i] = total.astype(z.sum_type)
        for d in range(1, A):
            a_dq(i, d).start()

    def dq_end(i):
        total = dt2[i, a].astype(jnp.float32)
        for d in range(1, A):
            a_dq(i, d).wait_recv()
            total = total + dq3[i, d].astype(jnp.float32)
        dq_out[:, pl.ds(pl.multiple_of(i * G, HEAD_DIM), G)] = total.astype(jnp.bfloat16)

    stages = [select, *[functools.partial(hop, h) for h in range(1, A - 1)], spread, relay]
    stages += [first_pass, stat_a, second_pass, dq_b, dq_a, dq_end]

    def step(t, carry):
        for delay, stage in enumerate(stages):
            i = t - delay
            pl.when((i >= 0) & (i < N))(functools.partial(stage, i))
        return carry

    lax.fori_loop(0, N + len(stages) - 1, step, 0)

    def drain(i):
        for n in range(2):
            for d in range(1, U):
                back(i, n, d).wait_send()
                back_wait(i, n, d).wait_recv()
        z_line(i)[1]()
        for n in range(3):
            spread_copy(i, n).wait_send()
        for k in range(1, len(near)):
            b_stat(i, k).wait_send()
        c_dq(i).wait_send()
        for d in range(1, B):
            b_dq(i, d).wait_send()
        for d in range(1, A):
            a_stat(i, d).wait_send()
            a_dq(i, d).wait_send()

    each(drain)
    far, close, others = ybuf.at[:, :, 1:], ybuf.at[:, :, 0, 1:], kv.at[:, :, 1:]
    pltpu.make_async_copy(far, far, y_s.at[0]).wait()
    pltpu.make_async_copy(close, close, y_s.at[1]).wait()
    pltpu.make_async_copy(others, others, kv_s.at[0]).wait()


def local(seq_size, ulys_size, queries, keys, values, dout, changed_blocks, half_mask):
    z = Sizes(seq_size, ulys_size, queries.shape[1])
    N, U, B, A, G, R = z.chunks, z.ulys, z.inner, z.outer, z.cols, z.shard
    bf16, f32 = jnp.bfloat16, jnp.float32
    line = pltpu.VMEM((N, 2, CHANGED, PART, G), bf16)
    near = INNER * CORES
    stat = (z.stat_rows, ROWS)
    dma = pltpu.SemaphoreType.DMA
    vmem = pl.BlockSpec(memory_space=pltpu.VMEM)
    hbm = pl.BlockSpec(memory_space=pl.ANY)
    smem = pl.BlockSpec(memory_space=pltpu.SMEM)
    scratch = [
        pltpu.VMEM((N, 2, U, near, PART, G), bf16),
        pltpu.VMEM((N, 2, U, BLOCK, G), bf16),
        *[line] * 5,
        pltpu.VMEM((N, near, 2, CHANGED, PART, G), bf16),
        pltpu.VMEM((z.heads, z.keys, ROWS), f32),
        pltpu.VMEM((z.heads, z.keys, ROWS), f32),
        pltpu.VMEM((N, near, *stat), f32),
        pltpu.VMEM((N, A, *stat), f32),
        pltpu.VMEM((N, *stat), f32),
        pltpu.VMEM((N, 2, U, BLOCK, G), bf16),
        pltpu.VMEM((N, CORES, B, A, R, G), f32),
        pltpu.VMEM((N, B, A, R, G), f32),
        pltpu.VMEM((N, B, A, R, G), z.sum_type),
        pltpu.VMEM((N, B, A, R, G), z.sum_type),
        pltpu.VMEM((N, A, R, G), z.sum_type),
        pltpu.VMEM((N, A, R, G), z.sum_type),
        dma((2,)),
        dma((N,)),
        dma((1,)),
        dma((N,)),
        *[dma((N, 2))] * 2,
        *[dma((N, 3))] * 2,
        *[dma((N, near))] * 2,
        *[dma((N, A))] * 2,
        *[dma((N, 2, U))] * 2,
        *[dma((N,))] * 2,
        *[dma((N, B))] * 2,
        *[dma((N, A))] * 2,
    ]
    return pl.pallas_call(
        functools.partial(kernel, z),
        out_shape=(
            jax.ShapeDtypeStruct((R, z.width), bf16),
            jax.ShapeDtypeStruct(keys.shape, bf16),
            jax.ShapeDtypeStruct(values.shape, bf16),
        ),
        in_specs=[smem, smem, hbm, hbm, hbm, hbm],
        out_specs=(vmem, vmem, vmem),
        scratch_shapes=scratch,
        compiler_params=pltpu.CompilerParams(
            collective_id=0, has_side_effects=True, vmem_limit_bytes=62 * 1024 * 1024
        ),
    )(changed_blocks, half_mask, queries, dout, keys, values)


class Split:
    def __init__(self, seq, ulys, width):
        self.ulys = ulys
        self.outer = seq // (INNER * CORES)
        self.groups = ulys * CORES
        self.width = width // self.groups
        self.chunks = self.width // HEAD_DIM
        self.seq = seq
        self.shard = ROWS // seq
        self.keys = self.groups * BLOCK

    @staticmethod
    def fits(seq, ulys, width):
        return (
            width % (ulys * CORES * HEAD_DIM) == 0
            and seq == INNER * CORES * CHANGED
            and ROWS // seq % 16 == 0
            and ulys * CORES * BLOCK <= 512
        )


def split_kernel(
    z,
    changed, live, q_in, do_in, k_in, v_in,
    dq_out, dk_out, dv_out,
    ybuf, kv, z0, za, zb, zc, full, expo, dpro, stats, sums, ret, dq0, dq1, dt1, dq2,
    y_s, y_r, kv_s, kv_r, za_s, za_r, zb_s, zb_r, g_s, g_r, x_s, x_r, st_s, st_r,
    o_s, o_r, l_s, d1_s, d1_r, d2_s, d2_r,
):
    seq = lax.axis_index("seq")
    u = lax.axis_index("ulys")
    c = lax.rem(seq, CORES)
    b = lax.rem(seq // CORES, INNER)
    a = seq // (CORES * INNER)
    U, B, A, C, W, N = z.ulys, INNER, z.outer, CORES, z.width, z.chunks
    D = HEAD_DIM

    def dev(da, db, dc, du):
        a_, b_, c_, u_ = at_a(da), at_b(db), at_c(dc), at_u(du)
        return ((a_ * B + b_) * C + c_, u_)

    def at_u(d):
        return lax.rem(u + U + d, U)

    def at_c(d):
        return lax.rem(c + C + d, C)

    def at_b(d):
        return lax.rem(b + B + d, B)

    def at_a(d):
        return lax.rem(a + A + d, A)

    def copy(src, dst, ss, rs, to):
        return pltpu.make_async_remote_copy(
            src_ref=src, dst_ref=dst, send_sem=ss, recv_sem=rs, device_id=to, device_id_type=MESH
        )

    def arrived(ref, sem):
        pltpu.make_async_copy(ref, ref, sem).wait()

    def col(u_, c_, i):
        return pl.ds(pl.multiple_of((u_ * C + c_) * W + i * D, D), D)

    owners = [(du, dc) for du in range(U) for dc in range(C)]
    near = [(db, du, dc) for db in range(B) for du, dc in owners]
    others = [(da, db) for da in range(A) for db in range(B)]
    rows = [(da, dc) for da in range(A) for dc in range(C)]

    mate = a + 1 - 2 * lax.rem(a, 2)
    outside = (a == 0) | (a == A - 1)
    inside = (a != 0) & (a != A - 1)

    def line_dev(a_):
        return ((a_ * B + b) * C + c, u)

    barrier = pltpu.get_barrier_semaphore()
    for db, du, dc in near:
        if db or du or dc:
            peer = dev(0, db, dc, du)
            pl.semaphore_signal(barrier, inc=1, device_id=peer, device_id_type=MESH)
    pl.semaphore_signal(barrier, inc=1, device_id=line_dev(mate), device_id_type=MESH)

    @pl.when(inside)
    def _():
        pl.semaphore_signal(barrier, inc=1, device_id=line_dev(A - 1 - a), device_id_type=MESH)
        pl.semaphore_wait(barrier, len(near) + 1)

    @pl.when(outside)
    def _():
        pl.semaphore_wait(barrier, len(near))

    def send_y(i):
        for n, ref in enumerate((q_in, do_in)):
            for k, (db, du, dc) in enumerate(near):
                part = pl.ds(pl.multiple_of(at_b(db) * HALF, HALF), HALF)
                src, dst = ref.at[part, col(at_u(du), at_c(dc), i)], ybuf.at[i, n, k]
                if k:
                    copy(src, dst, y_s.at[0], y_r.at[i, n], dev(0, db, dc, du)).start()
                else:
                    pltpu.make_async_copy(src, dst, y_r.at[i, n]).start()

    def send_kv(i):
        for k, (du, dc) in enumerate(owners):
            for n, ref in enumerate((k_in, v_in)):
                src = ref.at[:, col(at_u(du), at_c(dc), i)]
                if k:
                    copy(src, kv.at[i, n, k], kv_s.at[0], kv_r.at[i], dev(0, 0, dc, du)).start()
                else:
                    pltpu.make_async_copy(src, kv.at[i, n, k], kv_r.at[i]).start()

    def each(body):
        def step(i, carry):
            body(i)
            return carry

        lax.fori_loop(0, N, step, 0)

    each(send_y)

    def select(i):
        send_kv(i)
        for n in range(PIECES):
            arrived(ybuf.at[i, n], y_r.at[i, n])
            totals = [None] * CHANGED
            for k, (db, du, dc) in enumerate(near):
                block = ((a * B + at_b(-db)) * C + at_c(-dc)) * U + at_u(-du)
                piece = ybuf[i, n, k]
                for slot in range(CHANGED):
                    weight = jnp.where(changed[slot] == block, 1.0, 0.0)
                    if n:
                        alive = jnp.where(b == 0, live[0, slot], live[1, slot])
                        weight = weight * alive.astype(jnp.float32)
                    weight = jnp.full((HALF, D), weight, jnp.float32).astype(jnp.bfloat16)
                    term = piece * weight
                    totals[slot] = term if totals[slot] is None else totals[slot] + term
            for slot in range(CHANGED):
                z0[i, n, slot] = totals[slot]

            @pl.when(outside)
            def _():
                pair_copy(i, n).start()

    def pair_copy(i, p):
        return copy(
            z0.at[i, p], za.at[i, p], za_s.at[i, p], za_r.at[i, p], line_dev(mate)
        )

    def middle_copy(i, p):
        return copy(
            zb.at[i, p], zc.at[i, p], zb_s.at[i, p], zb_r.at[i, p],
            line_dev(A - 1 - a),
        )

    def back_copy(i, p):
        here = full.at[i, p, :, b]
        return copy(here, here, g_s.at[i, p], g_r.at[i, p], line_dev(mate))

    def x_copy(i, p, came=False):
        here = full.at[i, p, :, b]
        there = full.at[i, p, :, at_b(1)] if came else here
        return copy(here, there, x_s.at[i, p], x_r.at[i, p], dev(0, 1, 0, 0))

    def middle(i):
        @pl.when(inside)
        def _():
            for p in range(PIECES):
                pair_copy(i, p).wait_recv()
                zb[i, p] = z0[i, p] + za[i, p]
                middle_copy(i, p).start()

    def give_back(i):
        @pl.when(inside)
        def _():
            for p in range(PIECES):
                middle_copy(i, p).wait_recv()
                full[i, p, :, b] = zb[i, p] + zc[i, p]
                back_copy(i, p).start()
                x_copy(i, p).start()

    def across(i):
        @pl.when(outside)
        def _():
            for p in range(PIECES):
                back_copy(i, p).wait_recv()
                x_copy(i, p).start()

    def q_of(i, n):
        return full[i, n].reshape(ROWS, D)

    def kv_of(i, n):
        return kv[i, n].reshape(z.keys, D)

    def first_pass(i):
        arrived(kv.at[i], kv_r.at[i])
        x_copy(i, 0, True).wait_recv()
        scores = contract(kv_of(i, 0), q_of(i, 0), ((1,), (1,))) * SCALE
        top = jnp.max(scores, axis=0, keepdims=True)
        e = jnp.exp(scores - top)
        expo[i] = e
        x_copy(i, 1, True).wait_recv()
        dp = contract(kv_of(i, 1), q_of(i, 1), ((1,), (1,)))
        total = jnp.sum(e, axis=0, keepdims=True)
        mean = jnp.sum(e * dp, axis=0, keepdims=True) / total
        sums[i] = jnp.broadcast_to(total, sums.shape[1:])
        found = (top + jnp.log(total), mean)
        dpro[i] = dp
        for r, row in enumerate(found):
            for j in range(CHANGED):
                at = r * CHANGED + j
                stats[i, 0, at : at + 1, :] = row[:, j * BLOCK : (j + 1) * BLOCK]
        for k, (da, db) in enumerate(others):
            if k:
                copy(
                    stats.at[i, 0], stats.at[i, k], st_s.at[0], st_r.at[i], dev(da, db, 0, 0)
                ).start()

    def wide(x):
        return jnp.concatenate([x[j : j + 1] for j in range(CHANGED)], axis=1)

    def second_pass(i):
        arrived(stats.at[i, 1:], st_r.at[i])
        parts = [stats[i, k] for k in range(len(others))]
        top = functools.reduce(jnp.maximum, [part[0:CHANGED] for part in parts])
        shares = [jnp.exp(part[0:CHANGED] - top) for part in parts]
        whole = sum(shares)
        means = sum(part[CHANGED:] * share for part, share in zip(parts, shares))
        factor = wide(shares[0] / whole) / sums[i, 0:1]
        delta = wide(means / whole)
        probs = expo[i] * factor
        ds = (probs * (dpro[i] - delta)).astype(jnp.bfloat16)
        dq = contract(ds, kv_of(i, 0), ((0,), (0,))) * SCALE
        dq0[i] = dq.astype(jnp.bfloat16).reshape(A, B, z.shard * C, D)
        dq_x(i).start()
        dk = (contract(ds, q_of(i, 0), ((1,), (0,))) * SCALE).astype(jnp.bfloat16)
        ret[i, 0] = dk.reshape(len(owners), BLOCK, D)
        send_out(i, 0)
        dv = contract(probs.astype(jnp.bfloat16), q_of(i, 1), ((1,), (0,))).astype(jnp.bfloat16)
        ret[i, 1] = dv.reshape(len(owners), BLOCK, D)
        send_out(i, 1)

    def send_out(i, n):
        out = (dk_out, dv_out)[n].at[:, col(u, c, i)]
        for k, (du, dc) in enumerate(owners):
            if k:
                copy(ret.at[i, n, k], out, o_s.at[0], o_r.at[0], dev(0, 0, -dc, -du)).start()
            else:
                pltpu.make_async_copy(ret.at[i, n, k], out, l_s.at[0]).start()

    def dq_x(i):
        return copy(
            dq0.at[i, :, at_b(1)], dq1.at[i], d1_s.at[i], d1_r.at[i], dev(0, 1, 0, 0)
        )

    def dq_mid(i):
        dq_x(i).wait_recv()
        mine = dq0[i, :, b].astype(jnp.float32) + dq1[i].astype(jnp.float32)
        dt1[i] = mine.astype(jnp.bfloat16).reshape(A, C, z.shard, D)
        for k, (da, dc) in enumerate(rows):
            if k:
                copy(
                    dt1.at[i, at_a(da), at_c(dc)], dq2.at[i, k - 1],
                    d2_s.at[0], d2_r.at[i], dev(da, 0, dc, 0),
                ).start()

    def dq_end(i):
        arrived(dq2.at[i], d2_r.at[i])
        for dc in range(C):
            total = None
            for k, (da, e) in enumerate(rows):
                if e == dc:
                    term = (dq2[i, k - 1] if k else dt1[i, a, c]).astype(jnp.float32)
                    total = term if total is None else total + term
            at = pl.ds(pl.multiple_of(at_c(-dc) * W + i * D, D), D)
            dq_out[:, at] = total.astype(jnp.bfloat16)

    stages = [select, middle, give_back, across, first_pass, second_pass, dq_mid, dq_end]

    def step(t, carry):
        for stage, delay in reversed(list(zip(stages, DELAYS))):
            i = t - delay
            pl.when((i >= 0) & (i < N))(functools.partial(stage, i))
        return carry

    lax.fori_loop(0, N + DELAYS[-1], step, 0)

    def drain(i):
        for p in range(PIECES):
            @pl.when(outside)
            def _():
                pair_copy(i, p).wait_send()

            @pl.when(inside)
            def _():
                middle_copy(i, p).wait_send()
                back_copy(i, p).wait_send()

            x_copy(i, p).wait_send()

        dq_x(i).wait_send()
        for k in range(1, len(others)):
            arrived(stats.at[i, k], st_s.at[0])

    each(drain)
    arrived(ybuf.at[:, :, 1:], y_s.at[0])
    arrived(kv.at[:, :, 1:], kv_s.at[0])
    arrived(dq2, d2_s.at[0])
    arrived(ret.at[:, :, 1:], o_s.at[0])
    arrived(ret.at[:, :, 1:], o_r.at[0])
    arrived(ret.at[:, :, 0], l_s.at[0])


def hand_over(dq_in, dk_in, dv_in, dq_out, dk_out, dv_out, sems):
    pairs = ((dq_in, dq_out), (dk_in, dk_out), (dv_in, dv_out))
    copies = [pltpu.make_async_copy(src, dst, sems.at[n]) for n, (src, dst) in enumerate(pairs)]
    for one in copies:
        one.start()
    for one in copies:
        one.wait()


def split_local(seq_size, ulys_size, queries, keys, values, dout, changed_blocks, half_mask):
    z = Split(seq_size, ulys_size, queries.shape[1])
    N, U, A, C, D, R = z.chunks, z.ulys, z.outer, CORES, HEAD_DIM, z.shard
    bf16, f32 = jnp.bfloat16, jnp.float32
    dma = pltpu.SemaphoreType.DMA
    vmem = pl.BlockSpec(memory_space=pltpu.VMEM)
    hbm = pl.BlockSpec(memory_space=pl.ANY)
    smem = pl.BlockSpec(memory_space=pltpu.SMEM)
    scratch = [
        pltpu.VMEM((N, 2, INNER * z.groups, HALF, D), bf16),
        pltpu.VMEM((N, 2, z.groups, BLOCK, D), bf16),
        *[pltpu.VMEM((N, 2, CHANGED, HALF, D), bf16)] * 4,
        pltpu.VMEM((N, 2, CHANGED, INNER, HALF, D), bf16),
        pltpu.VMEM((N, z.keys, ROWS), f32),
        pltpu.VMEM((N, z.keys, ROWS), f32),
        pltpu.VMEM((N, A * INNER, 2 * CHANGED, BLOCK), f32),
        pltpu.VMEM((N, 8, ROWS), f32),
        pltpu.VMEM((N, 2, z.groups, BLOCK, D), bf16),
        pltpu.VMEM((N, A, INNER, C * R, D), bf16),
        pltpu.VMEM((N, A, C * R, D), bf16),
        pltpu.VMEM((N, A, C, R, D), bf16),
        pltpu.VMEM((N, A * C - 1, R, D), bf16),
        dma((1,)), dma((N, PIECES)),
        dma((1,)), dma((N,)),
        *[dma((N, PIECES))] * 8,
        dma((1,)), dma((N,)),
        dma((1,)), dma((1,)), dma((1,)),
        dma((N,)), dma((N,)),
        dma((1,)), dma((N,)),
    ]
    outs = (
        jax.ShapeDtypeStruct((R, z.width * C), bf16),
        jax.ShapeDtypeStruct(keys.shape, bf16),
        jax.ShapeDtypeStruct(values.shape, bf16),
    )
    found = pl.pallas_call(
        functools.partial(split_kernel, z),
        out_shape=tuple(pltpu.VMEM(out.shape, bf16) for out in outs),
        in_specs=[smem, smem, hbm, hbm, hbm, hbm],
        out_specs=(vmem, vmem, vmem),
        scratch_shapes=scratch,
        compiler_params=pltpu.CompilerParams(
            collective_id=1, has_side_effects=True, vmem_limit_bytes=56 * 1024 * 1024
        ),
    )(changed_blocks, half_mask.T, queries, dout, keys, values)
    return pl.pallas_call(
        hand_over,
        out_shape=outs,
        in_specs=[vmem] * 3,
        out_specs=[hbm] * 3,
        scratch_shapes=[dma((len(outs),))],
    )(*[pltpu.with_memory_space_constraint(x, pltpu.VMEM) for x in found])


def solution(mesh):
    rows = P(("seq", "ulys"), None)
    seq, ulys = mesh.shape["seq"], mesh.shape["ulys"]

    def run(queries, keys, values, dout, changed_blocks, half_mask):
        body = split_local if Split.fits(seq, ulys, queries.shape[1]) else local
        return body(seq, ulys, queries, keys, values, dout, changed_blocks, half_mask)

    return jax.shard_map(
        run,
        mesh=mesh,
        in_specs=(rows, rows, rows, rows, P(), P()),
        out_specs=(P("seq", "ulys"), rows, rows),
        check_vma=False,
    )
```

```python
import functools

import jax
import jax.numpy as jnp
from jax import lax
from jax.experimental import pallas as pl
from jax.experimental.pallas import tpu as pltpu
from jax.sharding import PartitionSpec as P

HEAD_DIM = 128
BLOCK = 128
PART = 32
CHANGED = 4
ROWS = CHANGED * BLOCK
CORES = 2
INNER = 2
SCALE = 1.0 / HEAD_DIM**0.5
HALF = BLOCK // 2
PIECES = 2
SPAN = CHANGED // PIECES
DELAYS = (0, 2, 4, 6, 9, 12, 15, 18)
MESH = pl.DeviceIdType.MESH


class Sizes:
    def __init__(self, seq, ulys, width):
        self.ulys = ulys
        self.inner = INNER
        self.outer = seq // (INNER * CORES)
        self.width = width // ulys
        self.heads = self.width // HEAD_DIM
        self.group = 2 if self.heads % 2 == 0 else 1
        self.cols = self.group * HEAD_DIM
        self.chunks = self.heads // self.group
        self.shard = ROWS // seq
        self.seq = seq
        self.keys = ulys * BLOCK
        self.stat_rows = -(-3 * self.group // 8) * 8
        self.sum_type = jnp.bfloat16 if self.shard >= 16 else jnp.float32


def contract(a, b, dims):
    return lax.dot_general(a, b, (dims, ((), ())), preferred_element_type=jnp.float32)


def kernel(
    z,
    changed, live, q_in, do_in, k_in, v_in,
    dq_out, dk_out, dv_out,
    ybuf, kv, z0, zr, zl, zro, zlo, full,
    expo, dpro, stb, sta, fin, ret,
    dq0, dq1, dt1, dq2, dt2, dq3,
    y_s, y_r, kv_s, kv_r, zs, zrs, f_s, f_r,
    sb_s, sb_r, sa_s, sa_r, ret_s, ret_r,
    d1_s, d1_r, d2_s, d2_r, d3_s, d3_r,
):
    seq = lax.axis_index("seq")
    u = lax.axis_index("ulys")
    c = lax.rem(seq, CORES)
    b = lax.rem(seq // CORES, z.inner)
    a = seq // (CORES * z.inner)
    U, B, A, G, W, N, g = z.ulys, z.inner, z.outer, z.cols, z.width, z.chunks, z.group

    def dev(a_, b_, c_, u_):
        return ((a_ * B + b_) * CORES + c_, u_)

    def copy(src, dst, ss, rs, to):
        return pltpu.make_async_remote_copy(
            src_ref=src, dst_ref=dst, send_sem=ss, recv_sem=rs, device_id=to, device_id_type=MESH
        )

    def at_u(d):
        return lax.rem(u + d, U)

    def at_c(d):
        return lax.rem(c + d, CORES)

    def at_b(d):
        return lax.rem(b + d, B)

    def at_a(d):
        return lax.rem(a + d, A)

    def col(block, i):
        return pl.ds(pl.multiple_of(block * W + i * G, HEAD_DIM), G)

    part = b * CORES + c
    near = [(db, dc) for db in range(B) for dc in range(CORES)]
    pairs = [(du, k) for k in range(len(near)) for du in range(U)]

    def near_dev(k, u_):
        return dev(a, at_b(near[k][0]), at_c(near[k][1]), u_)

    def part_of(k):
        return at_b(near[k][0]) * CORES + at_c(near[k][1])

    peers = [near_dev(k, at_u(du)) for du, k in pairs if du or k]
    peers += [dev(at_a(d), b, c, u) for d in range(1, A)]
    barrier = pltpu.get_barrier_semaphore()
    for peer in peers:
        pl.semaphore_signal(barrier, inc=1, device_id=peer, device_id_type=MESH)
    pl.semaphore_wait(barrier, len(peers))

    def y_rows(k):
        return pl.ds(pl.multiple_of(part_of(k) * PART, PART), PART)

    def y_copy(i, n, du, k):
        ref = (q_in, do_in)[n]
        return copy(
            ref.at[y_rows(k), col(at_u(du), i)], ybuf.at[i, n, du, k],
            y_s.at[0 if du else 1], y_r.at[i], near_dev(k, at_u(du)),
        )

    def y_own(i, n):
        ref = (q_in, do_in)[n]
        return pltpu.make_async_copy(
            ref.at[y_rows(0), col(u, i)], ybuf.at[i, n, 0, 0], y_r.at[i]
        )

    def kv_own(i, n):
        ref = (k_in, v_in)[n]
        return pltpu.make_async_copy(ref.at[:, col(u, i)], kv.at[i, n, 0], kv_r.at[i])

    def kv_copy(i, n, du):
        ref = (k_in, v_in)[n]
        return copy(
            ref.at[:, col(at_u(du), i)], kv.at[i, n, du],
            kv_s.at[0], kv_r.at[i], dev(a, b, c, at_u(du)),
        )

    def each(body):
        def step(i, carry):
            body(i)
            return carry

        lax.fori_loop(0, N, step, 0)

    def send_y(i):
        for n in range(2):
            y_own(i, n).start()
            for du, k in pairs:
                if du or k:
                    y_copy(i, n, du, k).start()

    def send_kv(i):
        for n in range(2):
            kv_own(i, n).start()
            for du in range(1, U):
                kv_copy(i, n, du).start()

    each(send_y)
    each(send_kv)

    def line(i, p, n, right, left, src, rin, lin, rout, lout, ss, rs):
        def r_copy():
            return copy(rout.at[i], rin.at[i], ss.at[i, 0], rs.at[i, 0], right)

        def l_copy():
            return copy(lout.at[i], lin.at[i], ss.at[i, 1], rs.at[i, 1], left)

        def do_right():
            @pl.when(p == 0)
            def _():
                rin[i] = jnp.zeros(rin.shape[1:], rin.dtype)

            @pl.when(p > 0)
            def _():
                r_copy().wait_recv()

            @pl.when(p < n - 1)
            def _():
                rout[i] = src[i] + rin[i]
                r_copy().start()

        def do_left():
            @pl.when(p == n - 1)
            def _():
                lin[i] = jnp.zeros(lin.shape[1:], lin.dtype)

            @pl.when(p < n - 1)
            def _():
                l_copy().wait_recv()

            @pl.when(p > 0)
            def _():
                lout[i] = src[i] + lin[i]
                l_copy().start()

        def hop(h):
            pl.when(p == h)(do_right)
            pl.when(p == n - 1 - h)(do_left)

        def finish():
            @pl.when(p < n - 1)
            def _():
                r_copy().wait_send()

            @pl.when(p > 0)
            def _():
                l_copy().wait_send()

        return hop, finish

    def z_line(i):
        return line(
            i, a, A, dev(lax.rem(a + 1, A), b, c, u), dev(lax.rem(a + A - 1, A), b, c, u),
            z0, zr, zl, zro, zlo, zs, zrs,
        )

    def select(i):
        pltpu.make_async_copy(ybuf.at[i], ybuf.at[i], y_r.at[i]).wait()
        for n in range(2):
            totals = [None] * CHANGED
            for du, k in pairs:
                from_b = lax.rem(b + B - near[k][0], B)
                from_c = lax.rem(c + CORES - near[k][1], CORES)
                from_u = lax.rem(u + U - du, U)
                block = ((a * B + from_b) * CORES + from_c) * U + from_u
                piece = ybuf[i, n, du, k]
                for slot in range(CHANGED):
                    weight = jnp.where(changed[slot] == block, 1.0, 0.0)
                    if n == 1:
                        weight = weight * jnp.where(
                            b == 0, live[slot, 0], live[slot, 1]
                        ).astype(jnp.float32)
                    weight = jnp.full((PART, G), weight, jnp.float32).astype(jnp.bfloat16)
                    term = piece * weight
                    totals[slot] = term if totals[slot] is None else totals[slot] + term
            for slot in range(CHANGED):
                z0[i, n, slot] = totals[slot]
        z_line(i)[0](0)

    def hop(h, i):
        z_line(i)[0](h)

    def spread_copy(i, n, came=False):
        at = (part, part, at_b(1) * CORES + c)[n]
        to = (dev(a, b, at_c(1), u), dev(a, at_b(1), c, u), dev(a, b, at_c(1), u))[n]
        if came:
            at_in = (
                b * CORES + at_c(1), at_b(1) * CORES + c, at_b(1) * CORES + at_c(1)
            )[n]
            return copy(full.at[i, at], full.at[i, at_in], f_s.at[i, n], f_r.at[i, n], to)
        return copy(full.at[i, at], full.at[i, at], f_s.at[i, n], f_r.at[i, n], to)

    def spread(i):
        z_line(i)[0](A - 1)
        full[i, part] = z0[i] + zr[i] + zl[i]
        spread_copy(i, 1).start()
        spread_copy(i, 0).start()

    def relay(i):
        spread_copy(i, 1, True).wait_recv()
        spread_copy(i, 2).start()

    def head(j):
        return slice(j * HEAD_DIM, (j + 1) * HEAD_DIM)

    def q_of(i, j):
        return full[i, :, 0, :, :, head(j)].reshape(ROWS, HEAD_DIM)

    def do_of(i, j):
        return full[i, :, 1, :, :, head(j)].reshape(ROWS, HEAD_DIM)

    def kv_of(i, n, j):
        return kv[i, n, :, :, head(j)].reshape(z.keys, HEAD_DIM)

    def b_stat(i, k):
        return copy(
            stb.at[i, 0], stb.at[i, k], sb_s.at[i, k], sb_r.at[i, k], near_dev(k, u)
        )

    def a_stat(i, d):
        return copy(
            sta.at[i, 0], sta.at[i, d], sa_s.at[i, d], sa_r.at[i, d], dev(at_a(d), b, c, u)
        )

    def first_pass(i):
        spread_copy(i, 0, True).wait_recv()
        spread_copy(i, 2, True).wait_recv()
        pltpu.make_async_copy(kv.at[i], kv.at[i], kv_r.at[i]).wait()
        for j in range(g):
            scores = contract(kv_of(i, 0, j), q_of(i, j), ((1,), (1,))) * SCALE
            top = jnp.max(scores, axis=0, keepdims=True)
            e = jnp.exp(scores - top)
            dp = contract(kv_of(i, 1, j), do_of(i, j), ((1,), (1,)))
            stb[i, 0, j : j + 1, :] = top
            stb[i, 0, g + j : g + j + 1, :] = jnp.sum(e, axis=0, keepdims=True)
            stb[i, 0, 2 * g + j : 2 * g + j + 1, :] = jnp.sum(e * dp, axis=0, keepdims=True)
            expo[i * g + j] = e
            dpro[i * g + j] = dp
        for row in range(3 * g, z.stat_rows):
            stb[i, 0, row : row + 1, :] = jnp.zeros((1, ROWS), jnp.float32)
        for k in range(1, len(near)):
            b_stat(i, k).start()

    def merge(src, i, n, dst):
        parts = [src[i, d] for d in range(n)]
        top = functools.reduce(jnp.maximum, [part[0:g] for part in parts])
        factors = [jnp.exp(part[0:g] - top) for part in parts]
        total = sum(part[g : 2 * g] * f for part, f in zip(parts, factors))
        weighted = sum(part[2 * g : 3 * g] * f for part, f in zip(parts, factors))
        dst[0:g, :] = top
        dst[g : 2 * g, :] = total
        dst[2 * g : 3 * g, :] = weighted
        if z.stat_rows > 3 * g:
            dst[3 * g :, :] = jnp.zeros((z.stat_rows - 3 * g, ROWS), jnp.float32)

    def stat_a(i):
        for k in range(1, len(near)):
            b_stat(i, k).wait_recv()
        merge(stb, i, len(near), sta.at[i, 0])
        for d in range(1, A):
            a_stat(i, d).start()

    def back(i, n, d):
        out = (dk_out, dv_out)[n]
        return copy(
            ret.at[i, n, d], out.at[:, col(u, i)], ret_s.at[i, n, d], ret_r.at[i, n, d],
            dev(a, b, c, lax.rem(u + U - d, U)),
        )

    def back_wait(i, n, d):
        out = (dk_out, dv_out)[n]
        return copy(
            ret.at[i, n, d], out.at[:, col(at_u(d), i)], ret_s.at[i, n, d], ret_r.at[i, n, d],
            dev(a, b, c, lax.rem(u + U - d, U)),
        )

    def c_dq(i):
        return copy(
            dq0.at[i, at_c(1)], dq1.at[i], d1_s.at[i], d1_r.at[i], dev(a, b, at_c(1), u)
        )

    def b_dq(i, d):
        return copy(
            dt1.at[i, at_b(d)], dq2.at[i, d], d2_s.at[i, d], d2_r.at[i, d], dev(a, at_b(d), c, u)
        )

    def a_dq(i, d):
        return copy(
            dt2.at[i, at_a(d)], dq3.at[i, d], d3_s.at[i, d], d3_r.at[i, d], dev(at_a(d), b, c, u)
        )

    def second_pass(i):
        for d in range(1, A):
            a_stat(i, d).wait_recv()
        merge(sta, i, A, fin.at[i])
        for j in range(g):
            factor = jnp.exp(stb[i, 0, j : j + 1, :] - fin[i, j : j + 1, :])
            total = fin[i, g + j : g + j + 1, :]
            factor = factor / total
            delta = fin[i, 2 * g + j : 2 * g + j + 1, :] / total
            probs = expo[i * g + j] * factor
            ds = (probs * (dpro[i * g + j] - delta)).astype(jnp.bfloat16)
            dk = (contract(ds, q_of(i, j), ((1,), (0,))) * SCALE).astype(jnp.bfloat16)
            dv = contract(probs.astype(jnp.bfloat16), do_of(i, j), ((1,), (0,)))
            dv = dv.astype(jnp.bfloat16)
            ret[i, 0, :, :, head(j)] = dk.reshape(U, BLOCK, HEAD_DIM)
            ret[i, 1, :, :, head(j)] = dv.reshape(U, BLOCK, HEAD_DIM)
            dq = contract(ds, kv_of(i, 0, j), ((0,), (0,))) * SCALE
            for s in range(z.seq):
                row = s * z.shard
                at = (row % BLOCK) // PART * (CHANGED * PART) + row // BLOCK * PART + row % PART
                dq0[i, s % CORES, s // CORES % B, s // (CORES * B), :, head(j)] = dq[
                    at : at + z.shard
                ]
        c_dq(i).start()
        for n in range(2):
            for d in range(1, U):
                back(i, n, d).start()
        dk_out[:, col(u, i)] = ret[i, 0, 0]
        dv_out[:, col(u, i)] = ret[i, 1, 0]

    def dq_b(i):
        c_dq(i).wait_recv()
        dt1[i] = (dq0[i, c] + dq1[i]).astype(z.sum_type)
        for d in range(1, B):
            b_dq(i, d).start()

    def dq_a(i):
        total = dt1[i, b].astype(jnp.float32)
        for d in range(1, B):
            b_dq(i, d).wait_recv()
            total = total + dq2[i, d].astype(jnp.float32)
        dt2[i] = total.astype(z.sum_type)
        for d in range(1, A):
            a_dq(i, d).start()

    def dq_end(i):
        total = dt2[i, a].astype(jnp.float32)
        for d in range(1, A):
            a_dq(i, d).wait_recv()
            total = total + dq3[i, d].astype(jnp.float32)
        dq_out[:, pl.ds(pl.multiple_of(i * G, HEAD_DIM), G)] = total.astype(jnp.bfloat16)

    stages = [select, *[functools.partial(hop, h) for h in range(1, A - 1)], spread, relay]
    stages += [first_pass, stat_a, second_pass, dq_b, dq_a, dq_end]

    def step(t, carry):
        for delay, stage in enumerate(stages):
            i = t - delay
            pl.when((i >= 0) & (i < N))(functools.partial(stage, i))
        return carry

    lax.fori_loop(0, N + len(stages) - 1, step, 0)

    def drain(i):
        for n in range(2):
            for d in range(1, U):
                back(i, n, d).wait_send()
                back_wait(i, n, d).wait_recv()
        z_line(i)[1]()
        for n in range(3):
            spread_copy(i, n).wait_send()
        for k in range(1, len(near)):
            b_stat(i, k).wait_send()
        c_dq(i).wait_send()
        for d in range(1, B):
            b_dq(i, d).wait_send()
        for d in range(1, A):
            a_stat(i, d).wait_send()
            a_dq(i, d).wait_send()

    each(drain)
    far, close, others = ybuf.at[:, :, 1:], ybuf.at[:, :, 0, 1:], kv.at[:, :, 1:]
    pltpu.make_async_copy(far, far, y_s.at[0]).wait()
    pltpu.make_async_copy(close, close, y_s.at[1]).wait()
    pltpu.make_async_copy(others, others, kv_s.at[0]).wait()


def local(seq_size, ulys_size, queries, keys, values, dout, changed_blocks, half_mask):
    z = Sizes(seq_size, ulys_size, queries.shape[1])
    N, U, B, A, G, R = z.chunks, z.ulys, z.inner, z.outer, z.cols, z.shard
    bf16, f32 = jnp.bfloat16, jnp.float32
    line = pltpu.VMEM((N, 2, CHANGED, PART, G), bf16)
    near = INNER * CORES
    stat = (z.stat_rows, ROWS)
    dma = pltpu.SemaphoreType.DMA
    vmem = pl.BlockSpec(memory_space=pltpu.VMEM)
    hbm = pl.BlockSpec(memory_space=pl.ANY)
    smem = pl.BlockSpec(memory_space=pltpu.SMEM)
    scratch = [
        pltpu.VMEM((N, 2, U, near, PART, G), bf16),
        pltpu.VMEM((N, 2, U, BLOCK, G), bf16),
        *[line] * 5,
        pltpu.VMEM((N, near, 2, CHANGED, PART, G), bf16),
        pltpu.VMEM((z.heads, z.keys, ROWS), f32),
        pltpu.VMEM((z.heads, z.keys, ROWS), f32),
        pltpu.VMEM((N, near, *stat), f32),
        pltpu.VMEM((N, A, *stat), f32),
        pltpu.VMEM((N, *stat), f32),
        pltpu.VMEM((N, 2, U, BLOCK, G), bf16),
        pltpu.VMEM((N, CORES, B, A, R, G), f32),
        pltpu.VMEM((N, B, A, R, G), f32),
        pltpu.VMEM((N, B, A, R, G), z.sum_type),
        pltpu.VMEM((N, B, A, R, G), z.sum_type),
        pltpu.VMEM((N, A, R, G), z.sum_type),
        pltpu.VMEM((N, A, R, G), z.sum_type),
        dma((2,)),
        dma((N,)),
        dma((1,)),
        dma((N,)),
        *[dma((N, 2))] * 2,
        *[dma((N, 3))] * 2,
        *[dma((N, near))] * 2,
        *[dma((N, A))] * 2,
        *[dma((N, 2, U))] * 2,
        *[dma((N,))] * 2,
        *[dma((N, B))] * 2,
        *[dma((N, A))] * 2,
    ]
    return pl.pallas_call(
        functools.partial(kernel, z),
        out_shape=(
            jax.ShapeDtypeStruct((R, z.width), bf16),
            jax.ShapeDtypeStruct(keys.shape, bf16),
            jax.ShapeDtypeStruct(values.shape, bf16),
        ),
        in_specs=[smem, smem, hbm, hbm, hbm, hbm],
        out_specs=(vmem, vmem, vmem),
        scratch_shapes=scratch,
        compiler_params=pltpu.CompilerParams(
            collective_id=0, has_side_effects=True, vmem_limit_bytes=62 * 1024 * 1024
        ),
    )(changed_blocks, half_mask, queries, dout, keys, values)


class Split:
    def __init__(self, seq, ulys, width):
        self.ulys = ulys
        self.outer = seq // (INNER * CORES)
        self.groups = ulys * CORES
        self.width = width // self.groups
        self.chunks = self.width // HEAD_DIM
        self.seq = seq
        self.shard = ROWS // seq
        self.keys = self.groups * BLOCK

    @staticmethod
    def fits(seq, ulys, width):
        return (
            width % (ulys * CORES * HEAD_DIM) == 0
            and seq == INNER * CORES * CHANGED
            and ROWS // seq % 16 == 0
            and ulys * CORES * BLOCK <= 512
        )


def split_kernel(
    z,
    changed, live, q_in, do_in, k_in, v_in,
    dq_out, dk_out, dv_out,
    ybuf, kv, z0, za, zb, zc, full, expo, dpro, stats, sums, ret, dq0, dq1, dt1, dq2,
    y_s, y_r, kv_s, kv_r, za_s, za_r, zb_s, zb_r, g_s, g_r, x_s, x_r, st_s, st_r,
    o_s, o_r, l_s, d1_s, d1_r, d2_s, d2_r,
):
    seq = lax.axis_index("seq")
    u = lax.axis_index("ulys")
    c = lax.rem(seq, CORES)
    b = lax.rem(seq // CORES, INNER)
    a = seq // (CORES * INNER)
    U, B, A, C, W, N = z.ulys, INNER, z.outer, CORES, z.width, z.chunks
    D = HEAD_DIM

    def dev(da, db, dc, du):
        a_, b_, c_, u_ = at_a(da), at_b(db), at_c(dc), at_u(du)
        return ((a_ * B + b_) * C + c_, u_)

    def at_u(d):
        return lax.rem(u + U + d, U)

    def at_c(d):
        return lax.rem(c + C + d, C)

    def at_b(d):
        return lax.rem(b + B + d, B)

    def at_a(d):
        return lax.rem(a + A + d, A)

    def copy(src, dst, ss, rs, to):
        return pltpu.make_async_remote_copy(
            src_ref=src, dst_ref=dst, send_sem=ss, recv_sem=rs, device_id=to, device_id_type=MESH
        )

    def arrived(ref, sem):
        pltpu.make_async_copy(ref, ref, sem).wait()

    def col(u_, c_, i):
        return pl.ds(pl.multiple_of((u_ * C + c_) * W + i * D, D), D)

    owners = [(du, dc) for du in range(U) for dc in range(C)]
    near = [(db, du, dc) for db in range(B) for du, dc in owners]
    others = [(da, db) for da in range(A) for db in range(B)]
    rows = [(da, dc) for da in range(A) for dc in range(C)]

    mate = a + 1 - 2 * lax.rem(a, 2)
    outside = (a == 0) | (a == A - 1)
    inside = (a != 0) & (a != A - 1)

    def line_dev(a_):
        return ((a_ * B + b) * C + c, u)

    barrier = pltpu.get_barrier_semaphore()
    for db, du, dc in near:
        if db or du or dc:
            peer = dev(0, db, dc, du)
            pl.semaphore_signal(barrier, inc=1, device_id=peer, device_id_type=MESH)
    pl.semaphore_signal(barrier, inc=1, device_id=line_dev(mate), device_id_type=MESH)

    @pl.when(inside)
    def _():
        pl.semaphore_signal(barrier, inc=1, device_id=line_dev(A - 1 - a), device_id_type=MESH)
        pl.semaphore_wait(barrier, len(near) + 1)

    @pl.when(outside)
    def _():
        pl.semaphore_wait(barrier, len(near))

    def send_y(i):
        for k, (db, du, dc) in enumerate(near):
            part = pl.ds(pl.multiple_of(at_b(db) * HALF, HALF), HALF)
            for n, ref in enumerate((q_in, do_in)):
                src = ref.at[part, col(at_u(du), at_c(dc), i)]
                if k:
                    copy(src, ybuf.at[i, n, k], y_s.at[0], y_r.at[i], dev(0, db, dc, du)).start()
                else:
                    pltpu.make_async_copy(src, ybuf.at[i, n, k], y_r.at[i]).start()

    def send_kv(i):
        for k, (du, dc) in enumerate(owners):
            for n, ref in enumerate((k_in, v_in)):
                src = ref.at[:, col(at_u(du), at_c(dc), i)]
                if k:
                    copy(src, kv.at[i, n, k], kv_s.at[0], kv_r.at[i], dev(0, 0, dc, du)).start()
                else:
                    pltpu.make_async_copy(src, kv.at[i, n, k], kv_r.at[i]).start()

    def each(body):
        def step(i, carry):
            body(i)
            return carry

        lax.fori_loop(0, N, step, 0)

    each(send_y)

    def select(i):
        send_kv(i)
        arrived(ybuf.at[i], y_r.at[i])
        totals = [[None] * CHANGED for _ in range(2)]
        for k, (db, du, dc) in enumerate(near):
            block = ((a * B + at_b(-db)) * C + at_c(-dc)) * U + at_u(-du)
            pieces = [ybuf[i, n, k] for n in range(2)]
            for slot in range(CHANGED):
                here = jnp.where(changed[slot] == block, 1.0, 0.0)
                lives = jnp.where(b == 0, live[0, slot], live[1, slot]).astype(jnp.float32)
                for n, weight in enumerate((here, here * lives)):
                    weight = jnp.full((HALF, D), weight, jnp.float32).astype(jnp.bfloat16)
                    term = pieces[n] * weight
                    old = totals[n][slot]
                    totals[n][slot] = term if old is None else old + term
        for slot in range(CHANGED):
            for n in range(2):
                z0[i, n, slot] = totals[n][slot]

        @pl.when(outside)
        def _():
            for p in range(PIECES):
                pair_copy(i, p).start()

    def some(p):
        return slice(p * SPAN, (p + 1) * SPAN)

    def pair_copy(i, p):
        return copy(
            z0.at[i, :, some(p)], za.at[i, :, some(p)], za_s.at[i, p], za_r.at[i, p], line_dev(mate)
        )

    def middle_copy(i, p):
        return copy(
            zb.at[i, :, some(p)], zc.at[i, :, some(p)], zb_s.at[i, p], zb_r.at[i, p],
            line_dev(A - 1 - a),
        )

    def back_copy(i, p):
        here = full.at[i, :, some(p), b]
        return copy(here, here, g_s.at[i, p], g_r.at[i, p], line_dev(mate))

    def x_copy(i, p, came=False):
        here = full.at[i, :, some(p), b]
        there = full.at[i, :, some(p), at_b(1)] if came else here
        return copy(here, there, x_s.at[i, p], x_r.at[i, p], dev(0, 1, 0, 0))

    def middle(i):
        @pl.when(inside)
        def _():
            for p in range(PIECES):
                pair_copy(i, p).wait_recv()
                zb[i, :, some(p)] = z0[i, :, some(p)] + za[i, :, some(p)]
                middle_copy(i, p).start()

    def give_back(i):
        @pl.when(inside)
        def _():
            for p in range(PIECES):
                middle_copy(i, p).wait_recv()
                full[i, :, some(p), b] = zb[i, :, some(p)] + zc[i, :, some(p)]
                back_copy(i, p).start()
                x_copy(i, p).start()

    def across(i):
        @pl.when(outside)
        def _():
            for p in range(PIECES):
                back_copy(i, p).wait_recv()
                x_copy(i, p).start()

    def q_of(i, n):
        return full[i, n].reshape(ROWS, D)

    def kv_of(i, n):
        return kv[i, n].reshape(z.keys, D)

    def first_pass(i):
        for p in range(PIECES):
            x_copy(i, p, True).wait_recv()
        arrived(kv.at[i], kv_r.at[i])
        scores = contract(kv_of(i, 0), q_of(i, 0), ((1,), (1,))) * SCALE
        top = jnp.max(scores, axis=0, keepdims=True)
        e = jnp.exp(scores - top)
        dp = contract(kv_of(i, 1), q_of(i, 1), ((1,), (1,)))
        total = jnp.sum(e, axis=0, keepdims=True)
        mean = jnp.sum(e * dp, axis=0, keepdims=True) / total
        sums[i] = jnp.broadcast_to(total, sums.shape[1:])
        found = (top + jnp.log(total), mean)
        expo[i] = e
        dpro[i] = dp
        for r, row in enumerate(found):
            for j in range(CHANGED):
                at = r * CHANGED + j
                stats[i, 0, at : at + 1, :] = row[:, j * BLOCK : (j + 1) * BLOCK]
        for k, (da, db) in enumerate(others):
            if k:
                copy(
                    stats.at[i, 0], stats.at[i, k], st_s.at[0], st_r.at[i], dev(da, db, 0, 0)
                ).start()

    def wide(x):
        return jnp.concatenate([x[j : j + 1] for j in range(CHANGED)], axis=1)

    def second_pass(i):
        arrived(stats.at[i, 1:], st_r.at[i])
        parts = [stats[i, k] for k in range(len(others))]
        top = functools.reduce(jnp.maximum, [part[0:CHANGED] for part in parts])
        shares = [jnp.exp(part[0:CHANGED] - top) for part in parts]
        whole = sum(shares)
        means = sum(part[CHANGED:] * share for part, share in zip(parts, shares))
        factor = wide(shares[0] / whole) / sums[i, 0:1]
        delta = wide(means / whole)
        probs = expo[i] * factor
        ds = (probs * (dpro[i] - delta)).astype(jnp.bfloat16)
        dk = (contract(ds, q_of(i, 0), ((1,), (0,))) * SCALE).astype(jnp.bfloat16)
        ret[i, 0] = dk.reshape(len(owners), BLOCK, D)
        send_out(i, 0)
        dq = contract(ds, kv_of(i, 0), ((0,), (0,))) * SCALE
        dq0[i] = dq.astype(jnp.bfloat16).reshape(A, B, z.shard * C, D)
        dq_x(i).start()
        dv = contract(probs.astype(jnp.bfloat16), q_of(i, 1), ((1,), (0,))).astype(jnp.bfloat16)
        ret[i, 1] = dv.reshape(len(owners), BLOCK, D)
        send_out(i, 1)

    def send_out(i, n):
        out = (dk_out, dv_out)[n].at[:, col(u, c, i)]
        for k, (du, dc) in enumerate(owners):
            if k:
                copy(ret.at[i, n, k], out, o_s.at[0], o_r.at[0], dev(0, 0, -dc, -du)).start()
            else:
                pltpu.make_async_copy(ret.at[i, n, k], out, l_s.at[0]).start()

    def dq_x(i):
        return copy(
            dq0.at[i, :, at_b(1)], dq1.at[i], d1_s.at[i], d1_r.at[i], dev(0, 1, 0, 0)
        )

    def dq_mid(i):
        dq_x(i).wait_recv()
        mine = dq0[i, :, b].astype(jnp.float32) + dq1[i].astype(jnp.float32)
        dt1[i] = mine.astype(jnp.bfloat16).reshape(A, C, z.shard, D)
        for k, (da, dc) in enumerate(rows):
            if k:
                copy(
                    dt1.at[i, at_a(da), at_c(dc)], dq2.at[i, k - 1],
                    d2_s.at[0], d2_r.at[i], dev(da, 0, dc, 0),
                ).start()

    def dq_end(i):
        arrived(dq2.at[i], d2_r.at[i])
        for dc in range(C):
            total = None
            for k, (da, e) in enumerate(rows):
                if e == dc:
                    term = (dq2[i, k - 1] if k else dt1[i, a, c]).astype(jnp.float32)
                    total = term if total is None else total + term
            at = pl.ds(pl.multiple_of(at_c(-dc) * W + i * D, D), D)
            dq_out[:, at] = total.astype(jnp.bfloat16)

    stages = [select, middle, give_back, across, first_pass, second_pass, dq_mid, dq_end]

    def step(t, carry):
        for stage, delay in reversed(list(zip(stages, DELAYS))):
            i = t - delay
            pl.when((i >= 0) & (i < N))(functools.partial(stage, i))
        return carry

    lax.fori_loop(0, N + DELAYS[-1], step, 0)

    def drain(i):
        for p in range(PIECES):
            @pl.when(outside)
            def _():
                pair_copy(i, p).wait_send()

            @pl.when(inside)
            def _():
                middle_copy(i, p).wait_send()
                back_copy(i, p).wait_send()

            x_copy(i, p).wait_send()

        dq_x(i).wait_send()
        for k in range(1, len(others)):
            arrived(stats.at[i, k], st_s.at[0])

    each(drain)
    arrived(ybuf.at[:, :, 1:], y_s.at[0])
    arrived(kv.at[:, :, 1:], kv_s.at[0])
    arrived(dq2, d2_s.at[0])
    arrived(ret.at[:, :, 1:], o_s.at[0])
    arrived(ret.at[:, :, 1:], o_r.at[0])
    arrived(ret.at[:, :, 0], l_s.at[0])


def hand_over(dq_in, dk_in, dv_in, dq_out, dk_out, dv_out, sems):
    pairs = ((dq_in, dq_out), (dk_in, dk_out), (dv_in, dv_out))
    copies = [pltpu.make_async_copy(src, dst, sems.at[n]) for n, (src, dst) in enumerate(pairs)]
    for one in copies:
        one.start()
    for one in copies:
        one.wait()


def split_local(seq_size, ulys_size, queries, keys, values, dout, changed_blocks, half_mask):
    z = Split(seq_size, ulys_size, queries.shape[1])
    N, U, A, C, D, R = z.chunks, z.ulys, z.outer, CORES, HEAD_DIM, z.shard
    bf16, f32 = jnp.bfloat16, jnp.float32
    dma = pltpu.SemaphoreType.DMA
    vmem = pl.BlockSpec(memory_space=pltpu.VMEM)
    hbm = pl.BlockSpec(memory_space=pl.ANY)
    smem = pl.BlockSpec(memory_space=pltpu.SMEM)
    scratch = [
        pltpu.VMEM((N, 2, INNER * z.groups, HALF, D), bf16),
        pltpu.VMEM((N, 2, z.groups, BLOCK, D), bf16),
        *[pltpu.VMEM((N, 2, CHANGED, HALF, D), bf16)] * 4,
        pltpu.VMEM((N, 2, CHANGED, INNER, HALF, D), bf16),
        pltpu.VMEM((N, z.keys, ROWS), f32),
        pltpu.VMEM((N, z.keys, ROWS), f32),
        pltpu.VMEM((N, A * INNER, 2 * CHANGED, BLOCK), f32),
        pltpu.VMEM((N, 8, ROWS), f32),
        pltpu.VMEM((N, 2, z.groups, BLOCK, D), bf16),
        pltpu.VMEM((N, A, INNER, C * R, D), bf16),
        pltpu.VMEM((N, A, C * R, D), bf16),
        pltpu.VMEM((N, A, C, R, D), bf16),
        pltpu.VMEM((N, A * C - 1, R, D), bf16),
        dma((1,)), dma((N,)),
        dma((1,)), dma((N,)),
        *[dma((N, PIECES))] * 8,
        dma((1,)), dma((N,)),
        dma((1,)), dma((1,)), dma((1,)),
        dma((N,)), dma((N,)),
        dma((1,)), dma((N,)),
    ]
    outs = (
        jax.ShapeDtypeStruct((R, z.width * C), bf16),
        jax.ShapeDtypeStruct(keys.shape, bf16),
        jax.ShapeDtypeStruct(values.shape, bf16),
    )
    found = pl.pallas_call(
        functools.partial(split_kernel, z),
        out_shape=tuple(pltpu.VMEM(out.shape, bf16) for out in outs),
        in_specs=[smem, smem, hbm, hbm, hbm, hbm],
        out_specs=(vmem, vmem, vmem),
        scratch_shapes=scratch,
        compiler_params=pltpu.CompilerParams(
            collective_id=1, has_side_effects=True, vmem_limit_bytes=56 * 1024 * 1024
        ),
    )(changed_blocks, half_mask.T, queries, dout, keys, values)
    return pl.pallas_call(
        hand_over,
        out_shape=outs,
        in_specs=[vmem] * 3,
        out_specs=[hbm] * 3,
        scratch_shapes=[dma((len(outs),))],
    )(*[pltpu.with_memory_space_constraint(x, pltpu.VMEM) for x in found])


def solution(mesh):
    rows = P(("seq", "ulys"), None)
    seq, ulys = mesh.shape["seq"], mesh.shape["ulys"]

    def run(queries, keys, values, dout, changed_blocks, half_mask):
        body = split_local if Split.fits(seq, ulys, queries.shape[1]) else local
        return body(seq, ulys, queries, keys, values, dout, changed_blocks, half_mask)

    return jax.shard_map(
        run,
        mesh=mesh,
        in_specs=(rows, rows, rows, rows, P(), P()),
        out_specs=(P("seq", "ulys"), rows, rows),
        check_vma=False,
    )
```
